32 devices in a mesh: dp: 16 (over z, y, core), tensor: 2 (over x).
Axes of the slice: x: 2, y: 2, z: 4, core: 2. Of those that a mesh axis runs over, the one named last changes fastest.
Arguments:
- tokens: bfloat16 [32768, 1024], P(('dp', 'tensor')), may hold values from -6 to 6
- weight_query: bfloat16 [1024, 1024], P('dp', 'tensor'), may hold values from -0.1875 to 0.1875
- weight_key: bfloat16 [1024, 1024], P('dp', 'tensor'), may hold values from -0.1875 to 0.1875
- weight_value: bfloat16 [1024, 1024], P('dp', 'tensor'), may hold values from -0.1875 to 0.1875
- weight_output: bfloat16 [1024, 1024], P('tensor', 'dp'), may hold values from -3 to 3
- weight_up: bfloat16 [1024, 4096], P('dp', 'tensor'), may hold values from -0.1875 to 0.1875
- weight_down: bfloat16 [4096, 1024], P('tensor', 'dp'), may hold values from -0.09375 to 0.09375
- bias_query: bfloat16 [1024], P(('dp', 'tensor')), may hold values from -3 to 3
- bias_value: bfloat16 [1024], P(('dp', 'tensor')), may hold values from -3 to 3
- bias_up: bfloat16 [4096], P(('dp', 'tensor')), may hold values from -3 to 3
- bias_output: bfloat16 [1024], P(('dp', 'tensor')), may hold values from -3 to 3
- bias_down: bfloat16 [1024], P(('dp', 'tensor')), may hold values from -3 to 3
- first_gain: bfloat16 [1024], P(('dp', 'tensor')), may hold values from 0.099609375 to 1.8984375
- first_shift: bfloat16 [1024], P(('dp', 'tensor')), may hold values from -3 to 3
- second_gain: bfloat16 [1024], P(('dp', 'tensor')), may hold values from 0.099609375 to 1.8984375
- second_shift: bfloat16 [1024], P(('dp', 'tensor')), may hold values from -3 to 3
- out_grad: bfloat16 [32768, 1024], P(('dp', 'tensor')), may hold values from -6 to 6
Outputs:
- layer_out: bfloat16 [32768, 1024], P(('dp', 'tensor'))
- input_grad: bfloat16 [32768, 1024], P(('dp', 'tensor'))
- grad_query: float32 [1024, 1024], P('dp', 'tensor')
- grad_key: float32 [1024, 1024], P('dp', 'tensor')
- grad_value: float32 [1024, 1024], P('dp', 'tensor')
- grad_output: float32 [1024, 1024], P('tensor', 'dp')
- grad_up: float32 [1024, 4096], P('dp', 'tensor')
- grad_down: float32 [4096, 1024], P('tensor', 'dp')
- grad_bias_query: float32 [1024], P(('dp', 'tensor'))
- grad_bias_value: float32 [1024], P(('dp', 'tensor'))
- grad_bias_up: float32 [4096], P(('dp', 'tensor'))
- grad_bias_output: float32 [1024], P(('dp', 'tensor'))
- grad_bias_down: float32 [1024], P(('dp', 'tensor'))
- grad_first_gain: float32 [1024], P(('dp', 'tensor'))
- grad_first_shift: float32 [1024], P(('dp', 'tensor'))
- grad_second_gain: float32 [1024], P(('dp', 'tensor'))
- grad_second_shift: float32 [1024], P(('dp', 'tensor'))
The draws below stay inside these ranges and needn't reach their ends.
All inputs are finite; a program needn't handle non-finite values.
Results may differ from the reference program's by a relative error of at most 0.022.
Values may be sent and summed in bfloat16 or wider, within the bound.
A program may use at most 256 MiB of HBM per device.

```python
import math
import jax
import jax.numpy as jnp
from jax import lax

D = 1024
HEADS = 16
HEAD_DIM = 64
FF = 4096
LEN = 1024
TOKENS = 32768


def spiked(drawn, own_key, source, target, parts, factor):
    owner, partner = [(jnp.arange(drawn.shape[position]) // (drawn.shape[position] // parts)).reshape([-1 if axis == position else 1 for axis in range(drawn.ndim)]) for position in (source, target)]
    chosen = jax.random.permutation(own_key, parts)[partner]
    strong = (owner == chosen) | (owner == (partner + parts // 2) % parts)
    return jnp.where(strong, factor * drawn, drawn)


def block_scale(own_key, shape, pieces, low, largest):
    def one(position, blocks):
        heights = jax.random.uniform(jax.random.fold_in(jax.random.fold_in(own_key, 6), position), (blocks,), jnp.float32, low / len(pieces), largest / len(pieces))
        return jnp.repeat(jnp.exp(heights), shape[position] // blocks).reshape((-1,) + (1,) * (len(shape) - position - 1))

    loudness = one(*pieces[0])
    for cut in pieces[1:]:
        loudness = loudness * one(*cut)
    return loudness


def bell_draw(key, shape, scale, most, pieces=(), dtype=jnp.bfloat16):
    drawn = scale * jax.random.normal(key, shape, jnp.float32)
    if pieces:
        drawn = drawn * block_scale(key, shape, pieces, -0.22, 0.18)
    return jnp.clip(drawn, -most, most).astype(dtype)


def bell_draw_with(rng, shape, deviation, most, pieces, heavy, held_as=jnp.bfloat16):
    values = deviation * jax.random.normal(rng, shape, jnp.float32)
    if pieces:
        values = values * block_scale(rng, shape, pieces, -0.22, 0.18)
    return jnp.clip(spiked(values, jax.random.fold_in(rng, 3), *heavy), -most, most).astype(held_as)


def setup_inputs(seed: int = 0) -> dict:
    arg_keys = jax.random.split(jax.random.key(seed), 18)
    tokens = bell_draw(arg_keys[0], (TOKENS, D), 1.0, 6.0, ((0, 32),))
    weight_query = bell_draw(arg_keys[1], (D, D), D ** -0.5, 0.1875, ((0, 16), (1, 2)))
    weight_key = bell_draw(arg_keys[2], (D, D), D ** -0.5, 0.1875, ((0, 16), (1, 2)))
    weight_value = bell_draw(arg_keys[3], (D, D), D ** -0.5, 0.1875, ((0, 16), (1, 2)))
    weight_output = bell_draw(arg_keys[4], (D, D), (max(1, 4 * D // LEN)) ** -0.5, 3.0, ((0, 2), (1, 16)))
    weight_up = bell_draw(arg_keys[5], (D, FF), D ** -0.5, 0.1875, ((0, 16), (1, 2)))
    weight_down = bell_draw(arg_keys[6], (FF, D), FF ** -0.5, 0.09375, ((0, 2), (1, 16)))
    bias_query = bell_draw(arg_keys[7], (D,), 0.5, 3.0, ((0, 32),))
    bias_value = bell_draw(arg_keys[8], (D,), 0.5, 3.0, ((0, 32),))
    bias_up = bell_draw(arg_keys[9], (FF,), 0.5, 3.0, ((0, 32),))
    bias_output = bell_draw(arg_keys[10], (D,), 0.5, 3.0, ((0, 32),))
    bias_down = bell_draw(arg_keys[11], (D,), 0.5, 3.0, ((0, 32),))
    first_gain = jnp.clip(1.0 + 0.18 * jax.random.normal(arg_keys[12], (D,), jnp.float32), 0.099609375, 1.8984375).astype(jnp.bfloat16)
    first_shift = bell_draw(arg_keys[13], (D,), 0.5, 3.0, ((0, 32),))
    second_gain = jnp.clip(1.0 + 0.18 * jax.random.normal(arg_keys[14], (D,), jnp.float32), 0.099609375, 1.8984375).astype(jnp.bfloat16)
    second_shift = bell_draw(arg_keys[15], (D,), 0.5, 3.0, ((0, 32),))
    out_grad = bell_draw_with(arg_keys[16], (TOKENS, D), 1.0, 6.0, ((0, 32),), (0, 1, 32, 2.75))
    return {"tokens": tokens, "weight_query": weight_query, "weight_key": weight_key, "weight_value": weight_value, "weight_output": weight_output, "weight_up": weight_up, "weight_down": weight_down, "bias_query": bias_query, "bias_value": bias_value, "bias_up": bias_up, "bias_output": bias_output, "bias_down": bias_down, "first_gain": first_gain, "first_shift": first_shift, "second_gain": second_gain, "second_shift": second_shift, "out_grad": out_grad}


EPS = 1e-05
HIGH = lax.Precision.HIGHEST

@jax.custom_vjp
def low(v):
    return lax.optimization_barrier(v.astype(jnp.bfloat16)).astype(jnp.float32)

@jax.custom_vjp
def low_back(v):
    return v

def low_keep(v):
    return (low(v), None)

def low_pass(kept, grad):
    return (grad,)

def back_keep(v):
    return (v, None)

def back_low(kept, grad):
    return (low(grad),)
low.defvjp(low_keep, low_pass)
low_back.defvjp(back_keep, back_low)

def matmul(left, right):
    return jnp.dot(left, right, precision=HIGH, preferred_element_type=jnp.float32)

def norm_layer(resid, gain, shift):
    center = resid - lax.optimization_barrier(jnp.mean(resid, axis=-1, keepdims=True))
    spread = lax.optimization_barrier(jnp.mean(center * center, axis=-1, keepdims=True))
    return center * lax.rsqrt(spread + EPS) * gain + shift

def attend(block):
    query, key_in, value = block
    query_h = query.reshape(LEN, HEADS, HEAD_DIM)
    key_h = key_in.reshape(LEN, HEADS, HEAD_DIM)
    value_h = value.reshape(LEN, HEADS, HEAD_DIM)
    scores = low_back(jnp.einsum('qhd,khd->hqk', query_h, key_h, precision=HIGH))
    attn_weights = low(jax.nn.softmax(scores, axis=-1))
    context = jnp.einsum('hqk,khd->qhd', attn_weights, value_h, precision=HIGH)
    return context.reshape(LEN, D)

def forward(inputs, w_query, w_key, w_value, w_output, w_up, w_down, b_query, b_value, b_up, b_output, b_down, gain_one, shift_one, gain_two, shift_two):
    scale = HEAD_DIM ** (-0.5)
    query = low_back(low((matmul(inputs, w_query) + b_query) * scale))
    key_all = low_back(low(matmul(inputs, w_key)))
    value = low_back(low(matmul(inputs, w_value) + b_value))
    seq_count = inputs.shape[0] // LEN
    context = lax.map(jax.checkpoint(attend), (query.reshape(seq_count, LEN, D), key_all.reshape(seq_count, LEN, D), value.reshape(seq_count, LEN, D)))
    context = low_back(low(context.reshape(-1, D)))
    attn = low_back(matmul(context, w_output) + b_output)
    hidden = norm_layer(inputs + attn, gain_one, shift_one)
    preact = low_back(matmul(low(hidden), w_up) + b_up)
    active = low(jax.nn.gelu(preact, approximate=False))
    down = low_back(matmul(active, w_down) + b_down)
    return norm_layer(hidden + down, gain_two, shift_two)

def reference(tokens, weight_query, weight_key, weight_value, weight_output, weight_up, weight_down, bias_query, bias_value, bias_up, bias_output, bias_down, first_gain, first_shift, second_gain, second_shift, out_grad):
    params = tuple((member.astype(jnp.float32) for member in (weight_query, weight_key, weight_value, weight_output, weight_up, weight_down, bias_query, bias_value, bias_up, bias_output, bias_down, first_gain, first_shift, second_gain, second_shift)))
    seq_total = tokens.shape[0] // LEN
    per_group = math.gcd(seq_total, max(1, 4096 // LEN))
    groups = seq_total // per_group
    group_rows = per_group * LEN
    inputs = tokens.astype(jnp.float32).reshape(groups, group_rows, D)
    cotangent = out_grad.astype(jnp.float32).reshape(groups, group_rows, D)

    def one_group(totals, block):
        block_in, block_cot = block
        result, pull = jax.vjp(forward, block_in, *params)
        grads = pull(block_cot)
        totals = tuple((total + grad for total, grad in zip(totals, grads[1:])))
        return (totals, (result.astype(jnp.bfloat16), grads[0].astype(jnp.bfloat16)))
    zeros = tuple((jnp.zeros_like(member) for member in params))
    totals, (results, in_grads) = lax.scan(one_group, zeros, (inputs, cotangent))
    return (results.reshape(-1, D), in_grads.reshape(-1, D), totals[0], totals[1], totals[2], totals[3], totals[4], totals[5], totals[6], totals[7], totals[8], totals[9], totals[10], totals[11], totals[12], totals[13], totals[14])
```

```python
import functools
import jax
import jax.numpy as jnp
from jax import lax
from jax.experimental import pallas as pl
from jax.experimental.pallas import tpu as pltpu
from jax.sharding import PartitionSpec as P

HEAD_DIM = 64
LEN = 1024
EPS = 1e-05
SQRT_HALF = 0.7071067811865476
INV_ROOT_TAU = 0.3989422804014327
BF, F32 = jnp.bfloat16, jnp.float32
MESH = pl.DeviceIdType.MESH
NT = (((1,), (1,)), ((), ()))
TN = (((0,), (0,)), ((), ()))
TILE = 256
WQ = 384
WO = 512
WF = 1024


def tile_rows(t):
    return pl.ds(t * TILE if isinstance(t, int) else pl.multiple_of(t * TILE, TILE), TILE)


def mm(a, b):
    return jnp.dot(a, b, preferred_element_type=F32)


def mm_nt(a, b):
    return lax.dot_general(a, b, NT, preferred_element_type=F32)


def gelu_both(z):
    far = 1.0 / (1.0 + (0.3275911 * SQRT_HALF) * jnp.abs(z))
    bell = jnp.exp(-0.5 * z * z)
    poly = far * (
        0.127414796
        + far * (-0.142248368 + far * (0.7107068705 + far * (-0.7265760135 + far * 0.5307027145)))
    )
    tail = poly * bell
    cdf = jnp.where(z >= 0, 1.0 - tail, tail)
    return z * cdf, cdf + z * bell * INV_ROOT_TAU


def where_am_i():
    dp, x = lax.axis_index("dp"), lax.axis_index("tensor")
    return dp // 4, lax.rem(dp // 2, 2), lax.rem(dp, 2), x


def device(z, y, c, x):
    return {"dp": (z * 2 + y) * 2 + c, "tensor": x}


def greet(nz, z, y, c, x):
    bar = pltpu.get_barrier_semaphore()
    others = [device(lax.rem(z + s, nz), y, c, x) for s in range(1, nz)]
    others += [device(z, 1 - y, c, x), device(z, y, 1 - c, x), device(z, y, c, 1 - x)]
    for other in others:
        pl.semaphore_signal(bar, inc=1, device_id=other, device_id_type=MESH)
    pl.semaphore_wait(bar, len(others))


class Gather:
    def __init__(self, nz, pos, send, recv):
        self.nz, self.pos, self.send, self.recv = nz, pos, send, recv
        self.sent = []

    def go(self, k, slot, src, dst, to):
        copy = pltpu.make_async_remote_copy(
            src_ref=src,
            dst_ref=dst,
            send_sem=self.send.at[k, slot],
            recv_sem=self.recv.at[k, slot],
            device_id=to,
            device_id_type=MESH,
        )
        copy.start()
        self.sent.append(copy)
        return copy


def ln_stats(resid):
    center = resid - jnp.mean(resid, axis=-1, keepdims=True)
    inverse = lax.rsqrt(jnp.mean(center * center, axis=-1, keepdims=True) + EPS)
    return center * inverse, inverse


def forward_kernel(
    nz,
    tok_hbm, og_hbm, sv, sq, so, sf,
    lo_out, dres_out, ddown_out, n1_out, inv1_out, hlow_out, act_out, slope_out, qa_out, k_out, v_out, ctx_out,
    gq_out, go_out, gf_out, bias_out, vsum_out,
    tok, og, gv, gq, go, gf, bias, bup, qs, kz, ks, vs, qa, ctx, hid, acc, hlow, act, slope, n1, inv1, ddown, vsum,
    send, recv, lsem,
):
    z, y, c, x = where_am_i()
    local = []

    def start_local(src, dst):
        copy = pltpu.make_async_copy(src, dst, lsem.at[len(local)])
        copy.start()
        local.append(copy)
        return copy

    tok_in = start_local(tok_hbm, tok)
    og_in = start_local(og_hbm, og)
    greet(nz, z, y, c, x)
    gather = Gather(nz, (z, y, c, x), send, recv)
    chunks = [(gv, sv)]
    chunks += [(gq.at[i], sq.at[i]) for i in range(4)]
    chunks += [(go, so)]
    chunks += [(gf.at[j], sf.at[j]) for j in range(4)]
    zc, c1, c2, cc = {}, {}, {}, {}

    def z_send(k):
        buf, own = chunks[k]
        zc[k] = [
            gather.go(k, s - 1, own, buf.at[x, z, y, c], device(lax.rem(z + s, nz), y, c, x))
            for s in range(1, nz)
        ]

    def z_wait(k):
        for copy in zc[k]:
            copy.wait_recv()

    def s1(k):
        buf = chunks[k][0]
        if k == 0:
            part = buf.at[x, :, y, c]
            c1[k] = [gather.go(k, 3, part, part, device(z, y, c, 1 - x))]
            return
        upper, lower = buf.at[x, :, y, c, pl.ds(0, 32)], buf.at[x, :, y, c, pl.ds(32, 32)]
        c1[k] = [
            gather.go(k, 3, upper, upper, device(z, y, c, 1 - x)),
            gather.go(k, 4, lower, lower, device(z, 1 - y, c, x)),
        ]

    def s2(k):
        buf = chunks[k][0]
        for copy in c1[k]:
            copy.wait_recv()
        if k == 0:
            part = buf.at[:, :, y, c]
            c2[k] = [gather.go(k, 5, part, part, device(z, 1 - y, c, x))]
            return
        upper, lower = buf.at[:, :, y, c, pl.ds(0, 32)], buf.at[x, :, :, c, pl.ds(32, 32)]
        c2[k] = [
            gather.go(k, 5, upper, upper, device(z, 1 - y, c, x)),
            gather.go(k, 6, lower, lower, device(z, y, c, 1 - x)),
        ]

    def core(k):
        buf = chunks[k][0]
        for copy in c2[k]:
            copy.wait_recv()
        part = buf.at[:, :, :, c]
        cc[k] = gather.go(k, 7, part, part, device(z, y, 1 - c, x))

    def tick(k):
        if k + 2 < len(chunks):
            z_wait(k + 2)
            s1(k + 2)
        if k + 1 < len(chunks):
            s2(k + 1)
        core(k)

    def ready(k):
        cc[k].wait_recv()

    for k in range(len(chunks)):
        z_send(k)
    for buf, own in chunks:
        buf[x, z, y, c] = own[...]
    z_wait(0)
    s1(0)
    z_wait(1)
    s1(1)
    s2(0)
    tick(0)
    tok_in.wait()
    tick(1)
    ready(0)
    for t in range(8):
        owners = [4 * t + m for m in range(4)]
        sums = None
        for m, owner in enumerate(owners):
            dp_o, x_o = owner // 2, owner % 2
            block = gv[x_o, dp_o // 4, dp_o // 2 % 2, dp_o % 2].astype(F32)
            sums = block if sums is None else sums + block
            bup[:, pl.ds(owner * 128, 128)] = jnp.broadcast_to(block[8:9], (8, 128))
        bias[:, pl.ds(t * 128, 128)] = sums
    bias_copy = start_local(bias, bias_out)

    lane = lax.broadcasted_iota(jnp.int32, (TILE, 128), 1)
    low_half = lane < 64
    rows_of = tile_rows
    tiles = LEN // TILE

    def project(i, xx, slot):
        pair = xx * 4 + i
        bq = bias[0:1, pair * 128 : pair * 128 + 128]
        bv = bias[1:2, pair * 128 : pair * 128 + 128]

        def body(t, carry):
            rows = rows_of(t)
            part = mm(tok[rows], gq[i, xx].reshape(1024, WQ))
            qs[rows] = ((part[:, :128] + bq) * 0.125).astype(BF)
            kk = part[:, 128:256].astype(BF)
            ks[slot, rows] = kk
            zero = jnp.zeros_like(kk)
            kz[0, rows] = jnp.where(low_half, kk, zero)
            kz[1, rows] = jnp.where(low_half, zero, kk)
            vs[slot, rows] = (part[:, 256:] + bv).astype(BF)
            return carry

        lax.fori_loop(0, tiles, body, 0)

    def attend(i, xx, slot):
        pair = xx * 4 + i

        def body(t, carry):
            rows = rows_of(t)
            q = qs[rows]
            outs = []
            for h in range(2):
                s = mm_nt(q, kz[h])
                top = jnp.max(s, axis=-1, keepdims=True)
                e = jnp.exp(s - top)
                total = jnp.sum(e, axis=-1, keepdims=True)
                o = mm(e.astype(BF), vs[slot])
                outs.append(o * (1.0 / total))
                lse = -(top + jnp.log(total))
                hi = lse.astype(BF).astype(F32)
                mid = (lse - hi).astype(BF).astype(F32)
                rest = lse - hi - mid
                at = 64 * (1 - h)
                extra = jnp.where(
                    lane == at, hi, jnp.where(lane == at + 1, mid, jnp.where(lane == at + 2, rest, 0.0))
                )
                mine = low_half if h == 0 else jnp.logical_not(low_half)
                qa[slot, h, rows] = jnp.where(mine, q.astype(F32), extra).astype(BF)
            ctx[rows, pair * 128 : pair * 128 + 128] = jnp.where(low_half, outs[0], outs[1]).astype(BF)
            return carry

        lax.fori_loop(0, tiles, body, 0)

    pending = {}
    step = 0
    next_tick = 2
    for i in range(4):
        while next_tick < i + 2:
            tick(next_tick)
            next_tick += 1
        ready(1 + i)
        start_local(gq.at[i], gq_out.at[i])
        for xx in range(2):
            slot = step % 2
            if step >= 2:
                for copy in pending[step - 2]:
                    copy.wait()
            project(i, xx, slot)
            attend(i, xx, slot)
            pair = xx * 4 + i
            pending[step] = [
                start_local(ks.at[slot], k_out.at[pair]),
                start_local(vs.at[slot], v_out.at[pair]),
                start_local(qa.at[slot], qa_out.at[pair]),
            ]
            if step in (0, 2, 4, 6):
                tick(next_tick)
                next_tick += 1
            step += 1
    while next_tick < 6:
        tick(next_tick)
        next_tick += 1
    ready(5)
    start_local(go, go_out)
    ctx_copy = start_local(ctx, ctx_out)

    def first_norm(t, carry):
        rows = rows_of(t)
        attn = mm_nt(ctx[rows, :WO], go[0].reshape(1024, WO)) + mm_nt(ctx[rows, WO:], go[1].reshape(1024, WO))
        normed, inverse = ln_stats(tok[rows].astype(F32) + (attn + bias[2:3]))
        n1[rows] = normed.astype(BF)
        inv1[rows] = jnp.broadcast_to(inverse, (TILE, 128))
        h = normed * bias[4:5] + bias[5:6]
        hid[rows] = h
        hlow[rows] = h.astype(BF)
        acc[rows] = jnp.zeros((TILE, 1024), F32)
        return carry

    lax.fori_loop(0, tiles, first_norm, 0)
    start_local(n1, n1_out)
    start_local(inv1, inv1_out)
    start_local(hlow, hlow_out)

    pend = {}
    step = 0
    for j in range(4):
        while next_tick < min(j + 7, 10):
            tick(next_tick)
            next_tick += 1
        ready(6 + j)
        start_local(gf.at[j], gf_out.at[j])
        for xx in range(2):
            slot = step % 2
            if step >= 2:
                for copy in pend[step - 2]:
                    copy.wait()
            first = xx * 2048 + j * 512
            b_up = bup[0:1, first : first + 512]

            def body(t, carry):
                rows = rows_of(t)
                pre = mm(hlow[rows], gf[j, xx, :, :, :, :, pl.ds(0, 512)].reshape(1024, 512)) + b_up
                value, grade = gelu_both(pre)
                value = value.astype(BF)
                act[slot, rows] = value
                slope[slot, rows] = grade.astype(BF)
                acc[rows] += mm_nt(value, gf[j, xx, :, :, :, :, pl.ds(512, 512)].reshape(1024, 512))
                return carry

            lax.fori_loop(0, tiles, body, 0)
            pend[step] = [
                start_local(act.at[slot], act_out.at[j, xx]),
                start_local(slope.at[slot], slope_out.at[j, xx]),
            ]
            if step in (0, 2, 4) and next_tick < 10:
                tick(next_tick)
                next_tick += 1
            step += 1
    og_in.wait()
    ctx_copy.wait()
    vsum[...] = jnp.zeros_like(vsum)

    def second_norm(t, carry):
        rows = rows_of(t)
        normed, inverse = ln_stats(hid[rows] + (acc[rows] + bias[3:4]))
        ctx[rows] = (normed * bias[6:7] + bias[7:8]).astype(BF)
        g = og[rows].astype(F32)
        u = g * bias[6:7]
        first_mean = jnp.mean(u, axis=-1, keepdims=True)
        second_mean = jnp.mean(u * normed, axis=-1, keepdims=True)
        d = inverse * (u - first_mean - normed * second_mean)
        acc[rows] = d
        low = d.astype(BF)
        ddown[rows] = low
        vsum[0:1] += jnp.sum(g * normed, axis=0, keepdims=True)
        vsum[1:2] += jnp.sum(g, axis=0, keepdims=True)
        vsum[2:3] += jnp.sum(low.astype(F32), axis=0, keepdims=True)
        return carry

    lax.fori_loop(0, tiles, second_norm, 0)
    start_local(ctx, lo_out)
    start_local(acc, dres_out)
    start_local(ddown, ddown_out)
    start_local(vsum, vsum_out)
    for copy in gather.sent:
        copy.wait_send()
    waited = [tok_in, og_in, ctx_copy] + [m for s in list(pending)[:-2] for m in pending[s]]
    waited += [m for s in list(pend)[:-2] for m in pend[s]]
    for copy in local:
        if not any(copy is w for w in waited):
            copy.wait()


def forward_call(nz, tok, og, sv, sq, so, sf):
    S = jax.ShapeDtypeStruct
    outs = [
        S((LEN, 1024), BF), S((LEN, 1024), F32), S((LEN, 1024), BF), S((LEN, 1024), BF), S((LEN, 128), F32),
        S((LEN, 1024), BF), S((4, 2, LEN, 512), BF), S((4, 2, LEN, 512), BF), S((8, 2, LEN, 128), BF),
        S((8, LEN, 128), BF), S((8, LEN, 128), BF), S((LEN, 1024), BF),
        S((4, 2, nz, 2, 2, 64, WQ), BF), S((2, nz, 2, 2, 64, WO), BF), S((4, 2, nz, 2, 2, 64, WF), BF),
        S((16, 1024), F32), S((8, 1024), F32),
    ]
    V = pltpu.VMEM
    scratch = [
        V((LEN, 1024), BF), V((LEN, 1024), BF), V((2, nz, 2, 2, 16, 128), BF), V((4, 2, nz, 2, 2, 64, WQ), BF),
        V((2, nz, 2, 2, 64, WO), BF), V((4, 2, nz, 2, 2, 64, WF), BF), V((16, 1024), F32), V((8, 4096), F32),
        V((LEN, 128), BF), V((2, LEN, 128), BF), V((2, LEN, 128), BF), V((2, LEN, 128), BF), V((2, 2, LEN, 128), BF),
        V((LEN, 1024), BF), V((LEN, 1024), F32), V((LEN, 1024), F32), V((LEN, 1024), BF),
        V((2, LEN, 512), BF), V((2, LEN, 512), BF), V((LEN, 1024), BF), V((LEN, 128), F32), V((LEN, 1024), BF),
        V((8, 1024), F32),
        pltpu.SemaphoreType.DMA((10, 8)), pltpu.SemaphoreType.DMA((10, 8)), pltpu.SemaphoreType.DMA((72,)),
    ]
    hbm, vmem = pl.BlockSpec(memory_space=pl.ANY), pl.BlockSpec(memory_space=pltpu.VMEM)
    return pl.pallas_call(
        functools.partial(forward_kernel, nz),
        out_shape=outs,
        in_specs=[hbm, hbm, vmem, vmem, vmem, vmem],
        out_specs=[hbm] * len(outs),
        scratch_shapes=scratch,
        compiler_params=pltpu.CompilerParams(
            collective_id=0, has_side_effects=True, vmem_limit_bytes=61 * 1024 * 1024
        ),
        cost_estimate=pl.CostEstimate(flops=30 * 10**9, bytes_accessed=10**8, transcendentals=2 * 10**7),
        name="forward",
    )(tok, og, sv, sq, so, sf)


def pack(wq, wk, wv, wo, wu, wd, vectors):
    parts = [m.reshape(64, 4, 128) for m in (wq, wk, wv)]
    sq = jnp.stack(parts, axis=2).transpose(1, 0, 2, 3).reshape(4, 64, WQ)
    so = wo.T
    sf = jnp.concatenate([wu.reshape(64, 4, 512), wd.T.reshape(64, 4, 512)], axis=2).transpose(1, 0, 2)
    dev = lax.axis_index("dp") * 2 + lax.axis_index("tensor")
    names = ("bq", "bv", "bo", "bd", "g1", "s1", "g2", "s2")
    rows = jnp.stack([vectors[n] for n in names])
    quarter = lax.broadcasted_iota(jnp.int32, (8, 128), 1) // 32
    rows = jnp.where(quarter == dev % 4, jnp.tile(rows, (1, 4)), jnp.zeros((), BF))
    sv = jnp.concatenate([rows, jnp.broadcast_to(vectors["bu"][None], (8, 128))], axis=0)
    return sv, sq, so, sf


class Scatter:
    def __init__(self, nz, pos, send, recv):
        self.nz, self.pos, self.send, self.recv = nz, pos, send, recv
        self.sent, self.chunks, self.flying, self.done = [], {}, {}, set()
        z, y, c, x = pos
        self.not_c, self.not_y, self.not_x = 1 - c, 1 - y, 1 - x
        self.z_at = [lax.rem(z + d, nz) for d in range(nz)]
        self.to_c, self.to_y, self.to_x = device(z, y, 1 - c, x), device(z, 1 - y, c, x), device(z, y, c, 1 - x)
        self.to_z = [device(at, y, c, x) for at in self.z_at]

    def add(self, k, buf, got, slot, split, finish):
        self.chunks[k] = (buf, lambda: tuple(g.at[slot] for g in got), split, finish)

    def go(self, k, sem, src, dst, to):
        def name():
            return pltpu.make_async_remote_copy(
                src_ref=src(),
                dst_ref=dst(),
                send_sem=self.send.at[k, sem],
                recv_sem=self.recv.at[k, sem],
                device_id=to,
                device_id_type=MESH,
            )

        name().start()
        self.sent.append(name)
        return name

    def stage(self, k, s):
        z, y, c, x = self.pos
        nz = self.nz
        whole, got, split, finish = self.chunks[k]
        buf = whole()
        got_c, got_y, got_x, got_y2, got_x2, got_z = got()
        half = buf.shape[4] // 2 if split else buf.shape[4]
        up, down = pl.ds(0, half), pl.ds(half, half)
        assert (k, s) not in self.done and (s == 0 or (k, s - 1) in self.done)
        assert s == 4 or k - 1 not in self.chunks or (k - 1, s + 1) in self.done
        self.done.add((k, s))
        for copy in self.flying.pop((k, s - 1), []):
            copy().wait_recv()
        if s == 0:
            copies = [self.go(k, 0, lambda: whole().at[:, :, :, self.not_c], lambda: got()[0], self.to_c)]
        elif s == 1:

            def fold(m, carry):
                xx, zz = m // nz, lax.rem(m, nz)
                buf[xx, zz, :, c] += got_c[xx, zz]
                return carry

            lax.fori_loop(0, 2 * nz, fold, 0)
            copies = [self.go(k, 1, lambda: whole().at[:, :, self.not_y, c, up], lambda: got()[1], self.to_y)]
            if split:
                copies.append(self.go(k, 2, lambda: whole().at[self.not_x, :, :, c, down], lambda: got()[2], self.to_x))
        elif s == 2:

            def fold(zz, carry):
                for xx in range(2):
                    buf[xx, zz, y, c, up] += got_y[xx, zz]
                if split:
                    for yy in range(2):
                        buf[x, zz, yy, c, down] += got_x[zz, yy]
                return carry

            lax.fori_loop(0, nz, fold, 0)
            copies = [self.go(k, 3, lambda: whole().at[self.not_x, :, y, c, up], lambda: got()[4], self.to_x)]
            if split:
                copies.append(self.go(k, 4, lambda: whole().at[x, :, self.not_y, c, down], lambda: got()[3], self.to_y))
        elif s == 3:

            def fold(zz, carry):
                buf[x, zz, y, c, up] += got_x2[zz]
                if split:
                    buf[x, zz, y, c, down] += got_y2[zz]
                return carry

            lax.fori_loop(0, nz, fold, 0)
            copies = [
                self.go(
                    k, 4 + d, lambda d=d: whole().at[x, self.z_at[d], y, c], lambda d=d: got()[5].at[d - 1], self.to_z[d]
                )
                for d in range(1, nz)
            ]
        else:
            total = buf[x, z, y, c].astype(F32)
            for d in range(1, nz):
                total = total + got_z[d - 1].astype(F32)
            finish(total)
            copies = []
        self.flying[(k, s)] = copies

    def tick(self, k):
        for s in (4, 3, 2, 1, 0):
            if k - s in self.chunks and (k - s, s) not in self.done:
                self.stage(k - s, s)


def backward_kernel(
    nz,
    tok_hbm, hlow_hbm, ddown_hbm, dres_hbm, n1_hbm, inv1_hbm, act_hbm, slope_hbm, qa_hbm, k_hbm, v_hbm, ctx_hbm,
    gq_hbm, go_hbm, gf_hbm, bias, vsum,
    ig_out, outf_hbm, outo_hbm, outq_hbm, outv_hbm,
    rbf, rbo, rbq, rbv, rcf, ryf, rxf, ry2f, rx2f, rzf, rco, ryo, rxo, ry2o, rx2o, rzo, rcq, ryq, rxq, ry2q, rx2q, rzq,
    rcv, ryv, rxv, ry2v, rx2v, rzv,
    dacc, dctx, ctx, vgrad, bup, outf, outo, outq, outv,
    send, recv, lsem,
):
    z, y, c, x = where_am_i()
    used = [0]

    def start_local(src, dst):
        at = used[0]
        used[0] += 1
        copy = pltpu.make_async_copy(src, dst, lsem.at[at])
        copy.start()
        return copy

    greet(nz, z, y, c, x)
    rs = Scatter(nz, (z, y, c, x), send, recv)
    tiles = LEN // TILE
    rows_of = tile_rows
    out_copies = []

    def finisher(refs):
        def finish(total):
            ref, hbm = refs()
            ref[...] = total
            at = used[0]
            start_local(ref, hbm)
            out_copies.append(lambda: pltpu.make_async_copy(*refs(), lsem.at[at]))

        return finish

    vgrad[...] = jnp.zeros_like(vgrad)
    bup[...] = jnp.zeros_like(bup)
    vgrad[6:8] = vsum[0:2]
    vgrad[3:4] = vsum[2:3]
    got_f, got_o, got_q, got_v = (
        (rcf, ryf, rxf, ry2f, rx2f, rzf), (rco, ryo, rxo, ry2o, rx2o, rzo),
        (rcq, ryq, rxq, ry2q, rx2q, rzq), (rcv, ryv, rxv, ry2v, rx2v, rzv),
    )

    def transpose_into(dst, src):
        for t in range(tiles):
            dst[:, t * TILE : t * TILE + TILE] = src[t * TILE : t * TILE + TILE].T

    def ffn(ddown_t, hlow_t, wf, act, slope, dpre):
        ins = {}

        def load(step):
            j, xx, slot = step // 2, step % 2, step % 2
            ins[step] = [
                start_local(gf_hbm.at[j, xx], wf.at[slot]),
                start_local(act_hbm.at[j, xx], act.at[slot]),
                start_local(slope_hbm.at[j, xx], slope.at[slot]),
            ]

        ddown = ctx
        first = [start_local(ddown_hbm, ddown), start_local(hlow_hbm, dctx)]
        load(0)
        for copy in first:
            copy.wait()
        transpose_into(ddown_t, ddown)
        transpose_into(hlow_t, dctx)
        for step in range(8):
            j, xx, slot = step // 2, step % 2, step % 2
            for copy in ins[step]:
                copy.wait()
            if step + 1 < 8:
                load(step + 1)
            at = xx * 2048 + j * 512

            def rows_body(t, carry):
                rows = rows_of(t)
                d_act = mm(ddown[rows], wf[slot, :, :, :, :, pl.ds(512, 512)].reshape(1024, 512))
                d_pre = (d_act * slope[slot, rows].astype(F32)).astype(BF)
                dpre[rows] = d_pre
                bup[0:1, at : at + 512] += jnp.sum(d_pre.astype(F32), axis=0, keepdims=True)
                grad = mm_nt(d_pre, wf[slot, :, :, :, :, pl.ds(0, 512)].reshape(1024, 512))
                if step == 0:
                    dacc[rows] = grad
                else:
                    dacc[rows] += grad
                return carry

            lax.fori_loop(0, tiles, rows_body, 0)

            def grads_body(t, carry):
                rows = rows_of(t)
                up = mm(hlow_t[rows], dpre[...]).astype(BF)
                rbf[j, xx, t, :, :, :, pl.ds(0, 512)] = up.reshape(2, 2, 64, 512)
                down = mm(ddown_t[rows], act[slot]).astype(BF)
                rbf[j, xx, t, :, :, :, pl.ds(512, 512)] = down.reshape(2, 2, 64, 512)
                return carry

            lax.fori_loop(0, tiles, grads_body, 0)
            if xx == 1:
                rs.add(j, lambda j=j: rbf.at[j], got_f, j % 2, True, finisher(lambda j=j: (outf.at[j], outf_hbm.at[j])))
            for op in FFN_PLAN.get(step, ()):
                rs.stage(*op)

    pl.run_scoped(
        ffn,
        pltpu.VMEM((1024, LEN), BF), pltpu.VMEM((1024, LEN), BF),
        pltpu.VMEM((2, nz, 2, 2, 64, WF), BF), pltpu.VMEM((2, LEN, 512), BF), pltpu.VMEM((2, LEN, 512), BF),
        pltpu.VMEM((LEN, 512), BF),
    )

    def middle(dres, n1, inv1, go, dattn, dattn_t):
        ctx_in = start_local(ctx_hbm, ctx)
        ins = [
            start_local(dres_hbm, dres), start_local(n1_hbm, n1), start_local(inv1_hbm, inv1), start_local(go_hbm, go)
        ]
        for copy in ins:
            copy.wait()

        def norm(t, carry):
            rows = rows_of(t)
            dh = dres[rows] + dacc[rows]
            normed = n1[rows].astype(F32)
            w = dh * bias[4:5]
            first_mean = jnp.mean(w, axis=-1, keepdims=True)
            second_mean = jnp.mean(w * normed, axis=-1, keepdims=True)
            d = inv1[rows, 0:1] * (w - first_mean - normed * second_mean)
            low = d.astype(BF)
            dacc[rows] = d
            dattn[rows] = low
            vgrad[4:5] += jnp.sum(dh * normed, axis=0, keepdims=True)
            vgrad[5:6] += jnp.sum(dh, axis=0, keepdims=True)
            vgrad[2:3] += jnp.sum(low.astype(F32), axis=0, keepdims=True)
            return carry

        lax.fori_loop(0, tiles, norm, 0)
        transpose_into(dattn_t, dattn)
        ctx_in.wait()

        def grads_body(t, carry):
            rows = rows_of(t)
            for xx in range(2):
                part = mm(dattn_t[rows], ctx[:, xx * 512 : xx * 512 + 512]).astype(BF)
                rbo[xx, t] = part.reshape(2, 2, 64, 512)
                dctx[rows, xx * 512 : xx * 512 + 512] = mm(dattn[rows], go[xx].reshape(1024, 512)).astype(BF)
            return carry

        lax.fori_loop(0, tiles, grads_body, 0)
        rs.add(4, lambda: rbo, got_o, 0, True, finisher(lambda: (outo, outo_hbm)))
        for op in MIDDLE_PLAN:
            rs.stage(*op)

    pl.run_scoped(
        middle,
        pltpu.VMEM((LEN, 1024), F32), pltpu.VMEM((LEN, 1024), BF), pltpu.VMEM((LEN, 128), F32),
        pltpu.VMEM((2, nz, 2, 2, 64, WO), BF), pltpu.VMEM((LEN, 1024), BF), pltpu.VMEM((1024, LEN), BF),
    )

    def attention(tok, tok_t, wq, qa, kk, vv, ka, va, doa, kt, dqt, dj):
        ins = {}

        def load(step):
            i, xx, slot = step // 2, step % 2, step % 2
            pair = xx * 4 + i
            ins[step] = [
                start_local(qa_hbm.at[pair], qa.at[slot]),
                start_local(k_hbm.at[pair], kk.at[slot]),
                start_local(v_hbm.at[pair], vv.at[slot]),
            ]
            if xx == 0:
                ins[step].append(start_local(gq_hbm.at[i], wq.at[i % 2]))

        tok_in = start_local(tok_hbm, tok)
        load(0)
        tok_in.wait()
        transpose_into(tok_t, tok)
        lane = lax.broadcasted_iota(jnp.int32, (TILE, 128), 1)
        low_half = lane < 64
        for step in range(8):
            i, xx, slot = step // 2, step % 2, step % 2
            pair = xx * 4 + i
            cols = slice(pair * 128, pair * 128 + 128)
            for copy in ins[step]:
                copy.wait()
            if step + 1 < 8:
                load(step + 1)

            def prepare(t, carry):
                rows = rows_of(t)
                k_t, v_t, do_t = kk[slot, rows], vv[slot, rows], dctx[rows, cols]
                prod = do_t.astype(F32) * ctx[rows, cols].astype(F32)
                for h in range(2):
                    mine = low_half if h == 0 else jnp.logical_not(low_half)
                    at = 64 * (1 - h)
                    spare = jnp.where((lane >= at) & (lane < at + 3), 1.0, 0.0).astype(BF)
                    ka[h, rows] = jnp.where(mine, k_t, spare)
                    va[h, rows] = jnp.where(mine, v_t, spare)
                    inner = -jnp.sum(jnp.where(mine, prod, 0.0), axis=-1, keepdims=True)
                    hi = inner.astype(BF).astype(F32)
                    mid = (inner - hi).astype(BF).astype(F32)
                    rest = inner - hi - mid
                    extra = jnp.where(
                        lane == at, hi, jnp.where(lane == at + 1, mid, jnp.where(lane == at + 2, rest, 0.0))
                    )
                    doa[h, rows] = jnp.where(mine, do_t.astype(F32), extra).astype(BF)
                kt[:, rows] = k_t.T
                return carry

            for t in range(tiles):
                prepare(t, 0)

            def keys_body(t, carry):
                rows = rows_of(t)
                grads_k, grads_v = [], []
                for h in range(2):
                    scores = mm_nt(ka[h, rows], qa[slot, h])
                    probs = jnp.exp(scores)
                    d_weights = mm_nt(va[h, rows], doa[h])
                    d_scores = (probs * d_weights).astype(BF)
                    grads_v.append(mm(probs.astype(BF), dctx[:, cols]))
                    grads_k.append(mm(d_scores, qa[slot, h]))
                    part = mm(kt[h * 64 : h * 64 + 64, rows], d_scores)
                    dqt[h * 64 : h * 64 + 64] += part
                dj[xx, rows, 128:256] = jnp.where(low_half, grads_k[0], grads_k[1]).astype(BF)
                dj[xx, rows, 256:384] = jnp.where(low_half, grads_v[0], grads_v[1]).astype(BF)
                return carry

            dqt[...] = jnp.zeros_like(dqt)
            lax.fori_loop(0, tiles, keys_body, 0)
            for t in range(tiles):
                piece = dqt[:, t * TILE : t * TILE + TILE].astype(BF).astype(F32).T
                dj[xx, t * TILE : t * TILE + TILE, 0:128] = (piece * 0.125).astype(BF)
            sums = jnp.sum(dj[xx].astype(F32), axis=0, keepdims=True)
            vgrad[0:1, cols] = sums[:, 0:128]
            vgrad[1:2, cols] = sums[:, 256:384]

            def grads_body(t, carry):
                part = mm(tok_t[rows_of(t)], dj[xx]).astype(BF)
                rbq[i, xx, t] = part.reshape(2, 2, 64, WQ)
                return carry

            lax.fori_loop(0, tiles, grads_body, 0)

            def back(step_xx, step_i):
                def rows_body(t, carry):
                    rows = rows_of(t)
                    dacc[rows] += mm_nt(dj[step_xx, rows], wq[step_i % 2, step_xx].reshape(1024, WQ))
                    return carry

                lax.fori_loop(0, tiles, rows_body, 0)

            if step < 6:
                back(xx, i)
            if xx == 1:
                rs.add(5 + i, lambda i=i: rbq.at[i], got_q, i % 2, True, finisher(lambda i=i: (outq.at[i], outq_hbm.at[i])))
            if step == 7:


                def vectors_body(dev, carry):
                    to = rbv.at[lax.rem(dev, 2), dev // 8, lax.rem(dev // 4, 2), lax.rem(dev // 2, 2)]
                    to[0:8] = vgrad[:, pl.ds(pl.multiple_of(dev // 4 * 128, 128), 128)]
                    to[8:16] = bup[:, pl.ds(pl.multiple_of(dev * 128, 128), 128)]
                    return carry

                lax.fori_loop(0, 8 * nz, vectors_body, 0)
                rs.add(9, lambda: rbv, got_v, 0, False, finisher(lambda: (outv, outv_hbm)))
            for op in ATTN_PLAN.get(step, ()):
                rs.stage(*op)
        for op in DRAIN_PLAN[0]:
            rs.stage(*op)
        back(0, 3)
        for op in DRAIN_PLAN[1]:
            rs.stage(*op)
        back(1, 3)

        def last(t, carry):
            rows = rows_of(t)
            tok[rows] = dacc[rows].astype(BF)
            return carry

        lax.fori_loop(0, tiles, last, 0)
        ig = start_local(tok, ig_out)
        for op in DRAIN_PLAN[2]:
            rs.stage(*op)
        ig.wait()

    pl.run_scoped(
        attention,
        pltpu.VMEM((LEN, 1024), BF), pltpu.VMEM((1024, LEN), BF), pltpu.VMEM((2, 2, nz, 2, 2, 64, WQ), BF),
        pltpu.VMEM((2, 2, LEN, 128), BF), pltpu.VMEM((2, LEN, 128), BF), pltpu.VMEM((2, LEN, 128), BF),
        pltpu.VMEM((2, LEN, 128), BF), pltpu.VMEM((2, LEN, 128), BF), pltpu.VMEM((2, LEN, 128), BF),
        pltpu.VMEM((128, LEN), BF), pltpu.VMEM((128, LEN), F32), pltpu.VMEM((2, LEN, WQ), BF),
    )
    assert len(rs.done) == 50
    for name in rs.sent:
        name().wait_send()
    for name in out_copies:
        name().wait()


def ticks(*ks):
    return [(k - s, s) for k in ks for s in (4, 3, 2, 1, 0) if 0 <= k - s <= 9]


FFN_PLAN = {1: [(0, 0)], 2: [(0, 1)], 3: [(1, 0)], 4: [(0, 2), (1, 1)], 5: [(2, 0)], 7: [(0, 3), (1, 2), (2, 1), (3, 0)]}
MIDDLE_PLAN = []
ATTN_PLAN = {
    0: ticks(4),
    2: ticks(5),
    3: ticks(6),
    5: ticks(7),
    7: ticks(8),
}
DRAIN_PLAN = (ticks(9), ticks(10), ticks(11, 12, 13))


def backward_call(nz, tok, fwd):
    (_, dres, ddown, n1, inv1, hlow, act, slope, qa, k, v, ctx, gq, go, gf, bias, vsum) = fwd
    S, V = jax.ShapeDtypeStruct, pltpu.VMEM
    outs = [
        S((LEN, 1024), BF), S((4, 64, WF), F32), S((64, WO), F32), S((4, 64, WQ), F32), S((16, 128), F32),
    ]

    def slots(n, rows, w, kind):
        split = 2 if rows == 64 else 1
        r = rows // split
        return [
            V((n, 2, nz, 2, rows, w), kind), V((n, 2, nz, r, w), kind), V((n, nz, 2, r, w), kind),
            V((n, nz, r, w), kind), V((n, nz, r, w), kind), V((n, nz - 1, rows, w), kind),
        ]

    scratch = [
        V((4, 2, nz, 2, 2, 64, WF), BF), V((2, nz, 2, 2, 64, WO), BF), V((4, 2, nz, 2, 2, 64, WQ), BF),
        V((2, nz, 2, 2, 16, 128), F32),
        *slots(2, 64, WF, BF), *slots(1, 64, WO, BF), *slots(2, 64, WQ, BF), *slots(1, 16, 128, F32),
        V((LEN, 1024), F32), V((LEN, 1024), BF), V((LEN, 1024), BF), V((8, 1024), F32), V((8, 4096), F32),
        V((4, 64, WF), F32), V((64, WO), F32), V((4, 64, WQ), F32), V((16, 128), F32),
        pltpu.SemaphoreType.DMA((10, 8)), pltpu.SemaphoreType.DMA((10, 8)), pltpu.SemaphoreType.DMA((80,)),
    ]
    hbm, vmem = pl.BlockSpec(memory_space=pl.ANY), pl.BlockSpec(memory_space=pltpu.VMEM)
    return pl.pallas_call(
        functools.partial(backward_kernel, nz),
        out_shape=outs,
        in_specs=[hbm] * 15 + [vmem, vmem],
        out_specs=[hbm] * len(outs),
        scratch_shapes=scratch,
        compiler_params=pltpu.CompilerParams(
            collective_id=1, has_side_effects=True, vmem_limit_bytes=63 * 1024 * 1024
        ),
        cost_estimate=pl.CostEstimate(flops=60 * 10**9, bytes_accessed=10**8, transcendentals=2 * 10**7),
        name="backward",
    )(tok, hlow, ddown, dres, n1, inv1, act, slope, qa, k, v, ctx, gq, go, gf, bias, vsum)


def unpack(back):
    ig, gf, go, gq, gv = back
    parts = gq.reshape(4, 64, 3, 128).transpose(2, 1, 0, 3).reshape(3, 64, 512)
    up = gf[:, :, :512].transpose(1, 0, 2).reshape(64, 2048)
    down = gf[:, :, 512:].transpose(0, 2, 1).reshape(2048, 64)
    dev = lax.axis_index("dp") * 2 + lax.axis_index("tensor")
    mine = lax.dynamic_slice_in_dim(gv[:8], (dev % 4) * 32, 32, axis=1)
    vec = [mine[r] for r in range(8)]
    return (
        ig, parts[0], parts[1], parts[2], go.T, up, down,
        vec[0], vec[1], gv[8], vec[2], vec[3], vec[4], vec[5], vec[6], vec[7],
    )


def layer_stats(resid):
    center = resid - jnp.mean(resid, axis=-1, keepdims=True)
    inverse = lax.rsqrt(jnp.mean(center * center, axis=-1, keepdims=True) + EPS)
    return (center * inverse, inverse)


def norm_back(grad_in, normed, inverse, gain):
    scaled = grad_in * gain
    first_mean = jnp.mean(scaled, axis=-1, keepdims=True)
    second_mean = jnp.mean(scaled * normed, axis=-1, keepdims=True)
    return inverse * (scaled - first_mean - normed * second_mean)


def gelu_slope(values):
    return (
        0.5 * (1.0 + lax.erf(values * SQRT_HALF))
        + values * jnp.exp(-0.5 * values * values) * INV_ROOT_TAU
    )


def split_heads(matrix):
    return matrix.reshape(matrix.shape[0], matrix.shape[1] // HEAD_DIM, HEAD_DIM)


def widen(part_sum, full_length, offset):
    return lax.dynamic_update_slice_in_dim(
        jnp.zeros((full_length,), jnp.float32), part_sum, offset, 0
    )


def attend_forward(block):
    query_b, key_b, value_b = block
    query_h = split_heads(query_b)
    key_h = split_heads(key_b)
    value_h = split_heads(value_b)
    scores = jnp.einsum("qhd,khd->hqk", query_h, key_h, preferred_element_type=jnp.float32)
    largest = jnp.max(scores, axis=-1, keepdims=True)
    expons = jnp.exp(scores - largest)
    totals = jnp.sum(expons, axis=-1, keepdims=True)
    attn_weights = (expons / totals).astype(jnp.bfloat16)
    context = jnp.einsum("hqk,khd->qhd", attn_weights, value_h, preferred_element_type=jnp.float32)
    return (
        context.reshape(query_b.shape).astype(jnp.bfloat16),
        (largest + jnp.log(totals))[:, :, 0],
    )


def attend_backward(block):
    query_b, key_b, value_b, logsum, grad_ctx = block
    query_h = split_heads(query_b)
    key_h = split_heads(key_b)
    value_h = split_heads(value_b)
    grad_h = split_heads(grad_ctx)
    scores = jnp.einsum("qhd,khd->hqk", query_h, key_h, preferred_element_type=jnp.float32)
    weights_full = jnp.exp(scores - logsum[:, :, None])
    weights_low = weights_full.astype(jnp.bfloat16)
    grad_value = jnp.einsum("hqk,qhd->khd", weights_low, grad_h, preferred_element_type=jnp.float32)
    grad_weights = jnp.einsum("qhd,khd->hqk", grad_h, value_h, preferred_element_type=jnp.float32)
    inner = jnp.sum(weights_full * grad_weights, axis=-1, keepdims=True)
    grad_scores = (weights_full * (grad_weights - inner)).astype(jnp.bfloat16)
    grad_query = jnp.einsum("hqk,khd->qhd", grad_scores, key_h, preferred_element_type=jnp.float32)
    grad_key = jnp.einsum("hqk,qhd->khd", grad_scores, query_h, preferred_element_type=jnp.float32)
    full_shape = query_b.shape
    return (
        grad_query.reshape(full_shape).astype(jnp.bfloat16),
        grad_key.reshape(full_shape).astype(jnp.bfloat16),
        grad_value.reshape(full_shape).astype(jnp.bfloat16),
    )


def on_device(
    tokens,
    weight_query,
    weight_key,
    weight_value,
    weight_output,
    weight_up,
    weight_down,
    bias_query,
    bias_value,
    bias_up,
    bias_output,
    bias_down,
    first_gain,
    first_shift,
    second_gain,
    second_shift,
    out_grad,
):
    w_query, w_key, w_value, w_output, w_up, w_down = (
        lax.all_gather(weight_query, "dp", axis=0, tiled=True),
        lax.all_gather(weight_key, "dp", axis=0, tiled=True),
        lax.all_gather(weight_value, "dp", axis=0, tiled=True),
        lax.all_gather(weight_output, "dp", axis=1, tiled=True),
        lax.all_gather(weight_up, "dp", axis=0, tiled=True),
        lax.all_gather(weight_down, "dp", axis=1, tiled=True),
    )
    vectors = (
        lax.all_gather(bias_query, ("dp", "tensor"), axis=0, tiled=True),
        lax.all_gather(bias_value, ("dp", "tensor"), axis=0, tiled=True),
        lax.all_gather(bias_up, ("dp", "tensor"), axis=0, tiled=True),
        lax.all_gather(bias_output, ("dp", "tensor"), axis=0, tiled=True),
        lax.all_gather(bias_down, ("dp", "tensor"), axis=0, tiled=True),
        lax.all_gather(first_gain, ("dp", "tensor"), axis=0, tiled=True),
        lax.all_gather(first_shift, ("dp", "tensor"), axis=0, tiled=True),
        lax.all_gather(second_gain, ("dp", "tensor"), axis=0, tiled=True),
        lax.all_gather(second_shift, ("dp", "tensor"), axis=0, tiled=True),
    )
    query_all, value_all, up_all, out_bias, down_bias, gain_one, shift_one, gain_two, shift_two = [
        member.astype(jnp.float32) for member in vectors
    ]
    width_here = w_query.shape[1]
    hidden_here = w_up.shape[1]
    full_hidden = up_all.shape[0]
    model_width = tokens.shape[1]
    tensor_pos = lax.axis_index("tensor")
    query_bias = lax.dynamic_slice_in_dim(query_all, tensor_pos * width_here, width_here)
    value_bias = lax.dynamic_slice_in_dim(value_all, tensor_pos * width_here, width_here)
    scale = HEAD_DIM ** (-0.5)
    gathered = lax.all_gather(tokens, "tensor", axis=0, tiled=True)
    joined = jnp.concatenate([w_query, w_key, w_value], axis=1)
    projected = jnp.dot(gathered, joined, preferred_element_type=jnp.float32)
    query_b = ((projected[:, :width_here] + query_bias) * scale).astype(jnp.bfloat16)
    key_b = projected[:, width_here : 2 * width_here].astype(jnp.bfloat16)
    value_b = (projected[:, 2 * width_here :] + value_bias).astype(jnp.bfloat16)
    seq_count = gathered.shape[0] // LEN

    def by_sequence(matrix):
        return matrix.reshape(seq_count, LEN, matrix.shape[-1])

    context, logsum = lax.map(
        attend_forward, (by_sequence(query_b), by_sequence(key_b), by_sequence(value_b))
    )
    context = context.reshape(-1, width_here)
    attn_sum = lax.psum_scatter(
        jnp.dot(context, w_output, preferred_element_type=jnp.float32).astype(jnp.bfloat16),
        "tensor",
        scatter_dimension=0,
        tiled=True,
    ).astype(jnp.float32)
    resid_one = tokens.astype(jnp.float32) + (attn_sum + out_bias)
    normed_one, inverse_one = layer_stats(resid_one)
    hidden = normed_one * gain_one + shift_one
    hidden_low = hidden.astype(jnp.bfloat16)
    ffn_rows = lax.all_gather(hidden_low, "tensor", axis=0, tiled=True)
    up_use, down_use = (w_up, w_down)
    up_bias = lax.dynamic_slice_in_dim(up_all, tensor_pos * hidden_here, hidden_here)
    preact = jnp.dot(ffn_rows, up_use, preferred_element_type=jnp.float32) + up_bias
    active = jax.nn.gelu(preact, approximate=False).astype(jnp.bfloat16)
    down_sum = lax.psum_scatter(
        jnp.dot(active, down_use, preferred_element_type=jnp.float32).astype(jnp.bfloat16),
        "tensor",
        scatter_dimension=0,
        tiled=True,
    ).astype(jnp.float32)
    resid_two = hidden + (down_sum + down_bias)
    normed_two, inverse_two = layer_stats(resid_two)
    layer_out = (normed_two * gain_two + shift_two).astype(jnp.bfloat16)
    grad_top = out_grad.astype(jnp.float32)
    grad_gain_two = jnp.sum(grad_top * normed_two, axis=0)
    grad_shift_two = jnp.sum(grad_top, axis=0)
    d_resid_two = norm_back(grad_top, normed_two, inverse_two, gain_two)
    d_down = d_resid_two.astype(jnp.bfloat16)
    grad_down_bias = jnp.sum(d_down, axis=0, dtype=jnp.float32)
    d_rows = lax.all_gather(d_down, "tensor", axis=0, tiled=True)
    grad_down = jnp.einsum("nf,nd->fd", active, d_rows, preferred_element_type=jnp.float32)
    d_active = jnp.einsum("nd,fd->nf", d_rows, down_use, preferred_element_type=jnp.float32)
    d_pre = (d_active * gelu_slope(preact)).astype(jnp.bfloat16)
    grad_up_part = jnp.sum(d_pre, axis=0, dtype=jnp.float32)
    grad_up = jnp.einsum("nd,nf->df", ffn_rows, d_pre, preferred_element_type=jnp.float32)
    d_from_ffn = lax.psum_scatter(
        jnp.einsum("nf,df->nd", d_pre, up_use, preferred_element_type=jnp.float32).astype(
            jnp.bfloat16
        ),
        "tensor",
        scatter_dimension=0,
        tiled=True,
    ).astype(jnp.float32)
    grad_up_bias = widen(grad_up_part, full_hidden, tensor_pos * hidden_here)
    d_hidden = d_resid_two + d_from_ffn
    grad_gain_one = jnp.sum(d_hidden * normed_one, axis=0)
    grad_shift_one = jnp.sum(d_hidden, axis=0)
    d_resid_one = norm_back(d_hidden, normed_one, inverse_one, gain_one)
    d_attn = d_resid_one.astype(jnp.bfloat16)
    grad_out_bias = jnp.sum(d_attn, axis=0, dtype=jnp.float32)
    d_attn_rows = lax.all_gather(d_attn, "tensor", axis=0, tiled=True)
    grad_output = jnp.einsum("nc,nd->cd", context, d_attn_rows, preferred_element_type=jnp.float32)
    d_context = jnp.einsum(
        "nd,cd->nc", d_attn_rows, w_output, preferred_element_type=jnp.float32
    ).astype(jnp.bfloat16)
    d_query, d_key, d_value = lax.map(
        attend_backward,
        (
            by_sequence(query_b),
            by_sequence(key_b),
            by_sequence(value_b),
            logsum,
            by_sequence(d_context),
        ),
    )
    d_joined = jnp.concatenate(
        [
            (d_query * scale).reshape(-1, width_here),
            d_key.reshape(-1, width_here),
            d_value.reshape(-1, width_here),
        ],
        axis=1,
    )
    grad_joined = jnp.einsum("nd,nc->dc", gathered, d_joined, preferred_element_type=jnp.float32)
    grad_query_w = grad_joined[:, :width_here]
    grad_key_w = grad_joined[:, width_here : 2 * width_here]
    grad_value_w = grad_joined[:, 2 * width_here :]
    bias_sums = jnp.sum(d_joined, axis=0, dtype=jnp.float32)
    grad_query_bias = widen(bias_sums[:width_here], model_width, tensor_pos * width_here)
    grad_value_bias = widen(bias_sums[2 * width_here :], model_width, tensor_pos * width_here)
    d_from_attn = lax.psum_scatter(
        jnp.einsum("nc,dc->nd", d_joined, joined, preferred_element_type=jnp.float32).astype(
            jnp.bfloat16
        ),
        "tensor",
        scatter_dimension=0,
        tiled=True,
    ).astype(jnp.float32)
    input_grad = (d_resid_one + d_from_attn).astype(jnp.bfloat16)
    grad_query_w, grad_key_w, grad_value_w, grad_output, grad_up, grad_down = (
        lax.psum_scatter(
            grad_query_w.astype(jnp.bfloat16), "dp", scatter_dimension=0, tiled=True
        ).astype(jnp.float32),
        lax.psum_scatter(
            grad_key_w.astype(jnp.bfloat16), "dp", scatter_dimension=0, tiled=True
        ).astype(jnp.float32),
        lax.psum_scatter(
            grad_value_w.astype(jnp.bfloat16), "dp", scatter_dimension=0, tiled=True
        ).astype(jnp.float32),
        lax.psum_scatter(
            grad_output.astype(jnp.bfloat16), "dp", scatter_dimension=1, tiled=True
        ).astype(jnp.float32),
        lax.psum_scatter(
            grad_up.astype(jnp.bfloat16), "dp", scatter_dimension=0, tiled=True
        ).astype(jnp.float32),
        lax.psum_scatter(
            grad_down.astype(jnp.bfloat16), "dp", scatter_dimension=1, tiled=True
        ).astype(jnp.float32),
    )
    vector_sums = (
        lax.psum_scatter(grad_query_bias, ("dp", "tensor"), scatter_dimension=0, tiled=True),
        lax.psum_scatter(grad_value_bias, ("dp", "tensor"), scatter_dimension=0, tiled=True),
        lax.psum_scatter(grad_up_bias, ("dp", "tensor"), scatter_dimension=0, tiled=True),
        lax.psum_scatter(grad_out_bias, ("dp", "tensor"), scatter_dimension=0, tiled=True),
        lax.psum_scatter(grad_down_bias, ("dp", "tensor"), scatter_dimension=0, tiled=True),
        lax.psum_scatter(grad_gain_one, ("dp", "tensor"), scatter_dimension=0, tiled=True),
        lax.psum_scatter(grad_shift_one, ("dp", "tensor"), scatter_dimension=0, tiled=True),
        lax.psum_scatter(grad_gain_two, ("dp", "tensor"), scatter_dimension=0, tiled=True),
        lax.psum_scatter(grad_shift_two, ("dp", "tensor"), scatter_dimension=0, tiled=True),
    )
    return (
        layer_out,
        input_grad,
        grad_query_w,
        grad_key_w,
        grad_value_w,
        grad_output,
        grad_up,
        grad_down,
    ) + tuple(vector_sums)


def whole_sequences(*args):
    (tokens, wq, wk, wv, wo, wu, wd, bq, bv, bu, bo, bd, g1, s1, g2, s2, out_grad) = args
    vectors = dict(bq=bq, bv=bv, bu=bu, bo=bo, bd=bd, g1=g1, s1=s1, g2=g2, s2=s2)
    shards = pack(wq, wk, wv, wo, wu, wd, vectors)
    nz = lax.axis_size("dp") // 4
    fwd = forward_call(nz, tokens, out_grad, *shards)
    back = backward_call(nz, tokens, fwd)
    return (fwd[0],) + unpack(back)


def either(*args):
    sizes = (lax.axis_size("dp"), lax.axis_size("tensor"))
    fits = args[0].shape == (LEN, 1024) and args[5].shape[1] * 2 == 4096 and sizes == (16, 2)
    return whole_sequences(*args) if fits else on_device(*args)


def solution(mesh):
    placed = (
        P(("dp", "tensor"), None),
        P("dp", "tensor"),
        P("dp", "tensor"),
        P("dp", "tensor"),
        P("tensor", "dp"),
        P("dp", "tensor"),
        P("tensor", "dp"),
        P(("dp", "tensor")),
        P(("dp", "tensor")),
        P(("dp", "tensor")),
        P(("dp", "tensor")),
        P(("dp", "tensor")),
        P(("dp", "tensor")),
        P(("dp", "tensor")),
        P(("dp", "tensor")),
        P(("dp", "tensor")),
        P(("dp", "tensor"), None),
    )
    return jax.shard_map(
        either,
        mesh=mesh,
        in_specs=placed,
        out_specs=(
            P(("dp", "tensor"), None),
            P(("dp", "tensor"), None),
            P("dp", "tensor"),
            P("dp", "tensor"),
            P("dp", "tensor"),
            P("tensor", "dp"),
            P("dp", "tensor"),
            P("tensor", "dp"),
            P(("dp", "tensor")),
            P(("dp", "tensor")),
            P(("dp", "tensor")),
            P(("dp", "tensor")),
            P(("dp", "tensor")),
            P(("dp", "tensor")),
            P(("dp", "tensor")),
            P(("dp", "tensor")),
            P(("dp", "tensor")),
        ),
        check_vma=False,
    )
```

```python
import functools
import jax
import jax.numpy as jnp
from jax import lax
from jax.experimental import pallas as pl
from jax.experimental.pallas import tpu as pltpu
from jax.sharding import PartitionSpec as P

HEAD_DIM = 64
LEN = 1024
EPS = 1e-05
SQRT_HALF = 0.7071067811865476
INV_ROOT_TAU = 0.3989422804014327
BF, F32 = jnp.bfloat16, jnp.float32
MESH = pl.DeviceIdType.MESH
NT = (((1,), (1,)), ((), ()))
TILE = 512
TILES = LEN // TILE
SIDE = 256
QW = 384
FW = 512

FORWARD_PLAN = {"a0": 2, "a2": 3, "a4": 4, "a5": 5, "a6": 6, "a7": 7, "n": 8, "f0": 9, "f2": 10, "f4": 12, "f6": 13}
BACKWARD_PLAN = {
    "f1": [(0, 0)], "f2": [(0, 1), (1, 0)], "f3": [(0, 2), (1, 1), (2, 0)], "f4": [2 + 1], "f5": [4],
    "f6": [5], "f7": [6], "m": [7], "a0": [8], "a2": [9], "a4": [10], "a6": [11],
}


def tile_rows(t):
    return pl.ds(t * TILE if isinstance(t, int) else pl.multiple_of(t * TILE, TILE), TILE)


def tile_blocks(t):
    return pl.ds(t * (TILE // 256), TILE // 256)


def mm(a, b):
    return jnp.dot(a, b, preferred_element_type=F32)


def mm_nt(a, b):
    return lax.dot_general(a, b, NT, preferred_element_type=F32)


def gelu_both(z):
    far = 1.0 / (1.0 + (0.3275911 * SQRT_HALF) * jnp.abs(z))
    bell = jnp.exp(-0.5 * z * z)
    poly = far * (
        0.127414796
        + far * (-0.142248368 + far * (0.7107068705 + far * (-0.7265760135 + far * 0.5307027145)))
    )
    tail = poly * bell
    cdf = jnp.where(z >= 0, 1.0 - tail, tail)
    return z * cdf, cdf + z * bell * INV_ROOT_TAU


def ln_stats(resid):
    center = resid - jnp.mean(resid, axis=-1, keepdims=True)
    inverse = lax.rsqrt(jnp.mean(center * center, axis=-1, keepdims=True) + EPS)
    return center * inverse, inverse


def three_terms(value, lane, at):
    hi = value.astype(BF).astype(F32)
    mid = (value - hi).astype(BF).astype(F32)
    rest = value - hi - mid
    return jnp.where(lane == at, hi, jnp.where(lane == at + 1, mid, jnp.where(lane == at + 2, rest, 0.0)))


def device(z, y, c, x):
    return {"dp": (z * 2 + y) * 2 + c, "tensor": x}


class Place:
    def __init__(self, nz):
        dp, x = lax.axis_index("dp"), lax.axis_index("tensor")
        z, y, c = dp // 4, lax.rem(dp // 2, 2), lax.rem(dp, 2)
        self.nz, self.z, self.y, self.c, self.x = nz, z, y, c, x
        self.not_y, self.not_c, self.not_x = 1 - y, 1 - c, 1 - x
        self.z_at = [z] + [lax.rem(z + s, nz) for s in range(1, nz)]
        self.to_z = [None] + [device(at, y, c, x) for at in self.z_at[1:]]
        self.to_y, self.to_c, self.to_x = device(z, 1 - y, c, x), device(z, y, 1 - c, x), device(z, y, c, 1 - x)

    def lanes(self, w):
        return pl.ds(pl.multiple_of(self.x * w, 128), w)

    def other_lanes(self, w):
        return pl.ds(pl.multiple_of(self.not_x * w, 128), w)

    def greet(self):
        bar = pltpu.get_barrier_semaphore()
        others = self.to_z[1:] + [self.to_y, self.to_c, self.to_x]
        for other in others:
            pl.semaphore_signal(bar, inc=1, device_id=other, device_id_type=MESH)
        pl.semaphore_wait(bar, len(others))


class Mover:
    def __init__(self, at, send, recv):
        self.at, self.send, self.recv, self.sent = at, send, recv, []

    def go(self, k, slot, src, dst, to):
        copy = pltpu.make_async_remote_copy(
            src_ref=src,
            dst_ref=dst,
            send_sem=self.send.at[k, slot],
            recv_sem=self.recv.at[k, slot],
            device_id=to,
            device_id_type=MESH,
        )
        copy.start()
        self.sent.append(copy)
        return copy


class Gather(Mover):
    def __init__(self, at, send, recv, chunks):
        super().__init__(at, send, recv)
        self.chunks, self.flying, self.next = chunks, {}, 0

    def wait(self, k, stage):
        for copy in self.flying.pop((k, stage)):
            copy.wait_recv()

    def along_z(self, k):
        at, (buf, w, split) = self.at, self.chunks[k]
        own = buf.at[at.z, at.y, at.c, :, at.lanes(w)]
        self.flying[(k, 0)] = [self.go(k, s - 1, own, own, at.to_z[s]) for s in range(1, at.nz)]

    def first(self, k):
        self.wait(k, 0)
        at, (buf, w, split) = self.at, self.chunks[k]
        r = 32 if split else buf.shape[3]
        up = buf.at[:, at.y, at.c, pl.ds(0, r), at.lanes(w)]
        copies = [self.go(k, 3, up, up, at.to_x)]
        if split:
            down = buf.at[:, at.y, at.c, pl.ds(r, r), at.lanes(w)]
            copies.append(self.go(k, 4, down, down, at.to_y))
        self.flying[(k, 1)] = copies

    def second(self, k):
        self.wait(k, 1)
        at, (buf, w, split) = self.at, self.chunks[k]
        r = 32 if split else buf.shape[3]
        up = buf.at[:, at.y, at.c, pl.ds(0, r)]
        copies = [self.go(k, 5, up, up, at.to_y)]
        if split:
            down = buf.at[:, :, at.c, pl.ds(r, r), at.lanes(w)]
            copies.append(self.go(k, 6, down, down, at.to_x))
        self.flying[(k, 2)] = copies

    def core(self, k):
        self.wait(k, 2)
        at, (buf, w, split) = self.at, self.chunks[k]
        part = buf.at[:, :, at.c]
        self.flying[(k, 3)] = [self.go(k, 7, part, part, at.to_c)]

    def push(self, upto):
        while self.next <= min(upto, len(self.chunks) - 1):
            k = self.next
            if k + 2 < len(self.chunks):
                self.first(k + 2)
            if k + 1 < len(self.chunks):
                self.second(k + 1)
            self.core(k)
            self.next += 1

    def ready(self, k):
        self.push(k)
        self.wait(k, 3)


class Scatter(Mover):
    def __init__(self, at, send, recv, count):
        super().__init__(at, send, recv)
        self.chunks, self.flying, self.done, self.count = {}, {}, set(), count

    def add(self, k, buf, w, got, split, finish):
        self.chunks[k] = (buf, w, got, split, finish)

    def stage(self, k, s):
        at, nz = self.at, self.at.nz
        z, y, c = at.z, at.y, at.c
        buf, w, (got_c, got_y, got_x, got_y2, got_x2, got_z), split, finish = self.chunks[k]
        r = 32 if split else buf.shape[3]
        up, down = pl.ds(0, r), pl.ds(r, r)
        mine, other = at.lanes(w), at.other_lanes(w)
        assert (k, s) not in self.done and (s == 0 or (k, s - 1) in self.done)
        assert s == 4 or k == 0 or (k - 1, s + 1) in self.done
        self.done.add((k, s))
        for copy in self.flying.pop((k, s - 1), []):
            copy.wait_recv()
        copies = []
        if s == 0:
            copies = [self.go(k, 0, buf.at[:, :, at.not_c], got_c, at.to_c)]
        elif s == 1:

            def fold(m, carry):
                zz, yy = m // 2, lax.rem(m, 2)
                buf[zz, yy, c] += got_c[zz, yy]
                return carry

            lax.fori_loop(0, 2 * nz, fold, 0)
            copies = [self.go(k, 1, buf.at[:, at.not_y, c, up], got_y, at.to_y)]
            if split:
                copies.append(self.go(k, 2, buf.at[:, :, c, down, other], got_x, at.to_x))
        elif s == 2:

            def fold(zz, carry):
                buf[zz, y, c, up] += got_y[zz]
                if split:
                    for yy in range(2):
                        buf[zz, yy, c, down, mine] += got_x[zz, yy]
                return carry

            lax.fori_loop(0, nz, fold, 0)
            copies = [self.go(k, 3, buf.at[:, y, c, up, other], got_x2, at.to_x)]
            if split:
                copies.append(self.go(k, 4, buf.at[:, at.not_y, c, down, mine], got_y2, at.to_y))
        elif s == 3:

            def fold(zz, carry):
                buf[zz, y, c, up, mine] += got_x2[zz]
                if split:
                    buf[zz, y, c, down, mine] += got_y2[zz]
                return carry

            lax.fori_loop(0, nz, fold, 0)
            copies = [
                self.go(k, 4 + d, buf.at[at.z_at[d], y, c, :, mine], got_z.at[d - 1], at.to_z[d])
                for d in range(1, nz)
            ]
        else:
            total = buf[z, y, c, :, mine].astype(F32)
            for d in range(1, nz):
                total = total + got_z[d - 1].astype(F32)
            finish(total)
        self.flying[(k, s)] = copies

    def run(self, plan):
        for item in plan:
            if isinstance(item, tuple):
                self.stage(*item)
                continue
            for s in (4, 3, 2, 1, 0):
                k = item - s
                if 0 <= k < self.count and (k, s) not in self.done:
                    self.stage(k, s)


def transpose_in_place(ref):
    for a in range(LEN // SIDE):
        for b in range(a, LEN // SIDE):
            ra, rb = slice(a * SIDE, a * SIDE + SIDE), slice(b * SIDE, b * SIDE + SIDE)
            first = ref[ra, rb].T
            if a != b:
                ref[ra, rb] = ref[rb, ra].T
            ref[rb, ra] = first


def transpose_into(dst, src):
    for t in range(LEN // SIDE):
        dst[:, t * SIDE : t * SIDE + SIDE] = src[t * SIDE : t * SIDE + SIDE].T


def layer_kernel(
    nz,
    tok_hbm, og_hbm, wq_hbm, wk_hbm, wv_hbm, wo_hbm, wu_hbm, wd_hbm, sv,
    lo_hbm, ig_hbm, outu_hbm, outd_hbm, outo_hbm, outq_hbm, outv_hbm, pair_hbm, qa_hbm, act_hbm,
    gv, gq, go, gu, gd, exq, bias, bup, tok, ctx, acc, n1, inv1, hlow, ddown, ddown_t, mixed, work,
    qs, kv, qa, kt, dqt, vgrad,
    rc, ry, rx, ry2, rx2, rz, rbv, rcv, ryv, rxv, ry2v, rx2v, rzv, out, outv,
    send, recv, send2, recv2, lsem,
):
    at = Place(nz)
    used = [0]

    def start_local(src, dst):
        copy = pltpu.make_async_copy(src, dst, lsem.at[used[0]])
        used[0] += 1
        copy.start()
        return copy

    def loop(body, n=TILES):
        def step(t, carry):
            body(t)
            return carry

        lax.fori_loop(0, n, step, 0)

    own = (at.z, at.y, at.c)
    chunks = [(gv, 128, False)]
    chunks += [(gq.at[i], QW, True) for i in range(4)] + [(go, FW, True)]
    for j in range(4):
        chunks += [(gu.at[j], FW, True), (gd.at[j], FW, True)]
    placed = [[] for _ in chunks]
    for i in range(4):
        for m, w_hbm in enumerate((wq_hbm, wk_hbm, wv_hbm)):
            lanes = pl.ds(pl.multiple_of(at.x * QW + m * 128, 128), 128)
            placed[1 + i].append(start_local(w_hbm.at[:, pl.ds(i * 128, 128)], gq.at[(i, *own, slice(None), lanes)]))
    tok_in = start_local(tok_hbm, tok)
    placed[5].append(start_local(wo_hbm, go.at[(*own, slice(None), at.lanes(FW))]))
    for j in range(4):
        for m, (w_hbm, g) in enumerate(((wu_hbm, gu), (wd_hbm, gd))):
            placed[6 + 2 * j + m].append(
                start_local(w_hbm.at[:, pl.ds(j * FW, FW)], g.at[(j, *own, slice(None), at.lanes(FW))])
            )
    og_in = start_local(og_hbm, mixed)
    gv[at.z, at.y, at.c, :, at.lanes(128)] = sv[...]
    at.greet()
    gather = Gather(at, send, recv, chunks)
    for k in range(len(chunks)):
        for copy in placed[k]:
            copy.wait()
        gather.along_z(k)
    gather.first(0)
    gather.first(1)
    gather.second(0)
    gather.ready(0)
    for t in range(8):
        sums = None
        for owner in range(4 * t, 4 * t + 4):
            dp_o, x_o = owner // 2, owner % 2
            block = gv[dp_o // 4, dp_o // 2 % 2, dp_o % 2, :, x_o * 128 : x_o * 128 + 128].astype(F32)
            sums = block if sums is None else sums + block
            bup[:, owner * 128 : owner * 128 + 128] = jnp.broadcast_to(block[8:9], (8, 128))
        bias[:, t * 128 : t * 128 + 128] = sums
    tok_in.wait()

    lane = lax.broadcasted_iota(jnp.int32, (TILE, 128), 1)
    low_half = lane < 64
    halves = (low_half, jnp.logical_not(low_half))

    def project(i):
        def body(t):
            rows = tile_rows(t)
            part = mm(tok[rows], gq[i].reshape(1024, 2 * QW))
            for xx in range(2):
                pair, base = xx * 4 + i, xx * QW
                bq = bias[0:1, pair * 128 : pair * 128 + 128]
                bv = bias[1:2, pair * 128 : pair * 128 + 128]
                qs[xx, rows] = ((part[:, base : base + 128] + bq) * 0.125).astype(BF)
                key = part[:, base + 128 : base + 256].astype(BF)
                value = (part[:, base + 256 : base + 384] + bv).astype(BF)
                one = jnp.ones_like(key)
                for h in range(2):
                    kv[xx, h, rows] = jnp.where(halves[h], key, one)
                    kv[xx, 2 + h, rows] = jnp.where(halves[h], value, one)

        loop(body)

    def attend(i, xx):
        pair = xx * 4 + i

        def body(t):
            rows = tile_rows(t)
            q = qs[xx, rows]
            scores = [mm_nt(jnp.where(halves[h], q, jnp.zeros_like(q)), kv[xx, h]) for h in range(2)]
            tops = [jnp.max(s, axis=-1, keepdims=True) for s in scores]
            expons = [jnp.exp(s - top).astype(BF) for s, top in zip(scores, tops)]
            outs = [mm(expons[h], kv[xx, 2 + h]) for h in range(2)]
            for h in range(2):
                extra = three_terms(-(tops[h] + jnp.log(outs[h])), lane, 64 * (1 - h))
                qa[xx, h, rows] = jnp.where(halves[h], q.astype(F32), extra).astype(BF)
            total = pltpu.roll(jnp.where(low_half, outs[1], outs[0]), 64, 1)
            ctx[rows, pair * 128 : pair * 128 + 128] = (jnp.where(low_half, outs[0], outs[1]) / total).astype(BF)

        loop(body)

    spilled = []
    for i in range(4):
        gather.ready(1 + i)
        for copy in spilled:
            copy.wait()
        spilled = []
        project(i)
        for xx in range(2):
            attend(i, xx)
            spilled += [start_local(kv.at[xx], pair_hbm.at[xx * 4 + i]), start_local(qa.at[xx], qa_hbm.at[xx * 4 + i])]
            gather.push(FORWARD_PLAN.get(f"a{2 * i + xx}", 0))

    gather.ready(5)

    def first_norm(t):
        rows = tile_rows(t)
        attn = mm_nt(ctx[rows], go[...].reshape(1024, 1024))
        normed, inverse = ln_stats(tok[rows].astype(F32) + (attn + bias[2:3]))
        n1[rows] = normed.astype(BF)
        inv1[rows] = jnp.broadcast_to(inverse, (TILE, 128))
        h = normed * bias[4:5] + bias[5:6]
        acc[rows] = h
        hlow[rows] = h.astype(BF)

    loop(first_norm)
    for copy in spilled:
        copy.wait()
    gather.push(FORWARD_PLAN.get("n", 0))
    transpose_in_place(tok)

    def ffn_step(j, xx, slot):
        up, down = gu.at[j, :, :, :, :, pl.ds(xx * FW, FW)], gd.at[j, :, :, :, :, pl.ds(xx * FW, FW)]
        first = xx * 2048 + j * FW
        b_up = bup[0:1, first : first + FW]

        def body(t):
            rows = tile_rows(t)
            value, grade = gelu_both(mm(hlow[rows], up[...].reshape(1024, FW)) + b_up)
            value = value.astype(BF)
            work[slot, rows, 0:FW] = value
            work[slot, rows, FW:] = grade.astype(BF)
            acc[rows] += mm_nt(value, down[...].reshape(1024, FW))

        loop(body)

    stored = {}
    for j in range(4):
        gather.ready(6 + 2 * j)
        gather.ready(7 + 2 * j)
        for xx in range(2):
            step = 2 * j + xx
            if step >= 2:
                stored.pop(step - 2).wait()
            ffn_step(j, xx, step % 2)
            stored[step] = start_local(work.at[step % 2], act_hbm.at[step])
            gather.push(FORWARD_PLAN.get(f"f{step}", 0))
    og_in.wait()
    vgrad[...] = jnp.zeros_like(vgrad)
    bgrad = bup
    bgrad[...] = jnp.zeros_like(bgrad)

    def second_norm(t):
        rows = tile_rows(t)
        normed, inverse = ln_stats(acc[rows] + bias[3:4])
        g = mixed[rows].astype(F32)
        mixed[rows] = (normed * bias[6:7] + bias[7:8]).astype(BF)
        u = g * bias[6:7]
        first_mean = jnp.mean(u, axis=-1, keepdims=True)
        second_mean = jnp.mean(u * normed, axis=-1, keepdims=True)
        d = inverse * (u - first_mean - normed * second_mean)
        acc[rows] = d
        low = d.astype(BF)
        ddown[rows] = low
        vgrad[6:7] += jnp.sum(g * normed, axis=0, keepdims=True)
        vgrad[7:8] += jnp.sum(g, axis=0, keepdims=True)
        vgrad[3:4] += jnp.sum(low.astype(F32), axis=0, keepdims=True)

    loop(second_norm)
    lo_copy = start_local(mixed, lo_hbm)
    for copy in gather.sent:
        copy.wait_send()

    rs = Scatter(at, send2, recv2, 14)
    out_copies = {}

    def finisher(k, hbm, w):
        def finish(total):
            if k - 2 in out_copies:
                out_copies.pop(k - 2).wait()
            stage = out.at[k % 2, :, pl.ds(0, w)]
            stage[...] = total
            out_copies[k] = start_local(stage, hbm)

        return finish

    def finish_vectors(total):
        outv[...] = total
        out_copies[99] = start_local(outv, outv_hbm)

    def slots(k, w):
        s = k % 2
        return (
            rc.at[s, :, :, :, pl.ds(0, 2 * w)], ry.at[s, :, :, pl.ds(0, 2 * w)], rx.at[s, :, :, :, pl.ds(0, w)],
            ry2.at[s, :, :, pl.ds(0, w)], rx2.at[s, :, :, pl.ds(0, w)], rz.at[s, :, :, pl.ds(0, w)],
        )

    transpose_into(ddown_t, ddown)
    transpose_in_place(hlow)
    loaded = {}

    def load_act(step):
        loaded[step] = start_local(act_hbm.at[step], work.at[step % 2])

    order = [6, 7, 0, 1, 2, 3, 4, 5]
    stored.pop(6).wait()
    stored.pop(7).wait()

    def ffn_back(n, step):
        j, xx, slot = step // 2, step % 2, step % 2
        up, down = gu.at[j, :, :, :, :, pl.ds(xx * FW, FW)], gd.at[j, :, :, :, :, pl.ds(xx * FW, FW)]
        rbu, rbd = gu.at[j], gd.at[j]
        first = xx * 2048 + j * FW

        def rows_body(t):
            rows = tile_rows(t)
            d_act = mm(ddown[rows], down[...].reshape(1024, FW))
            d_pre = (d_act * work[slot, rows, FW:].astype(F32)).astype(BF)
            work[slot, rows, FW:] = d_pre
            bgrad[0:1, first : first + FW] += jnp.sum(d_pre.astype(F32), axis=0, keepdims=True)
            acc[rows] += mm_nt(d_pre, up[...].reshape(1024, FW))

        loop(rows_body)

        def grads_body(t):
            rows = tile_rows(t)
            for rb, left, right in ((rbu, hlow, slice(FW, 2 * FW)), (rbd, ddown_t, slice(0, FW))):
                part = mm(left[rows], work[slot, :, right]).astype(BF)
                rb[tile_blocks(t), :, :, :, pl.ds(xx * FW, FW)] = part.reshape(-1, 2, 2, 64, FW)

        loop(grads_body)
        if xx == 1:
            m = n // 2
            rs.add(2 * m, rbu, FW, slots(2 * m, FW), True, finisher(2 * m, outu_hbm.at[j], FW))
            rs.add(2 * m + 1, rbd, FW, slots(2 * m + 1, FW), True, finisher(2 * m + 1, outd_hbm.at[j], FW))

    for n, step in enumerate(order):
        if step in loaded:
            loaded[step].wait()
        ffn_back(n, step)
        if n + 2 < 8:
            load_act(order[n + 2])
        rs.run(BACKWARD_PLAN.get(f"f{n}", ()))

    lo_copy.wait()
    dattn, dattn_t, dctx, doa = ddown, ddown_t, mixed, qs

    def first_norm_back(t):
        rows = tile_rows(t)
        dh = acc[rows]
        normed = n1[rows].astype(F32)
        w = dh * bias[4:5]
        first_mean = jnp.mean(w, axis=-1, keepdims=True)
        second_mean = jnp.mean(w * normed, axis=-1, keepdims=True)
        d = inv1[rows, 0:1] * (w - first_mean - normed * second_mean)
        low = d.astype(BF)
        acc[rows] = d
        dattn[rows] = low
        dctx[rows] = mm(low, go[...].reshape(1024, 1024)).astype(BF)
        vgrad[4:5] += jnp.sum(dh * normed, axis=0, keepdims=True)
        vgrad[5:6] += jnp.sum(dh, axis=0, keepdims=True)
        vgrad[2:3] += jnp.sum(low.astype(F32), axis=0, keepdims=True)

    loop(first_norm_back)
    pair_in = {}

    def load_pair(step):
        i, xx = step // 2, step % 2
        pair_in[step] = [start_local(pair_hbm.at[xx * 4 + i], kv.at[xx]), start_local(qa_hbm.at[xx * 4 + i], qa.at[xx])]

    load_pair(0)
    load_pair(1)
    transpose_into(dattn_t, dattn)

    def output_grads(t):
        part = mm(dattn_t[tile_rows(t)], ctx[...]).astype(BF)
        go[tile_blocks(t)] = part.reshape(-1, 2, 2, 64, 1024)

    loop(output_grads)
    rs.add(8, go, FW, slots(8, FW), True, finisher(8, outo_hbm, FW))
    rs.run(BACKWARD_PLAN.get("m", ()))

    def attend_back(i, xx, dj):
        pair = xx * 4 + i
        cols = slice(pair * 128, pair * 128 + 128)
        base = xx * QW

        for t in range(TILES):
            rows = tile_rows(t)
            do_t = dctx[rows, cols]
            prod = do_t.astype(F32) * ctx[rows, cols].astype(F32)
            for h in range(2):
                inner = -jnp.sum(jnp.where(halves[h], prod, 0.0), axis=-1, keepdims=True)
                doa[h, rows] = jnp.where(
                    halves[h], do_t.astype(F32), three_terms(inner, lane, 64 * (1 - h))
                ).astype(BF)
            kt[:, rows] = jnp.where(low_half, kv[xx, 0, rows], kv[xx, 1, rows]).T

        dqt[...] = jnp.zeros_like(dqt)

        def keys_body(t):
            rows = tile_rows(t)
            grads_k, grads_v = [], []
            for h in range(2):
                probs = jnp.exp(mm_nt(kv[xx, h, rows], qa[xx, h]))
                d_scores = (probs * mm_nt(kv[xx, 2 + h, rows], doa[h])).astype(BF)
                grads_v.append(mm(probs.astype(BF), dctx[:, cols]))
                grads_k.append(mm(d_scores, qa[xx, h]))
                dqt[h * 64 : h * 64 + 64] += mm(kt[h * 64 : h * 64 + 64, rows], d_scores)
            dj[rows, base + 128 : base + 256] = jnp.where(low_half, grads_k[0], grads_k[1]).astype(BF)
            dj[rows, base + 256 : base + 384] = jnp.where(low_half, grads_v[0], grads_v[1]).astype(BF)

        loop(keys_body)
        for t in range(LEN // SIDE):
            rows = slice(t * SIDE, t * SIDE + SIDE)
            dj[rows, base : base + 128] = (dqt[:, rows].T * 0.125).astype(BF)
        sums = jnp.sum(dj[:, base : base + QW].astype(F32), axis=0, keepdims=True)
        vgrad[0:1, cols] = sums[:, 0:128]
        vgrad[1:2, cols] = sums[:, 256:384]

    def joined_grads(dj, rbq):
        def body(t):
            part = mm(tok[tile_rows(t)], dj[...]).astype(BF)
            rbq[tile_blocks(t)] = part.reshape(-1, 2, 2, 64, 2 * QW)

        loop(body)

    def back(i, dj):
        def body(t):
            rows = tile_rows(t)
            acc[rows] += mm_nt(dj[rows], gq[i].reshape(1024, 2 * QW))

        loop(body)

    for i in range(4):
        dj = work.at[i % 2, :, pl.ds(0, 2 * QW)]
        for xx in range(2):
            step = 2 * i + xx
            for copy in pair_in[step]:
                copy.wait()
            attend_back(i, xx, dj)
            if step + 2 < 8:
                load_pair(step + 2)
            rs.run(BACKWARD_PLAN.get(f"a{step}", ()))
        rbq = gq.at[i]
        if i < 3:
            back(i, dj)
        else:
            rbq = exq
        joined_grads(dj, rbq)
        rs.add(9 + i, rbq, QW, slots(9 + i, QW), True, finisher(9 + i, outq_hbm.at[i], QW))

    def vectors_body(dev):
        to = rbv.at[dev // 8, lax.rem(dev // 4, 2), lax.rem(dev // 2, 2)]
        lanes = pl.ds(pl.multiple_of(lax.rem(dev, 2) * 128, 128), 128)
        to[0:8, lanes] = vgrad[:, pl.ds(pl.multiple_of(dev // 4 * 128, 128), 128)]
        to[8:16, lanes] = bgrad[:, pl.ds(pl.multiple_of(dev * 128, 128), 128)]

    rs.run([12])
    loop(vectors_body, 8 * nz)
    rs.add(13, rbv, 128, (rcv, ryv, rxv, ry2v, rx2v, rzv), False, finish_vectors)
    rs.run([13])
    back(3, work.at[1, :, pl.ds(0, 2 * QW)])
    rs.run([14])

    def last(t):
        rows = tile_rows(t)
        mixed[rows] = acc[rows].astype(BF)

    loop(last)
    ig_copy = start_local(mixed, ig_hbm)
    rs.run([15, 16, 17])
    assert len(rs.done) == 14 * 5
    ig_copy.wait()
    for copy in rs.sent:
        copy.wait_send()
    for copy in out_copies.values():
        copy.wait()


def layer_call(nz, tok, og, wq, wk, wv, wo, wu, wd, sv):
    S, V = jax.ShapeDtypeStruct, pltpu.VMEM
    outs = [
        S((LEN, 1024), BF), S((LEN, 1024), BF), S((4, 64, FW), F32), S((4, 64, FW), F32), S((64, FW), F32),
        S((4, 64, QW), F32), S((16, 128), F32),
        S((8, 4, LEN, 128), BF), S((8, 2, LEN, 128), BF), S((8, LEN, 1024), BF),
    ]

    def gots(n, rows, w, kind):
        r = 32 if rows == 64 else rows
        lead = (n,) if n else ()
        return [
            V((*lead, nz, 2, rows, 2 * w), kind), V((*lead, nz, r, 2 * w), kind), V((*lead, nz, 2, r, w), kind),
            V((*lead, nz, r, w), kind), V((*lead, nz, r, w), kind), V((*lead, nz - 1, rows, w), kind),
        ]

    block = lambda *s: V((*s[:-1], nz, 2, 2, 64, s[-1]), BF)
    scratch = [
        V((nz, 2, 2, 16, 256), BF), block(4, 2 * QW), block(2 * FW), block(4, 2 * FW), block(4, 2 * FW),
        block(2 * QW), V((16, 1024), F32), V((8, 4096), F32),
        V((LEN, 1024), BF), V((LEN, 1024), BF), V((LEN, 1024), F32), V((LEN, 1024), BF), V((LEN, 128), F32),
        V((LEN, 1024), BF), V((LEN, 1024), BF), V((LEN, 1024), BF), V((LEN, 1024), BF), V((2, LEN, 1024), BF),
        V((2, LEN, 128), BF), V((2, 4, LEN, 128), BF), V((2, 2, LEN, 128), BF),
        V((128, LEN), BF), V((128, LEN), F32), V((8, 1024), F32),
        *gots(2, 64, FW, BF), V((nz, 2, 2, 16, 256), F32), *gots(0, 16, 128, F32),
        V((2, 64, FW), F32), V((16, 128), F32),
        *[pltpu.SemaphoreType.DMA((14, 8))] * 4, pltpu.SemaphoreType.DMA((96,)),
    ]
    hbm, vmem = pl.BlockSpec(memory_space=pl.ANY), pl.BlockSpec(memory_space=pltpu.VMEM)
    return pl.pallas_call(
        functools.partial(layer_kernel, nz),
        out_shape=outs,
        in_specs=[hbm] * 8 + [vmem],
        out_specs=[hbm] * len(outs),
        scratch_shapes=scratch,
        compiler_params=pltpu.CompilerParams(
            collective_id=0, has_side_effects=True, vmem_limit_bytes=63 * 1024 * 1024 + 512 * 1024
        ),
        cost_estimate=pl.CostEstimate(flops=90 * 10**9, bytes_accessed=10**8, transcendentals=4 * 10**7),
        name="layer",
    )(tok, og, wq, wk, wv, wo, wu, wd, sv)


def pack_vectors(vectors):
    dev = lax.axis_index("dp") * 2 + lax.axis_index("tensor")
    rows = jnp.stack(vectors[:8])
    quarter = lax.broadcasted_iota(jnp.int32, (8, 128), 1) // 32
    rows = jnp.where(quarter == dev % 4, jnp.tile(rows, (1, 4)), jnp.zeros((), BF))
    return jnp.concatenate([rows, jnp.broadcast_to(vectors[8][None], (8, 128))], axis=0)


def whole_sequences(tokens, wq, wk, wv, wo, wu, wd, bq, bv, bu, bo, bd, g1, s1, g2, s2, out_grad):
    sv = pack_vectors((bq, bv, bo, bd, g1, s1, g2, s2, bu))
    nz = lax.axis_size("dp") // 4
    lo, ig, gu, gd, go, gq, gv, *_ = layer_call(nz, tokens, out_grad, wq, wk, wv, wo.T, wu, wd.T, sv)
    parts = gq.reshape(4, 64, 3, 128).transpose(2, 1, 0, 3).reshape(3, 64, 512)
    up = gu.transpose(1, 0, 2).reshape(64, 2048)
    down = gd.transpose(0, 2, 1).reshape(2048, 64)
    dev = lax.axis_index("dp") * 2 + lax.axis_index("tensor")
    mine = lax.dynamic_slice_in_dim(gv[:8], (dev % 4) * 32, 32, axis=1)
    return (
        lo, ig, parts[0], parts[1], parts[2], go.T, up, down,
        mine[0], mine[1], gv[8], mine[2], mine[3], mine[4], mine[5], mine[6], mine[7],
    )


def layer_stats(resid):
    center = resid - jnp.mean(resid, axis=-1, keepdims=True)
    inverse = lax.rsqrt(jnp.mean(center * center, axis=-1, keepdims=True) + EPS)
    return (center * inverse, inverse)


def norm_back(grad_in, normed, inverse, gain):
    scaled = grad_in * gain
    first_mean = jnp.mean(scaled, axis=-1, keepdims=True)
    second_mean = jnp.mean(scaled * normed, axis=-1, keepdims=True)
    return inverse * (scaled - first_mean - normed * second_mean)


def gelu_slope(values):
    return (
        0.5 * (1.0 + lax.erf(values * SQRT_HALF))
        + values * jnp.exp(-0.5 * values * values) * INV_ROOT_TAU
    )


def split_heads(matrix):
    return matrix.reshape(matrix.shape[0], matrix.shape[1] // HEAD_DIM, HEAD_DIM)


def widen(part_sum, full_length, offset):
    return lax.dynamic_update_slice_in_dim(
        jnp.zeros((full_length,), jnp.float32), part_sum, offset, 0
    )


def attend_forward(block):
    query_b, key_b, value_b = block
    query_h = split_heads(query_b)
    key_h = split_heads(key_b)
    value_h = split_heads(value_b)
    scores = jnp.einsum("qhd,khd->hqk", query_h, key_h, preferred_element_type=jnp.float32)
    largest = jnp.max(scores, axis=-1, keepdims=True)
    expons = jnp.exp(scores - largest)
    totals = jnp.sum(expons, axis=-1, keepdims=True)
    attn_weights = (expons / totals).astype(jnp.bfloat16)
    context = jnp.einsum("hqk,khd->qhd", attn_weights, value_h, preferred_element_type=jnp.float32)
    return (
        context.reshape(query_b.shape).astype(jnp.bfloat16),
        (largest + jnp.log(totals))[:, :, 0],
    )


def attend_backward(block):
    query_b, key_b, value_b, logsum, grad_ctx = block
    query_h = split_heads(query_b)
    key_h = split_heads(key_b)
    value_h = split_heads(value_b)
    grad_h = split_heads(grad_ctx)
    scores = jnp.einsum("qhd,khd->hqk", query_h, key_h, preferred_element_type=jnp.float32)
    weights_full = jnp.exp(scores - logsum[:, :, None])
    weights_low = weights_full.astype(jnp.bfloat16)
    grad_value = jnp.einsum("hqk,qhd->khd", weights_low, grad_h, preferred_element_type=jnp.float32)
    grad_weights = jnp.einsum("qhd,khd->hqk", grad_h, value_h, preferred_element_type=jnp.float32)
    inner = jnp.sum(weights_full * grad_weights, axis=-1, keepdims=True)
    grad_scores = (weights_full * (grad_weights - inner)).astype(jnp.bfloat16)
    grad_query = jnp.einsum("hqk,khd->qhd", grad_scores, key_h, preferred_element_type=jnp.float32)
    grad_key = jnp.einsum("hqk,qhd->khd", grad_scores, query_h, preferred_element_type=jnp.float32)
    full_shape = query_b.shape
    return (
        grad_query.reshape(full_shape).astype(jnp.bfloat16),
        grad_key.reshape(full_shape).astype(jnp.bfloat16),
        grad_value.reshape(full_shape).astype(jnp.bfloat16),
    )


def on_device(
    tokens,
    weight_query,
    weight_key,
    weight_value,
    weight_output,
    weight_up,
    weight_down,
    bias_query,
    bias_value,
    bias_up,
    bias_output,
    bias_down,
    first_gain,
    first_shift,
    second_gain,
    second_shift,
    out_grad,
):
    w_query, w_key, w_value, w_output, w_up, w_down = (
        lax.all_gather(weight_query, "dp", axis=0, tiled=True),
        lax.all_gather(weight_key, "dp", axis=0, tiled=True),
        lax.all_gather(weight_value, "dp", axis=0, tiled=True),
        lax.all_gather(weight_output, "dp", axis=1, tiled=True),
        lax.all_gather(weight_up, "dp", axis=0, tiled=True),
        lax.all_gather(weight_down, "dp", axis=1, tiled=True),
    )
    vectors = (
        lax.all_gather(bias_query, ("dp", "tensor"), axis=0, tiled=True),
        lax.all_gather(bias_value, ("dp", "tensor"), axis=0, tiled=True),
        lax.all_gather(bias_up, ("dp", "tensor"), axis=0, tiled=True),
        lax.all_gather(bias_output, ("dp", "tensor"), axis=0, tiled=True),
        lax.all_gather(bias_down, ("dp", "tensor"), axis=0, tiled=True),
        lax.all_gather(first_gain, ("dp", "tensor"), axis=0, tiled=True),
        lax.all_gather(first_shift, ("dp", "tensor"), axis=0, tiled=True),
        lax.all_gather(second_gain, ("dp", "tensor"), axis=0, tiled=True),
        lax.all_gather(second_shift, ("dp", "tensor"), axis=0, tiled=True),
    )
    query_all, value_all, up_all, out_bias, down_bias, gain_one, shift_one, gain_two, shift_two = [
        member.astype(jnp.float32) for member in vectors
    ]
    width_here = w_query.shape[1]
    hidden_here = w_up.shape[1]
    full_hidden = up_all.shape[0]
    model_width = tokens.shape[1]
    tensor_pos = lax.axis_index("tensor")
    query_bias = lax.dynamic_slice_in_dim(query_all, tensor_pos * width_here, width_here)
    value_bias = lax.dynamic_slice_in_dim(value_all, tensor_pos * width_here, width_here)
    scale = HEAD_DIM ** (-0.5)
    gathered = lax.all_gather(tokens, "tensor", axis=0, tiled=True)
    joined = jnp.concatenate([w_query, w_key, w_value], axis=1)
    projected = jnp.dot(gathered, joined, preferred_element_type=jnp.float32)
    query_b = ((projected[:, :width_here] + query_bias) * scale).astype(jnp.bfloat16)
    key_b = projected[:, width_here : 2 * width_here].astype(jnp.bfloat16)
    value_b = (projected[:, 2 * width_here :] + value_bias).astype(jnp.bfloat16)
    seq_count = gathered.shape[0] // LEN

    def by_sequence(matrix):
        return matrix.reshape(seq_count, LEN, matrix.shape[-1])

    context, logsum = lax.map(
        attend_forward, (by_sequence(query_b), by_sequence(key_b), by_sequence(value_b))
    )
    context = context.reshape(-1, width_here)
    attn_sum = lax.psum_scatter(
        jnp.dot(context, w_output, preferred_element_type=jnp.float32).astype(jnp.bfloat16),
        "tensor",
        scatter_dimension=0,
        tiled=True,
    ).astype(jnp.float32)
    resid_one = tokens.astype(jnp.float32) + (attn_sum + out_bias)
    normed_one, inverse_one = layer_stats(resid_one)
    hidden = normed_one * gain_one + shift_one
    hidden_low = hidden.astype(jnp.bfloat16)
    ffn_rows = lax.all_gather(hidden_low, "tensor", axis=0, tiled=True)
    up_use, down_use = (w_up, w_down)
    up_bias = lax.dynamic_slice_in_dim(up_all, tensor_pos * hidden_here, hidden_here)
    preact = jnp.dot(ffn_rows, up_use, preferred_element_type=jnp.float32) + up_bias
    active = jax.nn.gelu(preact, approximate=False).astype(jnp.bfloat16)
    down_sum = lax.psum_scatter(
        jnp.dot(active, down_use, preferred_element_type=jnp.float32).astype(jnp.bfloat16),
        "tensor",
        scatter_dimension=0,
        tiled=True,
    ).astype(jnp.float32)
    resid_two = hidden + (down_sum + down_bias)
    normed_two, inverse_two = layer_stats(resid_two)
    layer_out = (normed_two * gain_two + shift_two).astype(jnp.bfloat16)
    grad_top = out_grad.astype(jnp.float32)
    grad_gain_two = jnp.sum(grad_top * normed_two, axis=0)
    grad_shift_two = jnp.sum(grad_top, axis=0)
    d_resid_two = norm_back(grad_top, normed_two, inverse_two, gain_two)
    d_down = d_resid_two.astype(jnp.bfloat16)
    grad_down_bias = jnp.sum(d_down, axis=0, dtype=jnp.float32)
    d_rows = lax.all_gather(d_down, "tensor", axis=0, tiled=True)
    grad_down = jnp.einsum("nf,nd->fd", active, d_rows, preferred_element_type=jnp.float32)
    d_active = jnp.einsum("nd,fd->nf", d_rows, down_use, preferred_element_type=jnp.float32)
    d_pre = (d_active * gelu_slope(preact)).astype(jnp.bfloat16)
    grad_up_part = jnp.sum(d_pre, axis=0, dtype=jnp.float32)
    grad_up = jnp.einsum("nd,nf->df", ffn_rows, d_pre, preferred_element_type=jnp.float32)
    d_from_ffn = lax.psum_scatter(
        jnp.einsum("nf,df->nd", d_pre, up_use, preferred_element_type=jnp.float32).astype(
            jnp.bfloat16
        ),
        "tensor",
        scatter_dimension=0,
        tiled=True,
    ).astype(jnp.float32)
    grad_up_bias = widen(grad_up_part, full_hidden, tensor_pos * hidden_here)
    d_hidden = d_resid_two + d_from_ffn
    grad_gain_one = jnp.sum(d_hidden * normed_one, axis=0)
    grad_shift_one = jnp.sum(d_hidden, axis=0)
    d_resid_one = norm_back(d_hidden, normed_one, inverse_one, gain_one)
    d_attn = d_resid_one.astype(jnp.bfloat16)
    grad_out_bias = jnp.sum(d_attn, axis=0, dtype=jnp.float32)
    d_attn_rows = lax.all_gather(d_attn, "tensor", axis=0, tiled=True)
    grad_output = jnp.einsum("nc,nd->cd", context, d_attn_rows, preferred_element_type=jnp.float32)
    d_context = jnp.einsum(
        "nd,cd->nc", d_attn_rows, w_output, preferred_element_type=jnp.float32
    ).astype(jnp.bfloat16)
    d_query, d_key, d_value = lax.map(
        attend_backward,
        (
            by_sequence(query_b),
            by_sequence(key_b),
            by_sequence(value_b),
            logsum,
            by_sequence(d_context),
        ),
    )
    d_joined = jnp.concatenate(
        [
            (d_query * scale).reshape(-1, width_here),
            d_key.reshape(-1, width_here),
            d_value.reshape(-1, width_here),
        ],
        axis=1,
    )
    grad_joined = jnp.einsum("nd,nc->dc", gathered, d_joined, preferred_element_type=jnp.float32)
    grad_query_w = grad_joined[:, :width_here]
    grad_key_w = grad_joined[:, width_here : 2 * width_here]
    grad_value_w = grad_joined[:, 2 * width_here :]
    bias_sums = jnp.sum(d_joined, axis=0, dtype=jnp.float32)
    grad_query_bias = widen(bias_sums[:width_here], model_width, tensor_pos * width_here)
    grad_value_bias = widen(bias_sums[2 * width_here :], model_width, tensor_pos * width_here)
    d_from_attn = lax.psum_scatter(
        jnp.einsum("nc,dc->nd", d_joined, joined, preferred_element_type=jnp.float32).astype(
            jnp.bfloat16
        ),
        "tensor",
        scatter_dimension=0,
        tiled=True,
    ).astype(jnp.float32)
    input_grad = (d_resid_one + d_from_attn).astype(jnp.bfloat16)
    grad_query_w, grad_key_w, grad_value_w, grad_output, grad_up, grad_down = (
        lax.psum_scatter(
            grad_query_w.astype(jnp.bfloat16), "dp", scatter_dimension=0, tiled=True
        ).astype(jnp.float32),
        lax.psum_scatter(
            grad_key_w.astype(jnp.bfloat16), "dp", scatter_dimension=0, tiled=True
        ).astype(jnp.float32),
        lax.psum_scatter(
            grad_value_w.astype(jnp.bfloat16), "dp", scatter_dimension=0, tiled=True
        ).astype(jnp.float32),
        lax.psum_scatter(
            grad_output.astype(jnp.bfloat16), "dp", scatter_dimension=1, tiled=True
        ).astype(jnp.float32),
        lax.psum_scatter(
            grad_up.astype(jnp.bfloat16), "dp", scatter_dimension=0, tiled=True
        ).astype(jnp.float32),
        lax.psum_scatter(
            grad_down.astype(jnp.bfloat16), "dp", scatter_dimension=1, tiled=True
        ).astype(jnp.float32),
    )
    vector_sums = (
        lax.psum_scatter(grad_query_bias, ("dp", "tensor"), scatter_dimension=0, tiled=True),
        lax.psum_scatter(grad_value_bias, ("dp", "tensor"), scatter_dimension=0, tiled=True),
        lax.psum_scatter(grad_up_bias, ("dp", "tensor"), scatter_dimension=0, tiled=True),
        lax.psum_scatter(grad_out_bias, ("dp", "tensor"), scatter_dimension=0, tiled=True),
        lax.psum_scatter(grad_down_bias, ("dp", "tensor"), scatter_dimension=0, tiled=True),
        lax.psum_scatter(grad_gain_one, ("dp", "tensor"), scatter_dimension=0, tiled=True),
        lax.psum_scatter(grad_shift_one, ("dp", "tensor"), scatter_dimension=0, tiled=True),
        lax.psum_scatter(grad_gain_two, ("dp", "tensor"), scatter_dimension=0, tiled=True),
        lax.psum_scatter(grad_shift_two, ("dp", "tensor"), scatter_dimension=0, tiled=True),
    )
    return (
        layer_out,
        input_grad,
        grad_query_w,
        grad_key_w,
        grad_value_w,
        grad_output,
        grad_up,
        grad_down,
    ) + tuple(vector_sums)


def either(*args):
    sizes = (lax.axis_size("dp"), lax.axis_size("tensor"))
    fits = args[0].shape == (LEN, 1024) and args[5].shape[1] * 2 == 4096 and sizes == (16, 2)
    return whole_sequences(*args) if fits else on_device(*args)


def solution(mesh):
    placed = (
        P(("dp", "tensor"), None),
        P("dp", "tensor"),
        P("dp", "tensor"),
        P("dp", "tensor"),
        P("tensor", "dp"),
        P("dp", "tensor"),
        P("tensor", "dp"),
        P(("dp", "tensor")),
        P(("dp", "tensor")),
        P(("dp", "tensor")),
        P(("dp", "tensor")),
        P(("dp", "tensor")),
        P(("dp", "tensor")),
        P(("dp", "tensor")),
        P(("dp", "tensor")),
        P(("dp", "tensor")),
        P(("dp", "tensor"), None),
    )
    return jax.shard_map(
        either,
        mesh=mesh,
        in_specs=placed,
        out_specs=(
            P(("dp", "tensor"), None),
            P(("dp", "tensor"), None),
            P("dp", "tensor"),
            P("dp", "tensor"),
            P("dp", "tensor"),
            P("tensor", "dp"),
            P("dp", "tensor"),
            P("tensor", "dp"),
            P(("dp", "tensor")),
            P(("dp", "tensor")),
            P(("dp", "tensor")),
            P(("dp", "tensor")),
            P(("dp", "tensor")),
            P(("dp", "tensor")),
            P(("dp", "tensor")),
            P(("dp", "tensor")),
            P(("dp", "tensor")),
        ),
        check_vma=False,
    )
```

```python
import functools
import jax
import jax.numpy as jnp
from jax import lax
from jax.experimental import pallas as pl
from jax.experimental.pallas import tpu as pltpu
from jax.sharding import PartitionSpec as P

HEAD_DIM = 64
LEN = 1024
EPS = 1e-05
SQRT_HALF = 0.7071067811865476
INV_ROOT_TAU = 0.3989422804014327
BF, F32 = jnp.bfloat16, jnp.float32
MESH = pl.DeviceIdType.MESH
NT = (((1,), (1,)), ((), ()))
TILE = 512
TILES = LEN // TILE
SIDE = 256
QW = 384
FW = 512

FORWARD_PLAN = {"a0": 3, "a2": 4, "a4": 5, "a6": 6, "n": 7}
GATHER_MID = (7, 9, 11, 13)
SCATTER_MID = ()
BACKWARD_PLAN = {
    "f1": [0], "f2": [1], "f4": [2], "f6": [3], "n": [4], "a0": [5],
    "j0": [6], "a2": [7], "j1": [8], "a4": [9], "j2": [10], "a6": [11],
}


def tile_rows(t):
    return pl.ds(t * TILE if isinstance(t, int) else pl.multiple_of(t * TILE, TILE), TILE)


def tile_blocks(t):
    return pl.ds(t * (TILE // 256), TILE // 256)


def mm(a, b):
    return jnp.dot(a, b, preferred_element_type=F32)


def mm_nt(a, b):
    return lax.dot_general(a, b, NT, preferred_element_type=F32)


def gelu_both(z):
    far = 1.0 / (1.0 + (0.3275911 * SQRT_HALF) * jnp.abs(z))
    bell = jnp.exp(-0.5 * z * z)
    poly = far * (
        0.127414796
        + far * (-0.142248368 + far * (0.7107068705 + far * (-0.7265760135 + far * 0.5307027145)))
    )
    tail = poly * bell
    cdf = jnp.where(z >= 0, 1.0 - tail, tail)
    return z * cdf, cdf + z * bell * INV_ROOT_TAU


def ln_stats(resid):
    center = resid - jnp.mean(resid, axis=-1, keepdims=True)
    inverse = lax.rsqrt(jnp.mean(center * center, axis=-1, keepdims=True) + EPS)
    return center * inverse, inverse


def three_terms(value, lane, at):
    hi = value.astype(BF).astype(F32)
    mid = (value - hi).astype(BF).astype(F32)
    rest = value - hi - mid
    return jnp.where(lane == at, hi, jnp.where(lane == at + 1, mid, jnp.where(lane == at + 2, rest, 0.0)))


def device(z, y, c, x):
    return {"dp": (z * 2 + y) * 2 + c, "tensor": x}


class Place:
    def __init__(self, nz):
        dp, x = lax.axis_index("dp"), lax.axis_index("tensor")
        z, y, c = dp // 4, lax.rem(dp // 2, 2), lax.rem(dp, 2)
        self.nz, self.z, self.y, self.c, self.x = nz, z, y, c, x
        self.not_y, self.not_c, self.not_x = 1 - y, 1 - c, 1 - x
        self.z_at = [z] + [lax.rem(z + s, nz) for s in range(1, nz)]
        self.to_z = [None] + [device(at, y, c, x) for at in self.z_at[1:]]
        self.to_y, self.to_c, self.to_x = device(z, 1 - y, c, x), device(z, y, 1 - c, x), device(z, y, c, 1 - x)

    def lanes(self, w):
        return pl.ds(pl.multiple_of(self.x * w, 128), w)

    def other_lanes(self, w):
        return pl.ds(pl.multiple_of(self.not_x * w, 128), w)

    def greet(self):
        bar = pltpu.get_barrier_semaphore()
        others = self.to_z[1:] + [self.to_y, self.to_c, self.to_x]
        for other in others:
            pl.semaphore_signal(bar, inc=1, device_id=other, device_id_type=MESH)
        pl.semaphore_wait(bar, len(others))


class Mover:
    def __init__(self, at, send, recv):
        self.at, self.send, self.recv, self.sent = at, send, recv, {}

    def go(self, k, slot, src, dst, to):
        copy = pltpu.make_async_remote_copy(
            src_ref=src,
            dst_ref=dst,
            send_sem=self.send.at[k, slot],
            recv_sem=self.recv.at[k, slot],
            device_id=to,
            device_id_type=MESH,
        )
        copy.start()
        self.sent.setdefault(k, []).append(copy)
        return copy


class Gather(Mover):
    def __init__(self, at, send, recv, chunks, mid):
        super().__init__(at, send, recv)
        self.chunks, self.mid, self.flying, self.next = chunks, mid, {}, 0

    def wait(self, k, stage):
        for copy in self.flying.pop((k, stage)):
            copy.wait_recv()

    def begin(self, k):
        at, (buf, w, split) = self.at, self.chunks[k]
        if k in self.mid:
            up, down = (buf.at[at.z, at.y, at.c, pl.ds(r, 32), at.lanes(w)] for r in (0, 32))
            self.flying[(k, 0)] = [self.go(k, 3, up, up, at.to_x), self.go(k, 4, down, down, at.to_y)]
            return
        own = buf.at[at.z, at.y, at.c, :, at.lanes(w)]
        self.flying[(k, 0)] = [self.go(k, s - 1, own, own, at.to_z[s]) for s in range(1, at.nz)]

    def first(self, k):
        self.wait(k, 0)
        at, (buf, w, split) = self.at, self.chunks[k]
        r = 32 if split else buf.shape[3]
        if k in self.mid:
            up = buf.at[at.z, at.y, at.c, pl.ds(0, r)]
            down = buf.at[at.z, :, at.c, pl.ds(r, r), at.lanes(w)]
            copies = [self.go(k, s - 1, up, up, at.to_z[s]) for s in range(1, at.nz)]
            copies += [self.go(k, 7 + s, down, down, at.to_z[s]) for s in range(1, at.nz)]
        else:
            up = buf.at[:, at.y, at.c, pl.ds(0, r), at.lanes(w)]
            copies = [self.go(k, 3, up, up, at.to_x)]
            if split:
                down = buf.at[:, at.y, at.c, pl.ds(r, r), at.lanes(w)]
                copies.append(self.go(k, 4, down, down, at.to_y))
        self.flying[(k, 1)] = copies

    def second(self, k):
        self.wait(k, 1)
        at, (buf, w, split) = self.at, self.chunks[k]
        r = 32 if split else buf.shape[3]
        up = buf.at[:, at.y, at.c, pl.ds(0, r)]
        copies = [self.go(k, 5, up, up, at.to_y)]
        if split:
            down = buf.at[:, :, at.c, pl.ds(r, r), at.lanes(w)]
            copies.append(self.go(k, 6, down, down, at.to_x))
        self.flying[(k, 2)] = copies

    def core(self, k):
        self.wait(k, 2)
        at, (buf, w, split) = self.at, self.chunks[k]
        part = buf.at[:, :, at.c]
        self.flying[(k, 3)] = [self.go(k, 7, part, part, at.to_c)]

    def push(self, upto):
        last = len(self.chunks) - 1
        while self.next <= min(upto, last + 1):
            k = self.next
            if k > 0:
                self.core(k - 1)
            for m, stage, kinds in ((k + 6, self.begin, 1), (k + 5, self.begin, 0), (k + 4, self.first, 1), (k + 2, self.first, 0)):
                if m <= last and (m in self.mid) == bool(kinds):
                    stage(m)
            if k + 1 <= last:
                self.second(k + 1)
            self.next += 1

    def ready(self, k):
        self.push(k + 1)
        self.wait(k, 3)


class Scatter(Mover):
    def __init__(self, at, send, recv, count, mid, got_mid):
        super().__init__(at, send, recv)
        self.chunks, self.flying, self.done, self.count = {}, {}, set(), count
        self.mid, self.got_mid = mid, got_mid

    def add(self, k, buf, w, got, split, finish):
        self.chunks[k] = (buf, w, got, split, finish)

    def stage(self, k, s):
        at, nz = self.at, self.at.nz
        z, y, c = at.z, at.y, at.c
        buf, w, (got_c, got_y, got_x, got_y2, got_x2, got_z), split, finish = self.chunks[k]
        r = 32 if split else buf.shape[3]
        up, down = pl.ds(0, r), pl.ds(r, r)
        mine, other = at.lanes(w), at.other_lanes(w)
        assert (k, s) not in self.done and (s == 0 or (k, s - 1) in self.done)
        assert s == 4 or k == 0 or (k - 1, s + 1) in self.done
        self.done.add((k, s))
        for copy in self.flying.pop((k, s - 1), []):
            copy.wait_recv()
        copies = []
        if s == 0:
            copies = [self.go(k, 0, buf.at[:, :, at.not_c], got_c, at.to_c)]
        elif s == 1:

            def fold(m, carry):
                zz, yy = m // 2, lax.rem(m, 2)
                buf[zz, yy, c] += got_c[zz, yy]
                return carry

            lax.fori_loop(0, 2 * nz, fold, 0)
            copies = [self.go(k, 1, buf.at[:, at.not_y, c, up], got_y, at.to_y)]
            if split:
                copies.append(self.go(k, 2, buf.at[:, :, c, down, other], got_x, at.to_x))
        elif s == 2:

            def fold(zz, carry):
                buf[zz, y, c, up] += got_y[zz]
                if split:
                    for yy in range(2):
                        buf[zz, yy, c, down, mine] += got_x[zz, yy]
                return carry

            lax.fori_loop(0, nz, fold, 0)
            if k in self.mid:
                got_u, got_d, _, _ = self.got_mid(k)
                copies = []
                for d in range(1, nz):
                    copies.append(self.go(k, 4 + d, buf.at[at.z_at[d], y, c, up], got_u.at[d - 1], at.to_z[d]))
                    copies.append(
                        self.go(k, 7 + d, buf.at[at.z_at[d], :, c, down, mine], got_d.at[d - 1], at.to_z[d])
                    )
                self.flying[(k, s)] = copies
                return
            copies = [self.go(k, 3, buf.at[:, y, c, up, other], got_x2, at.to_x)]
            if split:
                copies.append(self.go(k, 4, buf.at[:, at.not_y, c, down, mine], got_y2, at.to_y))
        elif s == 3 and k in self.mid:
            got_u, got_d, got_x3, got_y3 = self.got_mid(k)
            for d in range(nz - 1):
                buf[z, y, c, up] += got_u[d]
                buf[z, :, c, down, mine] += got_d[d]
            copies = [
                self.go(k, 3, buf.at[z, y, c, up, other], got_x3, at.to_x),
                self.go(k, 4, buf.at[z, at.not_y, c, down, mine], got_y3, at.to_y),
            ]
        elif k in self.mid:
            _, _, got_x3, got_y3 = self.got_mid(k)
            halves = [
                buf[z, y, c, rows, mine].astype(F32) + got[...].astype(F32) for rows, got in ((up, got_x3), (down, got_y3))
            ]
            finish(jnp.concatenate(halves, axis=0))
        elif s == 3:

            def fold(zz, carry):
                buf[zz, y, c, up, mine] += got_x2[zz]
                if split:
                    buf[zz, y, c, down, mine] += got_y2[zz]
                return carry

            lax.fori_loop(0, nz, fold, 0)
            copies = [
                self.go(k, 4 + d, buf.at[at.z_at[d], y, c, :, mine], got_z.at[d - 1], at.to_z[d])
                for d in range(1, nz)
            ]
        else:
            total = buf[z, y, c, :, mine].astype(F32)
            for d in range(1, nz):
                total = total + got_z[d - 1].astype(F32)
            finish(total)
        self.flying[(k, s)] = copies

    def settle(self, k):
        assert (k, 4) in self.done
        for copy in self.sent.pop(k):
            copy.wait_send()

    def run(self, plan):
        for item in plan:
            if isinstance(item, tuple):
                self.stage(*item)
                continue
            for s in (4, 3, 2, 1, 0):
                k = item - s
                if 0 <= k < self.count and (k, s) not in self.done:
                    self.stage(k, s)


def transpose_in_place(ref):
    for a in range(LEN // SIDE):
        for b in range(a, LEN // SIDE):
            ra, rb = slice(a * SIDE, a * SIDE + SIDE), slice(b * SIDE, b * SIDE + SIDE)
            first = ref[ra, rb].T
            if a != b:
                ref[ra, rb] = ref[rb, ra].T
            ref[rb, ra] = first


def transpose_into(dst, src):
    for t in range(LEN // SIDE):
        dst[:, t * SIDE : t * SIDE + SIDE] = src[t * SIDE : t * SIDE + SIDE].T


def layer_kernel(
    nz,
    tok_hbm, og_hbm, wq_hbm, wk_hbm, wv_hbm, wo_hbm, wu_hbm, wd_hbm, sv, su,
    lo_hbm, ig_hbm, outu_hbm, outd_hbm, outo_hbm, outq_hbm, outv_hbm, pair_hbm, qa_hbm, act_hbm,
    gv, gq, go, gu, gd, bias, bup, tok, ctx, acc, n1, inv1, hlow, ddown, spare, mixed, work,
    qs, kv, qa, kt, dqt, vgrad,
    rc, ry, rx, ry2, rx2, rz, rzu, rzd, rx3, ry3, rbv, rcv, ryv, rxv, ry2v, rx2v, rzv, out, outv,
    send, recv, send2, recv2, lsem,
):
    at = Place(nz)
    used = [0]

    def start_local(src, dst):
        copy = pltpu.make_async_copy(src, dst, lsem.at[used[0]])
        used[0] += 1
        copy.start()
        return copy

    def loop(body, n=TILES):
        def step(t, carry):
            body(t)
            return carry

        lax.fori_loop(0, n, step, 0)

    own = (at.z, at.y, at.c)
    chunks = [(gv, 128, False)]
    chunks += [(gq.at[i], QW, True) for i in range(4)] + [(go, FW, True)]
    for j in range(4):
        chunks += [(gu.at[j], FW, True), (gd.at[j], FW, True)]
    placed = [[] for _ in chunks]
    for i in range(4):
        for m, w_hbm in enumerate((wq_hbm, wk_hbm, wv_hbm)):
            lanes = pl.ds(pl.multiple_of(at.x * QW + m * 128, 128), 128)
            placed[1 + i].append(start_local(w_hbm.at[:, pl.ds(i * 128, 128)], gq.at[(i, *own, slice(None), lanes)]))
    tok_in = start_local(tok_hbm, tok)
    placed[5].append(start_local(wo_hbm, go.at[(*own, slice(None), at.lanes(FW))]))
    for j in range(4):
        for m, (w_hbm, g) in enumerate(((wu_hbm, gu), (wd_hbm, gd))):
            placed[6 + 2 * j + m].append(
                start_local(w_hbm.at[:, pl.ds(j * FW, FW)], g.at[(j, *own, slice(None), at.lanes(FW))])
            )
    og_in = start_local(og_hbm, mixed)
    quarter = lax.broadcasted_iota(jnp.int32, (8, 128), 1) // 32
    mine = quarter == lax.rem(at.c, 2) * 2 + at.x
    pieces = jnp.where(mine, jnp.concatenate([sv[...].astype(F32)] * 4, axis=1), 0.0).astype(BF)
    gv[at.z, at.y, at.c, 0:8, at.lanes(128)] = pieces
    gv[at.z, at.y, at.c, 8:16, at.lanes(128)] = jnp.broadcast_to(su[...], (8, 128))
    at.greet()
    gather = Gather(at, send, recv, chunks, GATHER_MID)
    for k in range(len(chunks)):
        for copy in placed[k]:
            copy.wait()
        if k < 5:
            gather.begin(k)
    gather.first(0)
    gather.first(1)
    gather.second(0)
    gather.ready(0)
    for t in range(8):
        sums = None
        for owner in range(4 * t, 4 * t + 4):
            dp_o, x_o = owner // 2, owner % 2
            block = gv[dp_o // 4, dp_o // 2 % 2, dp_o % 2, :, x_o * 128 : x_o * 128 + 128].astype(F32)
            sums = block if sums is None else sums + block
            bup[:, owner * 128 : owner * 128 + 128] = jnp.broadcast_to(block[8:9], (8, 128))
        bias[:, t * 128 : t * 128 + 128] = sums
    tok_in.wait()

    lane = lax.broadcasted_iota(jnp.int32, (TILE, 128), 1)
    low_half = lane < 64
    halves = (low_half, jnp.logical_not(low_half))

    def project(i):
        def body(t):
            rows = tile_rows(t)
            part = mm(tok[rows], gq[i].reshape(1024, 2 * QW))
            for xx in range(2):
                pair, base = xx * 4 + i, xx * QW
                bq = bias[0:1, pair * 128 : pair * 128 + 128]
                bv = bias[1:2, pair * 128 : pair * 128 + 128]
                qs[xx, rows] = ((part[:, base : base + 128] + bq) * 0.125).astype(BF)
                key = part[:, base + 128 : base + 256].astype(BF)
                value = (part[:, base + 256 : base + 384] + bv).astype(BF)
                one = jnp.ones_like(key)
                for h in range(2):
                    kv[xx, h, rows] = jnp.where(halves[h], key, one)
                    kv[xx, 2 + h, rows] = jnp.where(halves[h], value, one)

        loop(body)

    def attend(i, xx):
        pair = xx * 4 + i

        def body(t):
            rows = tile_rows(t)
            q = qs[xx, rows]
            scores = [mm_nt(jnp.where(halves[h], q, jnp.zeros_like(q)), kv[xx, h]) for h in range(2)]
            tops = [jnp.max(s, axis=-1, keepdims=True) for s in scores]
            expons = [jnp.exp(s - top).astype(BF) for s, top in zip(scores, tops)]
            outs = [mm(expons[h], kv[xx, 2 + h]) for h in range(2)]
            for h in range(2):
                extra = three_terms(-(tops[h] + jnp.log(outs[h])), lane, 64 * (1 - h))
                qa[xx, h, rows] = jnp.where(halves[h], q.astype(F32), extra).astype(BF)
            total = pltpu.roll(jnp.where(low_half, outs[1], outs[0]), 64, 1)
            ctx[rows, pair * 128 : pair * 128 + 128] = (jnp.where(low_half, outs[0], outs[1]) / total).astype(BF)

        loop(body)

    spilled = []
    for i in range(4):
        gather.ready(1 + i)
        for copy in spilled:
            copy.wait()
        spilled = []
        project(i)
        for xx in range(2):
            attend(i, xx)
            spilled += [start_local(kv.at[xx], pair_hbm.at[xx * 4 + i]), start_local(qa.at[xx], qa_hbm.at[xx * 4 + i])]
            gather.push(FORWARD_PLAN.get(f"a{2 * i + xx}", 0))

    gather.ready(5)

    def first_norm(t):
        rows = tile_rows(t)
        attn = mm_nt(ctx[rows], go[...].reshape(1024, 1024))
        normed, inverse = ln_stats(tok[rows].astype(F32) + (attn + bias[2:3]))
        n1[rows] = normed.astype(BF)
        inv1[rows] = jnp.broadcast_to(inverse, (TILE, 128))
        h = normed * bias[4:5] + bias[5:6]
        acc[rows] = h
        hlow[rows] = h.astype(BF)

    loop(first_norm)
    for copy in spilled:
        copy.wait()
    gather.push(FORWARD_PLAN.get("n", 0))
    transpose_in_place(tok)
    hlow_t, ddown_t = spare, hlow
    transpose_into(hlow_t, hlow)

    def ffn_up(j, xx, slot):
        up = gu.at[j, :, :, :, :, pl.ds(xx * FW, FW)]
        first = xx * 2048 + j * FW
        b_up = bup[0:1, first : first + FW]

        def body(t):
            rows = tile_rows(t)
            value, grade = gelu_both(mm(hlow[rows], up[...].reshape(1024, FW)) + b_up)
            work[slot, rows, 0:FW] = value.astype(BF)
            work[slot, rows, FW:] = grade.astype(BF)

        loop(body)

    def ffn_down(j):
        down = gd.at[j]

        def body(t):
            rows = tile_rows(t)
            acc[rows] += sum(
                mm_nt(work[xx, rows, 0:FW], down[:, :, :, :, xx * FW : xx * FW + FW].reshape(1024, FW))
                for xx in range(2)
            )

        loop(body)

    stored = {}
    for j in range(4):
        gather.ready(6 + 2 * j)
        for xx in range(2):
            step = 2 * j + xx
            if step >= 2:
                stored.pop(step - 2).wait()
            ffn_up(j, xx, xx)
            stored[step] = start_local(work.at[xx], act_hbm.at[step])
            gather.push(FORWARD_PLAN.get(f"f{step}", 0))
        gather.ready(7 + 2 * j)
        ffn_down(j)
    og_in.wait()
    vgrad[...] = jnp.zeros_like(vgrad)
    bgrad = bup
    bgrad[...] = jnp.zeros_like(bgrad)

    def second_norm(t):
        rows = tile_rows(t)
        normed, inverse = ln_stats(acc[rows] + bias[3:4])
        g = mixed[rows].astype(F32)
        mixed[rows] = (normed * bias[6:7] + bias[7:8]).astype(BF)
        u = g * bias[6:7]
        first_mean = jnp.mean(u, axis=-1, keepdims=True)
        second_mean = jnp.mean(u * normed, axis=-1, keepdims=True)
        d = inverse * (u - first_mean - normed * second_mean)
        acc[rows] = d
        low = d.astype(BF)
        ddown[rows] = low
        vgrad[6:7] += jnp.sum(g * normed, axis=0, keepdims=True)
        vgrad[7:8] += jnp.sum(g, axis=0, keepdims=True)
        vgrad[3:4] += jnp.sum(low.astype(F32), axis=0, keepdims=True)

    loop(second_norm)
    lo_copy = start_local(mixed, lo_hbm)
    for copies in gather.sent.values():
        for copy in copies:
            copy.wait_send()

    def mid_slots(k):
        m = SCATTER_MID.index(k) % 2
        return rzu.at[m], rzd.at[m], rx3.at[m], ry3.at[m]

    rs = Scatter(at, send2, recv2, 14, SCATTER_MID, mid_slots)
    out_copies = {}

    def finisher(k, hbm, w):
        def finish(total):
            if k - 2 in out_copies:
                out_copies.pop(k - 2).wait()
            stage = out.at[k % 2, :, pl.ds(0, w)]
            stage[...] = total
            out_copies[k] = start_local(stage, hbm)

        return finish

    def finish_vectors(total):
        outv[...] = total
        out_copies[99] = start_local(outv, outv_hbm)

    plain = [k for k in range(14) if k not in SCATTER_MID and k != 12]

    def slots(k, w):
        s, t = k % 2, plain.index(k) % 2 if k in plain else 0
        return (
            rc.at[s, :, :, :, pl.ds(0, 2 * w)], ry.at[s, :, :, pl.ds(0, 2 * w)], rx.at[s, :, :, :, pl.ds(0, w)],
            ry2.at[t, :, :, pl.ds(0, w)], rx2.at[t, :, :, pl.ds(0, w)], rz.at[t, :, :, pl.ds(0, w)],
        )

    transpose_into(ddown_t, ddown)
    loaded = {}

    def load_act(step):
        loaded[step] = start_local(act_hbm.at[step], work.at[step % 2])

    order = [6, 7, 0, 1, 2, 3, 4, 5]
    stored.pop(6).wait()
    stored.pop(7).wait()

    def ffn_back(n, step):
        j, xx, slot = step // 2, step % 2, step % 2
        up, down = gu.at[j, :, :, :, :, pl.ds(xx * FW, FW)], gd.at[j, :, :, :, :, pl.ds(xx * FW, FW)]
        rbu, rbd = gu.at[j], gd.at[j]
        first = xx * 2048 + j * FW

        def rows_body(t):
            rows = tile_rows(t)
            d_act = mm(ddown[rows], down[...].reshape(1024, FW))
            d_pre = (d_act * work[slot, rows, FW:].astype(F32)).astype(BF)
            work[slot, rows, FW:] = d_pre
            bgrad[0:1, first : first + FW] += jnp.sum(d_pre.astype(F32), axis=0, keepdims=True)
            acc[rows] += mm_nt(d_pre, up[...].reshape(1024, FW))

        loop(rows_body)

        def grads_body(t):
            rows = tile_rows(t)
            for rb, left, right in ((rbu, hlow_t, slice(FW, 2 * FW)), (rbd, ddown_t, slice(0, FW))):
                part = mm(left[rows], work[slot, :, right]).astype(BF)
                rb[tile_blocks(t), :, :, :, pl.ds(xx * FW, FW)] = part.reshape(-1, 2, 2, 64, FW)

        loop(grads_body)
        if xx == 1:
            m = n // 2
            rs.add(2 * m, rbu, FW, slots(2 * m, FW), True, finisher(2 * m, outu_hbm.at[j], FW))
            rs.add(2 * m + 1, rbd, FW, slots(2 * m + 1, FW), True, finisher(2 * m + 1, outd_hbm.at[j], FW))

    for n, step in enumerate(order):
        if step in loaded:
            loaded[step].wait()
        ffn_back(n, step)
        if n + 2 < 8:
            load_act(order[n + 2])
        rs.run(BACKWARD_PLAN.get(f"f{n}", ()))

    lo_copy.wait()
    dattn, dattn_t, dctx, doa = ddown, ddown_t, mixed, qs

    def first_norm_back(t):
        rows = tile_rows(t)
        dh = acc[rows]
        normed = n1[rows].astype(F32)
        w = dh * bias[4:5]
        first_mean = jnp.mean(w, axis=-1, keepdims=True)
        second_mean = jnp.mean(w * normed, axis=-1, keepdims=True)
        d = inv1[rows, 0:1] * (w - first_mean - normed * second_mean)
        low = d.astype(BF)
        acc[rows] = d
        dattn[rows] = low
        dctx[rows] = mm(low, go[...].reshape(1024, 1024)).astype(BF)
        vgrad[4:5] += jnp.sum(dh * normed, axis=0, keepdims=True)
        vgrad[5:6] += jnp.sum(dh, axis=0, keepdims=True)
        vgrad[2:3] += jnp.sum(low.astype(F32), axis=0, keepdims=True)

    loop(first_norm_back)
    rs.run(BACKWARD_PLAN.get("n", ()))
    pair_in = {}

    def load_pair(step):
        i, xx = step // 2, step % 2
        pair_in[step] = [start_local(pair_hbm.at[xx * 4 + i], kv.at[xx]), start_local(qa_hbm.at[xx * 4 + i], qa.at[xx])]

    load_pair(0)
    load_pair(1)
    transpose_into(dattn_t, dattn)

    def output_grads(t):
        part = mm(dattn_t[tile_rows(t)], ctx[...]).astype(BF)
        go[tile_blocks(t)] = part.reshape(-1, 2, 2, 64, 1024)

    loop(output_grads)
    rs.add(8, go, FW, slots(8, FW), True, finisher(8, outo_hbm, FW))
    rs.run(BACKWARD_PLAN.get("m", ()))

    def attend_back(i, xx, dj):
        pair = xx * 4 + i
        cols = slice(pair * 128, pair * 128 + 128)
        base = xx * QW

        for t in range(TILES):
            rows = tile_rows(t)
            do_t = dctx[rows, cols]
            prod = do_t.astype(F32) * ctx[rows, cols].astype(F32)
            for h in range(2):
                inner = -jnp.sum(jnp.where(halves[h], prod, 0.0), axis=-1, keepdims=True)
                doa[h, rows] = jnp.where(
                    halves[h], do_t.astype(F32), three_terms(inner, lane, 64 * (1 - h))
                ).astype(BF)
            kt[:, rows] = jnp.where(low_half, kv[xx, 0, rows], kv[xx, 1, rows]).T

        dqt[...] = jnp.zeros_like(dqt)

        def keys_body(t):
            rows = tile_rows(t)
            grads_k, grads_v = [], []
            for h in range(2):
                probs = jnp.exp(mm_nt(kv[xx, h, rows], qa[xx, h]))
                d_scores = (probs * mm_nt(kv[xx, 2 + h, rows], doa[h])).astype(BF)
                grads_v.append(mm(probs.astype(BF), dctx[:, cols]))
                grads_k.append(mm(d_scores, qa[xx, h]))
                dqt[h * 64 : h * 64 + 64] += mm(kt[h * 64 : h * 64 + 64, rows], d_scores)
            dj[rows, base + 128 : base + 256] = jnp.where(low_half, grads_k[0], grads_k[1]).astype(BF)
            dj[rows, base + 256 : base + 384] = jnp.where(low_half, grads_v[0], grads_v[1]).astype(BF)

        loop(keys_body)
        for t in range(LEN // SIDE):
            rows = slice(t * SIDE, t * SIDE + SIDE)
            dj[rows, base : base + 128] = (dqt[:, rows].T * 0.125).astype(BF)
        sums = jnp.sum(dj[:, base : base + QW].astype(F32), axis=0, keepdims=True)
        vgrad[0:1, cols] = sums[:, 0:128]
        vgrad[1:2, cols] = sums[:, 256:384]

    def joined_grads(dj, rbq):
        def body(t):
            part = mm(tok[tile_rows(t)], dj[...]).astype(BF)
            rbq[tile_blocks(t)] = part.reshape(-1, 2, 2, 64, 2 * QW)

        loop(body)

    def back(i, dj):
        def body(t):
            rows = tile_rows(t)
            acc[rows] += mm_nt(dj[rows], gq[i].reshape(1024, 2 * QW))

        loop(body)

    def vectors_body(dev):
        to = rbv.at[dev // 8, lax.rem(dev // 4, 2), lax.rem(dev // 2, 2)]
        lanes = pl.ds(pl.multiple_of(lax.rem(dev, 2) * 128, 128), 128)
        to[0:8, lanes] = vgrad[:, pl.ds(pl.multiple_of(dev // 4 * 128, 128), 128)]
        to[8:16, lanes] = bgrad[:, pl.ds(pl.multiple_of(dev * 128, 128), 128)]

    for i in range(4):
        dj = work.at[i % 2, :, pl.ds(0, 2 * QW)]
        for xx in range(2):
            step = 2 * i + xx
            for copy in pair_in[step]:
                copy.wait()
            attend_back(i, xx, dj)
            if step + 2 < 8:
                load_pair(step + 2)
            rs.run(BACKWARD_PLAN.get(f"a{step}", ()))
        if i < 2:
            rbq = gq.at[i]
            back(i, dj)
        else:
            rs.settle(3 - i)
            rbq = (gu if i == 3 else gd).at[order[0] // 2, :, :, :, :, pl.ds(0, 2 * QW)]
        k = 9 + i
        if i == 3:
            loop(vectors_body, 8 * nz)
            rs.add(12, rbv, 128, (rcv, ryv, rxv, ry2v, rx2v, rzv), False, finish_vectors)
            rs.run([12])
            k = 13
        joined_grads(dj, rbq)
        rs.add(k, rbq, QW, slots(k, QW), True, finisher(9 + i, outq_hbm.at[i], QW))
        rs.run(BACKWARD_PLAN.get(f"j{i}", ()))

    rs.run([13])
    back(2, work.at[0, :, pl.ds(0, 2 * QW)])
    rs.run([14])
    back(3, work.at[1, :, pl.ds(0, 2 * QW)])
    rs.run([15])

    def last(t):
        rows = tile_rows(t)
        mixed[rows] = acc[rows].astype(BF)

    loop(last)
    ig_copy = start_local(mixed, ig_hbm)
    rs.run([16, 17])
    assert len(rs.done) == 14 * 5
    ig_copy.wait()
    for copies in rs.sent.values():
        for copy in copies:
            copy.wait_send()
    for copy in out_copies.values():
        copy.wait()


def layer_call(nz, tok, og, wq, wk, wv, wo, wu, wd, sv, su):
    S, V = jax.ShapeDtypeStruct, pltpu.VMEM
    outs = [
        S((LEN, 1024), BF), S((LEN, 1024), BF), S((4, 64, FW), F32), S((4, 64, FW), F32), S((64, FW), F32),
        S((4, 64, QW), F32), S((16, 128), F32),
        S((8, 4, LEN, 128), BF), S((8, 2, LEN, 128), BF), S((8, LEN, 1024), BF),
    ]

    def gots(n, rows, w, kind):
        r = 32 if rows == 64 else rows
        lead = (n,) if n else ()
        return [
            V((*lead, nz, 2, rows, 2 * w), kind), V((*lead, nz, r, 2 * w), kind), V((*lead, nz, 2, r, w), kind),
            V((*lead, nz, r, w), kind), V((*lead, nz, r, w), kind), V((*lead, nz - 1, rows, w), kind),
        ]

    block = lambda *s: V((*s[:-1], nz, 2, 2, 64, s[-1]), BF)
    scratch = [
        V((nz, 2, 2, 16, 256), BF), block(4, 2 * QW), block(2 * FW), block(4, 2 * FW), block(4, 2 * FW),
        V((16, 1024), F32), V((8, 4096), F32),
        V((LEN, 1024), BF), V((LEN, 1024), BF), V((LEN, 1024), F32), V((LEN, 1024), BF), V((LEN, 128), F32),
        V((LEN, 1024), BF), V((LEN, 1024), BF), V((LEN, 1024), BF), V((LEN, 1024), BF), V((2, LEN, 1024), BF),
        V((2, LEN, 128), BF), V((2, 4, LEN, 128), BF), V((2, 2, LEN, 128), BF),
        V((128, LEN), BF), V((128, LEN), F32), V((8, 1024), F32),
        *gots(2, 64, FW, BF), V((2, nz - 1, 32, 2 * FW), BF), V((2, nz - 1, 2, 32, FW), BF), V((2, 32, FW), BF),
        V((2, 32, FW), BF), V((nz, 2, 2, 16, 256), F32), *gots(0, 16, 128, F32),
        V((2, 64, FW), F32), V((16, 128), F32),
        *[pltpu.SemaphoreType.DMA((14, 11))] * 4, pltpu.SemaphoreType.DMA((96,)),
    ]
    hbm, vmem = pl.BlockSpec(memory_space=pl.ANY), pl.BlockSpec(memory_space=pltpu.VMEM)
    return pl.pallas_call(
        functools.partial(layer_kernel, nz),
        out_shape=outs,
        in_specs=[hbm] * 8 + [vmem, vmem],
        out_specs=[hbm] * len(outs),
        scratch_shapes=scratch,
        compiler_params=pltpu.CompilerParams(
            collective_id=0, has_side_effects=True, vmem_limit_bytes=63 * 1024 * 1024 + 512 * 1024
        ),
        cost_estimate=pl.CostEstimate(flops=90 * 10**9, bytes_accessed=10**8, transcendentals=4 * 10**7),
        name="layer",
    )(tok, og, wq, wk, wv, wo, wu, wd, sv, su)


def finish_kernel(
    lo_in, ig_in, gu_in, gd_in, go_in, gq_in, gv_in, lo, ig, wq, wk, wv, wo, wu, wd, vec, gu, gd, go, gq, gv, sem
):
    pairs = [(gd_in, gd), (gu_in, gu), (gq_in, gq), (go_in, go), (gv_in, gv), (lo_in, lo), (ig_in, ig)]
    copies = [pltpu.make_async_copy(src, dst, sem.at[n]) for n, (src, dst) in enumerate(pairs)]
    for copy in copies:
        copy.start()
    copies[0].wait()
    for i in range(4):
        wd[:, i * FW : i * FW + FW] = gd[i]
    copies[1].wait()
    for i in range(4):
        wu[:, i * FW : i * FW + FW] = gu[i]
    copies[2].wait()
    for i in range(4):
        for m, ref in enumerate((wq, wk, wv)):
            ref[:, i * 128 : i * 128 + 128] = gq[i, :, m * 128 : m * 128 + 128]
    copies[3].wait()
    wo[...] = go[...]
    copies[4].wait()
    quarter = lax.rem(lax.axis_index("dp") * 2 + lax.axis_index("tensor"), 4)
    rows = gv[0:8]
    mine = rows[:, 0:32]
    for q in range(1, 4):
        mine = jnp.where(quarter == q, rows[:, q * 32 : q * 32 + 32], mine)
    vec[0:8] = jnp.concatenate([mine] * 4, axis=1)
    vec[8:16] = gv[8:16]
    copies[5].wait()
    copies[6].wait()


def finish_call(lo, ig, gu, gd, go, gq, gv):
    S, V = jax.ShapeDtypeStruct, pltpu.VMEM
    hbm, vmem = pl.BlockSpec(memory_space=pltpu.MemorySpace.HBM), pl.BlockSpec(memory_space=pltpu.VMEM)
    return pl.pallas_call(
        finish_kernel,
        out_shape=[
            S(lo.shape, BF), S(ig.shape, BF), *[S((64, 512), F32)] * 4, *[S((64, 2048), F32)] * 2,
            S((16, 128), F32),
        ],
        in_specs=[hbm] * 7,
        out_specs=[vmem] * 9,
        scratch_shapes=[*[V(m.shape, F32) for m in (gu, gd, go, gq, gv)], pltpu.SemaphoreType.DMA((7,))],
        compiler_params=pltpu.CompilerParams(vmem_limit_bytes=62 * 1024 * 1024),
        name="finish",
    )(lo, ig, gu, gd, go, gq, gv)


def whole_sequences(tokens, wq, wk, wv, wo, wu, wd, bq, bv, bu, bo, bd, g1, s1, g2, s2, out_grad):
    nz = lax.axis_size("dp") // 4
    sv = jnp.stack([bq, bv, bo, bd, g1, s1, g2, s2])
    lo, ig, gu, gd, go, gq, gv, *_ = layer_call(nz, tokens, out_grad, wq, wk, wv, wo.T, wu, wd.T, sv, bu[None])
    lo, ig, d_wq, d_wk, d_wv, d_wo, d_wu, d_wd, vec = finish_call(lo, ig, gu, gd, go, gq, gv)
    v = [vec[r, :32] for r in range(8)]
    return (lo, ig, d_wq, d_wk, d_wv, d_wo.T, d_wu, d_wd.T, v[0], v[1], vec[8], *v[2:])


def layer_stats(resid):
    center = resid - jnp.mean(resid, axis=-1, keepdims=True)
    inverse = lax.rsqrt(jnp.mean(center * center, axis=-1, keepdims=True) + EPS)
    return (center * inverse, inverse)


def norm_back(grad_in, normed, inverse, gain):
    scaled = grad_in * gain
    first_mean = jnp.mean(scaled, axis=-1, keepdims=True)
    second_mean = jnp.mean(scaled * normed, axis=-1, keepdims=True)
    return inverse * (scaled - first_mean - normed * second_mean)


def gelu_slope(values):
    return (
        0.5 * (1.0 + lax.erf(values * SQRT_HALF))
        + values * jnp.exp(-0.5 * values * values) * INV_ROOT_TAU
    )


def split_heads(matrix):
    return matrix.reshape(matrix.shape[0], matrix.shape[1] // HEAD_DIM, HEAD_DIM)


def widen(part_sum, full_length, offset):
    return lax.dynamic_update_slice_in_dim(
        jnp.zeros((full_length,), jnp.float32), part_sum, offset, 0
    )


def attend_forward(block):
    query_b, key_b, value_b = block
    query_h = split_heads(query_b)
    key_h = split_heads(key_b)
    value_h = split_heads(value_b)
    scores = jnp.einsum("qhd,khd->hqk", query_h, key_h, preferred_element_type=jnp.float32)
    largest = jnp.max(scores, axis=-1, keepdims=True)
    expons = jnp.exp(scores - largest)
    totals = jnp.sum(expons, axis=-1, keepdims=True)
    attn_weights = (expons / totals).astype(jnp.bfloat16)
    context = jnp.einsum("hqk,khd->qhd", attn_weights, value_h, preferred_element_type=jnp.float32)
    return (
        context.reshape(query_b.shape).astype(jnp.bfloat16),
        (largest + jnp.log(totals))[:, :, 0],
    )


def attend_backward(block):
    query_b, key_b, value_b, logsum, grad_ctx = block
    query_h = split_heads(query_b)
    key_h = split_heads(key_b)
    value_h = split_heads(value_b)
    grad_h = split_heads(grad_ctx)
    scores = jnp.einsum("qhd,khd->hqk", query_h, key_h, preferred_element_type=jnp.float32)
    weights_full = jnp.exp(scores - logsum[:, :, None])
    weights_low = weights_full.astype(jnp.bfloat16)
    grad_value = jnp.einsum("hqk,qhd->khd", weights_low, grad_h, preferred_element_type=jnp.float32)
    grad_weights = jnp.einsum("qhd,khd->hqk", grad_h, value_h, preferred_element_type=jnp.float32)
    inner = jnp.sum(weights_full * grad_weights, axis=-1, keepdims=True)
    grad_scores = (weights_full * (grad_weights - inner)).astype(jnp.bfloat16)
    grad_query = jnp.einsum("hqk,khd->qhd", grad_scores, key_h, preferred_element_type=jnp.float32)
    grad_key = jnp.einsum("hqk,qhd->khd", grad_scores, query_h, preferred_element_type=jnp.float32)
    full_shape = query_b.shape
    return (
        grad_query.reshape(full_shape).astype(jnp.bfloat16),
        grad_key.reshape(full_shape).astype(jnp.bfloat16),
        grad_value.reshape(full_shape).astype(jnp.bfloat16),
    )


def on_device(
    tokens,
    weight_query,
    weight_key,
    weight_value,
    weight_output,
    weight_up,
    weight_down,
    bias_query,
    bias_value,
    bias_up,
    bias_output,
    bias_down,
    first_gain,
    first_shift,
    second_gain,
    second_shift,
    out_grad,
):
    w_query, w_key, w_value, w_output, w_up, w_down = (
        lax.all_gather(weight_query, "dp", axis=0, tiled=True),
        lax.all_gather(weight_key, "dp", axis=0, tiled=True),
        lax.all_gather(weight_value, "dp", axis=0, tiled=True),
        lax.all_gather(weight_output, "dp", axis=1, tiled=True),
        lax.all_gather(weight_up, "dp", axis=0, tiled=True),
        lax.all_gather(weight_down, "dp", axis=1, tiled=True),
    )
    vectors = (
        lax.all_gather(bias_query, ("dp", "tensor"), axis=0, tiled=True),
        lax.all_gather(bias_value, ("dp", "tensor"), axis=0, tiled=True),
        lax.all_gather(bias_up, ("dp", "tensor"), axis=0, tiled=True),
        lax.all_gather(bias_output, ("dp", "tensor"), axis=0, tiled=True),
        lax.all_gather(bias_down, ("dp", "tensor"), axis=0, tiled=True),
        lax.all_gather(first_gain, ("dp", "tensor"), axis=0, tiled=True),
        lax.all_gather(first_shift, ("dp", "tensor"), axis=0, tiled=True),
        lax.all_gather(second_gain, ("dp", "tensor"), axis=0, tiled=True),
        lax.all_gather(second_shift, ("dp", "tensor"), axis=0, tiled=True),
    )
    query_all, value_all, up_all, out_bias, down_bias, gain_one, shift_one, gain_two, shift_two = [
        member.astype(jnp.float32) for member in vectors
    ]
    width_here = w_query.shape[1]
    hidden_here = w_up.shape[1]
    full_hidden = up_all.shape[0]
    model_width = tokens.shape[1]
    tensor_pos = lax.axis_index("tensor")
    query_bias = lax.dynamic_slice_in_dim(query_all, tensor_pos * width_here, width_here)
    value_bias = lax.dynamic_slice_in_dim(value_all, tensor_pos * width_here, width_here)
    scale = HEAD_DIM ** (-0.5)
    gathered = lax.all_gather(tokens, "tensor", axis=0, tiled=True)
    joined = jnp.concatenate([w_query, w_key, w_value], axis=1)
    projected = jnp.dot(gathered, joined, preferred_element_type=jnp.float32)
    query_b = ((projected[:, :width_here] + query_bias) * scale).astype(jnp.bfloat16)
    key_b = projected[:, width_here : 2 * width_here].astype(jnp.bfloat16)
    value_b = (projected[:, 2 * width_here :] + value_bias).astype(jnp.bfloat16)
    seq_count = gathered.shape[0] // LEN

    def by_sequence(matrix):
        return matrix.reshape(seq_count, LEN, matrix.shape[-1])

    context, logsum = lax.map(
        attend_forward, (by_sequence(query_b), by_sequence(key_b), by_sequence(value_b))
    )
    context = context.reshape(-1, width_here)
    attn_sum = lax.psum_scatter(
        jnp.dot(context, w_output, preferred_element_type=jnp.float32).astype(jnp.bfloat16),
        "tensor",
        scatter_dimension=0,
        tiled=True,
    ).astype(jnp.float32)
    resid_one = tokens.astype(jnp.float32) + (attn_sum + out_bias)
    normed_one, inverse_one = layer_stats(resid_one)
    hidden = normed_one * gain_one + shift_one
    hidden_low = hidden.astype(jnp.bfloat16)
    ffn_rows = lax.all_gather(hidden_low, "tensor", axis=0, tiled=True)
    up_use, down_use = (w_up, w_down)
    up_bias = lax.dynamic_slice_in_dim(up_all, tensor_pos * hidden_here, hidden_here)
    preact = jnp.dot(ffn_rows, up_use, preferred_element_type=jnp.float32) + up_bias
    active = jax.nn.gelu(preact, approximate=False).astype(jnp.bfloat16)
    down_sum = lax.psum_scatter(
        jnp.dot(active, down_use, preferred_element_type=jnp.float32).astype(jnp.bfloat16),
        "tensor",
        scatter_dimension=0,
        tiled=True,
    ).astype(jnp.float32)
    resid_two = hidden + (down_sum + down_bias)
    normed_two, inverse_two = layer_stats(resid_two)
    layer_out = (normed_two * gain_two + shift_two).astype(jnp.bfloat16)
    grad_top = out_grad.astype(jnp.float32)
    grad_gain_two = jnp.sum(grad_top * normed_two, axis=0)
    grad_shift_two = jnp.sum(grad_top, axis=0)
    d_resid_two = norm_back(grad_top, normed_two, inverse_two, gain_two)
    d_down = d_resid_two.astype(jnp.bfloat16)
    grad_down_bias = jnp.sum(d_down, axis=0, dtype=jnp.float32)
    d_rows = lax.all_gather(d_down, "tensor", axis=0, tiled=True)
    grad_down = jnp.einsum("nf,nd->fd", active, d_rows, preferred_element_type=jnp.float32)
    d_active = jnp.einsum("nd,fd->nf", d_rows, down_use, preferred_element_type=jnp.float32)
    d_pre = (d_active * gelu_slope(preact)).astype(jnp.bfloat16)
    grad_up_part = jnp.sum(d_pre, axis=0, dtype=jnp.float32)
    grad_up = jnp.einsum("nd,nf->df", ffn_rows, d_pre, preferred_element_type=jnp.float32)
    d_from_ffn = lax.psum_scatter(
        jnp.einsum("nf,df->nd", d_pre, up_use, preferred_element_type=jnp.float32).astype(
            jnp.bfloat16
        ),
        "tensor",
        scatter_dimension=0,
        tiled=True,
    ).astype(jnp.float32)
    grad_up_bias = widen(grad_up_part, full_hidden, tensor_pos * hidden_here)
    d_hidden = d_resid_two + d_from_ffn
    grad_gain_one = jnp.sum(d_hidden * normed_one, axis=0)
    grad_shift_one = jnp.sum(d_hidden, axis=0)
    d_resid_one = norm_back(d_hidden, normed_one, inverse_one, gain_one)
    d_attn = d_resid_one.astype(jnp.bfloat16)
    grad_out_bias = jnp.sum(d_attn, axis=0, dtype=jnp.float32)
    d_attn_rows = lax.all_gather(d_attn, "tensor", axis=0, tiled=True)
    grad_output = jnp.einsum("nc,nd->cd", context, d_attn_rows, preferred_element_type=jnp.float32)
    d_context = jnp.einsum(
        "nd,cd->nc", d_attn_rows, w_output, preferred_element_type=jnp.float32
    ).astype(jnp.bfloat16)
    d_query, d_key, d_value = lax.map(
        attend_backward,
        (
            by_sequence(query_b),
            by_sequence(key_b),
            by_sequence(value_b),
            logsum,
            by_sequence(d_context),
        ),
    )
    d_joined = jnp.concatenate(
        [
            (d_query * scale).reshape(-1, width_here),
            d_key.reshape(-1, width_here),
            d_value.reshape(-1, width_here),
        ],
        axis=1,
    )
    grad_joined = jnp.einsum("nd,nc->dc", gathered, d_joined, preferred_element_type=jnp.float32)
    grad_query_w = grad_joined[:, :width_here]
    grad_key_w = grad_joined[:, width_here : 2 * width_here]
    grad_value_w = grad_joined[:, 2 * width_here :]
    bias_sums = jnp.sum(d_joined, axis=0, dtype=jnp.float32)
    grad_query_bias = widen(bias_sums[:width_here], model_width, tensor_pos * width_here)
    grad_value_bias = widen(bias_sums[2 * width_here :], model_width, tensor_pos * width_here)
    d_from_attn = lax.psum_scatter(
        jnp.einsum("nc,dc->nd", d_joined, joined, preferred_element_type=jnp.float32).astype(
            jnp.bfloat16
        ),
        "tensor",
        scatter_dimension=0,
        tiled=True,
    ).astype(jnp.float32)
    input_grad = (d_resid_one + d_from_attn).astype(jnp.bfloat16)
    grad_query_w, grad_key_w, grad_value_w, grad_output, grad_up, grad_down = (
        lax.psum_scatter(
            grad_query_w.astype(jnp.bfloat16), "dp", scatter_dimension=0, tiled=True
        ).astype(jnp.float32),
        lax.psum_scatter(
            grad_key_w.astype(jnp.bfloat16), "dp", scatter_dimension=0, tiled=True
        ).astype(jnp.float32),
        lax.psum_scatter(
            grad_value_w.astype(jnp.bfloat16), "dp", scatter_dimension=0, tiled=True
        ).astype(jnp.float32),
        lax.psum_scatter(
            grad_output.astype(jnp.bfloat16), "dp", scatter_dimension=1, tiled=True
        ).astype(jnp.float32),
        lax.psum_scatter(
            grad_up.astype(jnp.bfloat16), "dp", scatter_dimension=0, tiled=True
        ).astype(jnp.float32),
        lax.psum_scatter(
            grad_down.astype(jnp.bfloat16), "dp", scatter_dimension=1, tiled=True
        ).astype(jnp.float32),
    )
    vector_sums = (
        lax.psum_scatter(grad_query_bias, ("dp", "tensor"), scatter_dimension=0, tiled=True),
        lax.psum_scatter(grad_value_bias, ("dp", "tensor"), scatter_dimension=0, tiled=True),
        lax.psum_scatter(grad_up_bias, ("dp", "tensor"), scatter_dimension=0, tiled=True),
        lax.psum_scatter(grad_out_bias, ("dp", "tensor"), scatter_dimension=0, tiled=True),
        lax.psum_scatter(grad_down_bias, ("dp", "tensor"), scatter_dimension=0, tiled=True),
        lax.psum_scatter(grad_gain_one, ("dp", "tensor"), scatter_dimension=0, tiled=True),
        lax.psum_scatter(grad_shift_one, ("dp", "tensor"), scatter_dimension=0, tiled=True),
        lax.psum_scatter(grad_gain_two, ("dp", "tensor"), scatter_dimension=0, tiled=True),
        lax.psum_scatter(grad_shift_two, ("dp", "tensor"), scatter_dimension=0, tiled=True),
    )
    return (
        layer_out,
        input_grad,
        grad_query_w,
        grad_key_w,
        grad_value_w,
        grad_output,
        grad_up,
        grad_down,
    ) + tuple(vector_sums)


def either(*args):
    sizes = (lax.axis_size("dp"), lax.axis_size("tensor"))
    fits = args[0].shape == (LEN, 1024) and args[5].shape[1] * 2 == 4096 and sizes == (16, 2)
    return whole_sequences(*args) if fits else on_device(*args)


def solution(mesh):
    placed = (
        P(("dp", "tensor"), None),
        P("dp", "tensor"),
        P("dp", "tensor"),
        P("dp", "tensor"),
        P("tensor", "dp"),
        P("dp", "tensor"),
        P("tensor", "dp"),
        P(("dp", "tensor")),
        P(("dp", "tensor")),
        P(("dp", "tensor")),
        P(("dp", "tensor")),
        P(("dp", "tensor")),
        P(("dp", "tensor")),
        P(("dp", "tensor")),
        P(("dp", "tensor")),
        P(("dp", "tensor")),
        P(("dp", "tensor"), None),
    )
    return jax.shard_map(
        either,
        mesh=mesh,
        in_specs=placed,
        out_specs=(
            P(("dp", "tensor"), None),
            P(("dp", "tensor"), None),
            P("dp", "tensor"),
            P("dp", "tensor"),
            P("dp", "tensor"),
            P("tensor", "dp"),
            P("dp", "tensor"),
            P("tensor", "dp"),
            P(("dp", "tensor")),
            P(("dp", "tensor")),
            P(("dp", "tensor")),
            P(("dp", "tensor")),
            P(("dp", "tensor")),
            P(("dp", "tensor")),
            P(("dp", "tensor")),
            P(("dp", "tensor")),
            P(("dp", "tensor")),
        ),
        check_vma=False,
    )
```

```python
import functools
import jax
import jax.numpy as jnp
from jax import lax
from jax.experimental import pallas as pl
from jax.experimental.pallas import tpu as pltpu
from jax.sharding import PartitionSpec as P

HEAD_DIM = 64
LEN = 1024
EPS = 1e-05
SQRT_HALF = 0.7071067811865476
INV_ROOT_TAU = 0.3989422804014327
BF, F32 = jnp.bfloat16, jnp.float32
MESH = pl.DeviceIdType.MESH
NT = (((1,), (1,)), ((), ()))
TILE = 512
TILES = LEN // TILE
SIDE = 256
QW = 384
FW = 512

FORWARD_PLAN = {"a0": 3, "a2": 4, "a4": 5, "a6": 6, "n": 7}
GATHER_MID = (7, 9, 11, 13)
SCATTER_MID = ()
BACKWARD_PLAN = {
    "f1": [0], "f2": [1], "f4": [2], "f6": [3], "n": [4], "a0": [5],
    "j0": [6], "a2": [7], "j1": [8], "a4": [9], "j2": [10], "a6": [11],
}


def tile_rows(t):
    return pl.ds(t * TILE if isinstance(t, int) else pl.multiple_of(t * TILE, TILE), TILE)


def tile_blocks(t):
    return pl.ds(t * (TILE // 256), TILE // 256)


def mm(a, b):
    return jnp.dot(a, b, preferred_element_type=F32)


def mm_nt(a, b):
    return lax.dot_general(a, b, NT, preferred_element_type=F32)


def gelu_both(z):
    far = 1.0 / (1.0 + (0.3275911 * SQRT_HALF) * jnp.abs(z))
    bell = jnp.exp(-0.5 * z * z)
    poly = far * (
        0.127414796
        + far * (-0.142248368 + far * (0.7107068705 + far * (-0.7265760135 + far * 0.5307027145)))
    )
    tail = poly * bell
    cdf = jnp.where(z >= 0, 1.0 - tail, tail)
    return z * cdf, cdf + z * bell * INV_ROOT_TAU


def ln_stats(resid):
    center = resid - jnp.mean(resid, axis=-1, keepdims=True)
    inverse = lax.rsqrt(jnp.mean(center * center, axis=-1, keepdims=True) + EPS)
    return center * inverse, inverse


def three_terms(value, lane, at):
    hi = value.astype(BF).astype(F32)
    mid = (value - hi).astype(BF).astype(F32)
    rest = value - hi - mid
    return jnp.where(lane == at, hi, jnp.where(lane == at + 1, mid, jnp.where(lane == at + 2, rest, 0.0)))


def device(z, y, c, x):
    return {"dp": (z * 2 + y) * 2 + c, "tensor": x}


class Place:
    def __init__(self, nz):
        dp, x = lax.axis_index("dp"), lax.axis_index("tensor")
        z, y, c = dp // 4, lax.rem(dp // 2, 2), lax.rem(dp, 2)
        self.nz, self.z, self.y, self.c, self.x = nz, z, y, c, x
        self.not_y, self.not_c, self.not_x = 1 - y, 1 - c, 1 - x
        self.z_at = [z] + [lax.rem(z + s, nz) for s in range(1, nz)]
        self.to_z = [None] + [device(at, y, c, x) for at in self.z_at[1:]]
        self.to_y, self.to_c, self.to_x = device(z, 1 - y, c, x), device(z, y, 1 - c, x), device(z, y, c, 1 - x)

    def lanes(self, w):
        return pl.ds(pl.multiple_of(self.x * w, 128), w)

    def other_lanes(self, w):
        return pl.ds(pl.multiple_of(self.not_x * w, 128), w)

    def greet(self):
        bar = pltpu.get_barrier_semaphore()
        others = self.to_z[1:] + [self.to_y, self.to_c, self.to_x]
        for other in others:
            pl.semaphore_signal(bar, inc=1, device_id=other, device_id_type=MESH)
        pl.semaphore_wait(bar, len(others))


class Mover:
    def __init__(self, at, send, recv):
        self.at, self.send, self.recv, self.sent = at, send, recv, {}

    def go(self, k, slot, src, dst, to):
        copy = pltpu.make_async_remote_copy(
            src_ref=src,
            dst_ref=dst,
            send_sem=self.send.at[k, slot],
            recv_sem=self.recv.at[k, slot],
            device_id=to,
            device_id_type=MESH,
        )
        copy.start()
        self.sent.setdefault(k, []).append(copy)
        return copy


class Gather(Mover):
    def __init__(self, at, send, recv, chunks, mid):
        super().__init__(at, send, recv)
        self.chunks, self.mid, self.flying, self.next = chunks, mid, {}, 0

    def wait(self, k, stage):
        for copy in self.flying.pop((k, stage)):
            copy.wait_recv()

    def begin(self, k):
        at, (buf, w, split) = self.at, self.chunks[k]
        if k in self.mid:
            up, down = (buf.at[at.z, at.y, at.c, pl.ds(r, 32), at.lanes(w)] for r in (0, 32))
            self.flying[(k, 0)] = [self.go(k, 3, up, up, at.to_x), self.go(k, 4, down, down, at.to_y)]
            return
        own = buf.at[at.z, at.y, at.c, :, at.lanes(w)]
        self.flying[(k, 0)] = [self.go(k, s - 1, own, own, at.to_z[s]) for s in range(1, at.nz)]

    def first(self, k):
        self.wait(k, 0)
        at, (buf, w, split) = self.at, self.chunks[k]
        r = 32 if split else buf.shape[3]
        if k in self.mid:
            up = buf.at[at.z, at.y, at.c, pl.ds(0, r)]
            down = buf.at[at.z, :, at.c, pl.ds(r, r), at.lanes(w)]
            copies = [self.go(k, s - 1, up, up, at.to_z[s]) for s in range(1, at.nz)]
            copies += [self.go(k, 7 + s, down, down, at.to_z[s]) for s in range(1, at.nz)]
        else:
            up = buf.at[:, at.y, at.c, pl.ds(0, r), at.lanes(w)]
            copies = [self.go(k, 3, up, up, at.to_x)]
            if split:
                down = buf.at[:, at.y, at.c, pl.ds(r, r), at.lanes(w)]
                copies.append(self.go(k, 4, down, down, at.to_y))
        self.flying[(k, 1)] = copies

    def second(self, k):
        self.wait(k, 1)
        at, (buf, w, split) = self.at, self.chunks[k]
        r = 32 if split else buf.shape[3]
        up = buf.at[:, at.y, at.c, pl.ds(0, r)]
        copies = [self.go(k, 5, up, up, at.to_y)]
        if split:
            down = buf.at[:, :, at.c, pl.ds(r, r), at.lanes(w)]
            copies.append(self.go(k, 6, down, down, at.to_x))
        self.flying[(k, 2)] = copies

    def core(self, k):
        self.wait(k, 2)
        at, (buf, w, split) = self.at, self.chunks[k]
        part = buf.at[:, :, at.c]
        self.flying[(k, 3)] = [self.go(k, 7, part, part, at.to_c)]

    def push(self, upto):
        last = len(self.chunks) - 1
        while self.next <= min(upto, last + 1):
            k = self.next
            if k > 0:
                self.core(k - 1)
            for m, stage, kinds in ((k + 6, self.begin, 1), (k + 5, self.begin, 0), (k + 4, self.first, 1), (k + 2, self.first, 0)):
                if m <= last and (m in self.mid) == bool(kinds):
                    stage(m)
            if k + 1 <= last:
                self.second(k + 1)
            self.next += 1

    def ready(self, k):
        self.push(k + 1)
        self.wait(k, 3)


class Scatter(Mover):
    def __init__(self, at, send, recv, count, mid, got_mid):
        super().__init__(at, send, recv)
        self.chunks, self.flying, self.done, self.count = {}, {}, set(), count
        self.mid, self.got_mid = mid, got_mid

    def add(self, k, buf, w, got, split, finish):
        self.chunks[k] = (buf, w, got, split, finish)

    def stage(self, k, s):
        at, nz = self.at, self.at.nz
        z, y, c = at.z, at.y, at.c
        buf, w, (got_c, got_y, got_x, got_y2, got_x2, got_z), split, finish = self.chunks[k]
        r = 32 if split else buf.shape[3]
        up, down = pl.ds(0, r), pl.ds(r, r)
        mine, other = at.lanes(w), at.other_lanes(w)
        assert (k, s) not in self.done and (s == 0 or (k, s - 1) in self.done)
        assert s == 4 or k == 0 or (k - 1, s + 1) in self.done
        self.done.add((k, s))
        for copy in self.flying.pop((k, s - 1), []):
            copy.wait_recv()
        copies = []
        if s == 0:
            copies = [self.go(k, 0, buf.at[:, :, at.not_c], got_c, at.to_c)]
        elif s == 1:

            def fold(m, carry):
                zz, yy = m // 2, lax.rem(m, 2)
                buf[zz, yy, c] += got_c[zz, yy]
                return carry

            lax.fori_loop(0, 2 * nz, fold, 0)
            copies = [self.go(k, 1, buf.at[:, at.not_y, c, up], got_y, at.to_y)]
            if split:
                copies.append(self.go(k, 2, buf.at[:, :, c, down, other], got_x, at.to_x))
        elif s == 2:

            def fold(zz, carry):
                buf[zz, y, c, up] += got_y[zz]
                if split:
                    for yy in range(2):
                        buf[zz, yy, c, down, mine] += got_x[zz, yy]
                return carry

            lax.fori_loop(0, nz, fold, 0)
            if k in self.mid:
                got_u, got_d, _, _ = self.got_mid(k)
                copies = []
                for d in range(1, nz):
                    copies.append(self.go(k, 4 + d, buf.at[at.z_at[d], y, c, up], got_u.at[d - 1], at.to_z[d]))
                    copies.append(
                        self.go(k, 7 + d, buf.at[at.z_at[d], :, c, down, mine], got_d.at[d - 1], at.to_z[d])
                    )
                self.flying[(k, s)] = copies
                return
            copies = [self.go(k, 3, buf.at[:, y, c, up, other], got_x2, at.to_x)]
            if split:
                copies.append(self.go(k, 4, buf.at[:, at.not_y, c, down, mine], got_y2, at.to_y))
        elif s == 3 and k in self.mid:
            got_u, got_d, got_x3, got_y3 = self.got_mid(k)
            for d in range(nz - 1):
                buf[z, y, c, up] += got_u[d]
                buf[z, :, c, down, mine] += got_d[d]
            copies = [
                self.go(k, 3, buf.at[z, y, c, up, other], got_x3, at.to_x),
                self.go(k, 4, buf.at[z, at.not_y, c, down, mine], got_y3, at.to_y),
            ]
        elif k in self.mid:
            _, _, got_x3, got_y3 = self.got_mid(k)
            halves = [
                buf[z, y, c, rows, mine].astype(F32) + got[...].astype(F32) for rows, got in ((up, got_x3), (down, got_y3))
            ]
            finish(jnp.concatenate(halves, axis=0))
        elif s == 3:

            def fold(zz, carry):
                buf[zz, y, c, up, mine] += got_x2[zz]
                if split:
                    buf[zz, y, c, down, mine] += got_y2[zz]
                return carry

            lax.fori_loop(0, nz, fold, 0)
            copies = [
                self.go(k, 4 + d, buf.at[at.z_at[d], y, c, :, mine], got_z.at[d - 1], at.to_z[d])
                for d in range(1, nz)
            ]
        else:
            total = buf[z, y, c, :, mine].astype(F32)
            for d in range(1, nz):
                total = total + got_z[d - 1].astype(F32)
            finish(total)
        self.flying[(k, s)] = copies

    def settle(self, k):
        assert (k, 4) in self.done
        for copy in self.sent.pop(k):
            copy.wait_send()

    def run(self, plan):
        for item in plan:
            if isinstance(item, tuple):
                self.stage(*item)
                continue
            for s in (4, 3, 2, 1, 0):
                k = item - s
                if 0 <= k < self.count and (k, s) not in self.done:
                    self.stage(k, s)


def transpose_in_place(ref):
    for a in range(LEN // SIDE):
        for b in range(a, LEN // SIDE):
            ra, rb = slice(a * SIDE, a * SIDE + SIDE), slice(b * SIDE, b * SIDE + SIDE)
            first = ref[ra, rb].T
            if a != b:
                ref[ra, rb] = ref[rb, ra].T
            ref[rb, ra] = first


def transpose_into(dst, src):
    for t in range(LEN // SIDE):
        dst[:, t * SIDE : t * SIDE + SIDE] = src[t * SIDE : t * SIDE + SIDE].T


def layer_kernel(
    nz,
    tok_hbm, og_hbm, wq_hbm, wk_hbm, wv_hbm, wo_hbm, wu_hbm, wd_hbm, sv, su,
    lo_hbm, ig_hbm, outu_hbm, outd_hbm, outo_hbm, outq_hbm, outv_hbm, pair_hbm, qa_hbm, act_hbm,
    gv, gq, go, gu, gd, bias, bup, tok, ctx, acc, n1, inv1, hlow, ddown, spare, mixed, work,
    qs, kv, qa, kt, dqt, vgrad,
    rc, ry, rx, ry2, rx2, rz, rzu, rzd, rx3, ry3, rbv, rcv, ryv, rxv, ry2v, rx2v, rzv, out, outv,
    send, recv, send2, recv2, lsem,
):
    at = Place(nz)
    used = [0]

    def start_local(src, dst):
        copy = pltpu.make_async_copy(src, dst, lsem.at[used[0]])
        used[0] += 1
        copy.start()
        return copy

    def loop(body, n=TILES):
        def step(t, carry):
            body(t)
            return carry

        lax.fori_loop(0, n, step, 0)

    own = (at.z, at.y, at.c)
    chunks = [(gv, 128, False)]
    chunks += [(gq.at[i], QW, True) for i in range(4)] + [(go, FW, True)]
    for j in range(4):
        chunks += [(gu.at[j], FW, True), (gd.at[j], FW, True)]
    placed = [[] for _ in chunks]
    for i in range(4):
        for m, w_hbm in enumerate((wq_hbm, wk_hbm, wv_hbm)):
            lanes = pl.ds(pl.multiple_of(at.x * QW + m * 128, 128), 128)
            placed[1 + i].append(start_local(w_hbm.at[:, pl.ds(i * 128, 128)], gq.at[(i, *own, slice(None), lanes)]))
    tok_in = start_local(tok_hbm, tok)
    placed[5].append(start_local(wo_hbm, go.at[(*own, slice(None), at.lanes(FW))]))
    for j in range(4):
        for m, (w_hbm, g) in enumerate(((wu_hbm, gu), (wd_hbm, gd))):
            placed[6 + 2 * j + m].append(
                start_local(w_hbm.at[:, pl.ds(j * FW, FW)], g.at[(j, *own, slice(None), at.lanes(FW))])
            )
    og_in = start_local(og_hbm, mixed)
    quarter = lax.broadcasted_iota(jnp.int32, (8, 128), 1) // 32
    mine = quarter == lax.rem(at.c, 2) * 2 + at.x
    pieces = jnp.where(mine, jnp.concatenate([sv[...].astype(F32)] * 4, axis=1), 0.0).astype(BF)
    gv[at.z, at.y, at.c, 0:8, at.lanes(128)] = pieces
    gv[at.z, at.y, at.c, 8:16, at.lanes(128)] = jnp.broadcast_to(su[...], (8, 128))
    at.greet()
    gather = Gather(at, send, recv, chunks, GATHER_MID)
    for k in range(len(chunks)):
        for copy in placed[k]:
            copy.wait()
        if k < 5:
            gather.begin(k)
    gather.first(0)
    gather.first(1)
    gather.second(0)
    gather.ready(0)
    for t in range(8):
        sums = None
        for owner in range(4 * t, 4 * t + 4):
            dp_o, x_o = owner // 2, owner % 2
            block = gv[dp_o // 4, dp_o // 2 % 2, dp_o % 2, :, x_o * 128 : x_o * 128 + 128].astype(F32)
            sums = block if sums is None else sums + block
            bup[:, owner * 128 : owner * 128 + 128] = jnp.broadcast_to(block[8:9], (8, 128))
        bias[:, t * 128 : t * 128 + 128] = sums
    tok_in.wait()

    lane = lax.broadcasted_iota(jnp.int32, (TILE, 128), 1)
    low_half = lane < 64
    halves = (low_half, jnp.logical_not(low_half))

    def project(i):
        def body(t):
            rows = tile_rows(t)
            part = mm(tok[rows], gq[i].reshape(1024, 2 * QW))
            for xx in range(2):
                pair, base = xx * 4 + i, xx * QW
                bq = bias[0:1, pair * 128 : pair * 128 + 128]
                bv = bias[1:2, pair * 128 : pair * 128 + 128]
                qs[xx, rows] = ((part[:, base : base + 128] + bq) * 0.125).astype(BF)
                key = part[:, base + 128 : base + 256].astype(BF)
                value = (part[:, base + 256 : base + 384] + bv).astype(BF)
                one = jnp.ones_like(key)
                for h in range(2):
                    kv[xx, h, rows] = jnp.where(halves[h], key, one)
                    kv[xx, 2 + h, rows] = jnp.where(halves[h], value, one)

        loop(body)

    def attend(i, xx):
        pair = xx * 4 + i

        def body(t):
            rows = tile_rows(t)
            q = qs[xx, rows]
            scores = [mm_nt(jnp.where(halves[h], q, jnp.zeros_like(q)), kv[xx, h]) for h in range(2)]
            tops = [jnp.max(s, axis=-1, keepdims=True) for s in scores]
            expons = [jnp.exp(s - top).astype(BF) for s, top in zip(scores, tops)]
            outs = [mm(expons[h], kv[xx, 2 + h]) for h in range(2)]
            for h in range(2):
                extra = three_terms(-(tops[h] + jnp.log(outs[h])), lane, 64 * (1 - h))
                qa[xx, h, rows] = jnp.where(halves[h], q.astype(F32), extra).astype(BF)
            total = pltpu.roll(jnp.where(low_half, outs[1], outs[0]), 64, 1)
            ctx[rows, pair * 128 : pair * 128 + 128] = (jnp.where(low_half, outs[0], outs[1]) / total).astype(BF)

        loop(body)

    spilled = []
    for i in range(4):
        gather.ready(1 + i)
        for copy in spilled:
            copy.wait()
        spilled = []
        project(i)
        for xx in range(2):
            attend(i, xx)
            spilled += [start_local(kv.at[xx], pair_hbm.at[xx * 4 + i]), start_local(qa.at[xx], qa_hbm.at[xx * 4 + i])]
            gather.push(FORWARD_PLAN.get(f"a{2 * i + xx}", 0))

    gather.ready(5)

    def first_norm(t):
        rows = tile_rows(t)
        attn = mm_nt(ctx[rows], go[...].reshape(1024, 1024))
        normed, inverse = ln_stats(tok[rows].astype(F32) + (attn + bias[2:3]))
        n1[rows] = normed.astype(BF)
        inv1[rows] = jnp.broadcast_to(inverse, (TILE, 128))
        h = normed * bias[4:5] + bias[5:6]
        acc[rows] = h
        hlow[rows] = h.astype(BF)

    loop(first_norm)
    for copy in spilled:
        copy.wait()
    gather.push(FORWARD_PLAN.get("n", 0))
    transpose_in_place(tok)
    hlow_t, ddown_t = spare, hlow
    transpose_into(hlow_t, hlow)

    def ffn_up(j, xx, slot):
        up = gu.at[j, :, :, :, :, pl.ds(xx * FW, FW)]
        first = xx * 2048 + j * FW
        b_up = bup[0:1, first : first + FW]

        def body(t):
            rows = tile_rows(t)
            value, grade = gelu_both(mm(hlow[rows], up[...].reshape(1024, FW)) + b_up)
            work[slot, rows, 0:FW] = value.astype(BF)
            work[slot, rows, FW:] = grade.astype(BF)

        loop(body)

    def ffn_down(j):
        down = gd.at[j]

        def body(t):
            rows = tile_rows(t)
            acc[rows] += sum(
                mm_nt(work[xx, rows, 0:FW], down[:, :, :, :, xx * FW : xx * FW + FW].reshape(1024, FW))
                for xx in range(2)
            )

        loop(body)

    stored = {}
    for j in range(4):
        gather.ready(6 + 2 * j)
        for xx in range(2):
            step = 2 * j + xx
            if step >= 2:
                stored.pop(step - 2).wait()
            ffn_up(j, xx, xx)
            stored[step] = start_local(work.at[xx], act_hbm.at[step])
            gather.push(FORWARD_PLAN.get(f"f{step}", 0))
        gather.ready(7 + 2 * j)
        ffn_down(j)
    og_in.wait()
    vgrad[...] = jnp.zeros_like(vgrad)
    bgrad = bup
    bgrad[...] = jnp.zeros_like(bgrad)

    def second_norm(t):
        rows = tile_rows(t)
        normed, inverse = ln_stats(acc[rows] + bias[3:4])
        g = mixed[rows].astype(F32)
        mixed[rows] = (normed * bias[6:7] + bias[7:8]).astype(BF)
        u = g * bias[6:7]
        first_mean = jnp.mean(u, axis=-1, keepdims=True)
        second_mean = jnp.mean(u * normed, axis=-1, keepdims=True)
        d = inverse * (u - first_mean - normed * second_mean)
        acc[rows] = d
        low = d.astype(BF)
        ddown[rows] = low
        vgrad[6:7] += jnp.sum(g * normed, axis=0, keepdims=True)
        vgrad[7:8] += jnp.sum(g, axis=0, keepdims=True)
        vgrad[3:4] += jnp.sum(low.astype(F32), axis=0, keepdims=True)

    loop(second_norm)
    lo_copy = start_local(mixed, lo_hbm)
    for copies in gather.sent.values():
        for copy in copies:
            copy.wait_send()

    def mid_slots(k):
        m = SCATTER_MID.index(k) % 2
        return rzu.at[m], rzd.at[m], rx3.at[m], ry3.at[m]

    rs = Scatter(at, send2, recv2, 14, SCATTER_MID, mid_slots)
    out_copies = {}

    def finisher(k, hbm, w):
        def finish(total):
            if k - 2 in out_copies:
                out_copies.pop(k - 2).wait()
            stage = out.at[k % 2, :, pl.ds(0, w)]
            stage[...] = total
            out_copies[k] = start_local(stage, hbm)

        return finish

    def finish_vectors(total):
        outv[...] = total
        out_copies[99] = start_local(outv, outv_hbm)

    plain = [k for k in range(14) if k not in SCATTER_MID and k != 12]

    def slots(k, w):
        s, t = k % 2, plain.index(k) % 2 if k in plain else 0
        return (
            rc.at[s, :, :, :, pl.ds(0, 2 * w)], ry.at[s, :, :, pl.ds(0, 2 * w)], rx.at[s, :, :, :, pl.ds(0, w)],
            ry2.at[t, :, :, pl.ds(0, w)], rx2.at[t, :, :, pl.ds(0, w)], rz.at[t, :, :, pl.ds(0, w)],
        )

    transpose_into(ddown_t, ddown)
    loaded = {}

    def load_act(step):
        loaded[step] = start_local(act_hbm.at[step], work.at[step % 2])

    order = [6, 7, 0, 1, 2, 3, 4, 5]
    stored.pop(6).wait()
    stored.pop(7).wait()

    def ffn_back(n, step):
        j, xx, slot = step // 2, step % 2, step % 2
        up, down = gu.at[j, :, :, :, :, pl.ds(xx * FW, FW)], gd.at[j, :, :, :, :, pl.ds(xx * FW, FW)]
        rbu, rbd = gu.at[j], gd.at[j]
        first = xx * 2048 + j * FW

        def rows_body(t):
            rows = tile_rows(t)
            d_act = mm(ddown[rows], down[...].reshape(1024, FW))
            d_pre = (d_act * work[slot, rows, FW:].astype(F32)).astype(BF)
            work[slot, rows, FW:] = d_pre
            bgrad[0:1, first : first + FW] += jnp.sum(d_pre.astype(F32), axis=0, keepdims=True)
            acc[rows] += mm_nt(d_pre, up[...].reshape(1024, FW))

        loop(rows_body)

        for rb, left, right in ((rbu, hlow_t, FW), (rbd, ddown_t, 0)):
            for half in (0, 256):
                part = mm(left[...], work[slot, :, right + half : right + half + 256]).astype(BF)
                rb[:, :, :, :, pl.ds(xx * FW + half, 256)] = part.reshape(-1, 2, 2, 64, 256)
        if xx == 1:
            m = n // 2
            rs.add(2 * m, rbu, FW, slots(2 * m, FW), True, finisher(2 * m, outu_hbm.at[j], FW))
            rs.add(2 * m + 1, rbd, FW, slots(2 * m + 1, FW), True, finisher(2 * m + 1, outd_hbm.at[j], FW))

    for n, step in enumerate(order):
        if step in loaded:
            loaded[step].wait()
        ffn_back(n, step)
        if n + 2 < 8:
            load_act(order[n + 2])
        rs.run(BACKWARD_PLAN.get(f"f{n}", ()))

    lo_copy.wait()
    dattn, dattn_t, dctx, doa = ddown, ddown_t, mixed, qs

    def first_norm_back(t):
        rows = tile_rows(t)
        dh = acc[rows]
        normed = n1[rows].astype(F32)
        w = dh * bias[4:5]
        first_mean = jnp.mean(w, axis=-1, keepdims=True)
        second_mean = jnp.mean(w * normed, axis=-1, keepdims=True)
        d = inv1[rows, 0:1] * (w - first_mean - normed * second_mean)
        low = d.astype(BF)
        acc[rows] = d
        dattn[rows] = low
        dctx[rows] = mm(low, go[...].reshape(1024, 1024)).astype(BF)
        vgrad[4:5] += jnp.sum(dh * normed, axis=0, keepdims=True)
        vgrad[5:6] += jnp.sum(dh, axis=0, keepdims=True)
        vgrad[2:3] += jnp.sum(low.astype(F32), axis=0, keepdims=True)

    loop(first_norm_back)
    rs.run(BACKWARD_PLAN.get("n", ()))
    pair_in = {}

    def load_pair(step):
        i, xx = step // 2, step % 2
        pair_in[step] = [start_local(pair_hbm.at[xx * 4 + i], kv.at[xx]), start_local(qa_hbm.at[xx * 4 + i], qa.at[xx])]

    load_pair(0)
    load_pair(1)
    transpose_into(dattn_t, dattn)

    def output_grads(t):
        part = mm(dattn_t[tile_rows(t)], ctx[...]).astype(BF)
        go[tile_blocks(t)] = part.reshape(-1, 2, 2, 64, 1024)

    loop(output_grads)
    rs.add(8, go, FW, slots(8, FW), True, finisher(8, outo_hbm, FW))
    rs.run(BACKWARD_PLAN.get("m", ()))

    def attend_back(i, xx, dj):
        pair = xx * 4 + i
        cols = slice(pair * 128, pair * 128 + 128)
        base = xx * QW

        for t in range(TILES):
            rows = tile_rows(t)
            do_t = dctx[rows, cols]
            prod = do_t.astype(F32) * ctx[rows, cols].astype(F32)
            for h in range(2):
                inner = -jnp.sum(jnp.where(halves[h], prod, 0.0), axis=-1, keepdims=True)
                doa[h, rows] = jnp.where(
                    halves[h], do_t.astype(F32), three_terms(inner, lane, 64 * (1 - h))
                ).astype(BF)
            kt[:, rows] = jnp.where(low_half, kv[xx, 0, rows], kv[xx, 1, rows]).T

        dqt[...] = jnp.zeros_like(dqt)

        def keys_body(t):
            rows = tile_rows(t)
            grads_k, grads_v = [], []
            for h in range(2):
                probs = jnp.exp(mm_nt(kv[xx, h, rows], qa[xx, h]))
                d_scores = (probs * mm_nt(kv[xx, 2 + h, rows], doa[h])).astype(BF)
                grads_v.append(mm(probs.astype(BF), dctx[:, cols]))
                grads_k.append(mm(d_scores, qa[xx, h]))
                dqt[h * 64 : h * 64 + 64] += mm(kt[h * 64 : h * 64 + 64, rows], d_scores)
            dj[rows, base + 128 : base + 256] = jnp.where(low_half, grads_k[0], grads_k[1]).astype(BF)
            dj[rows, base + 256 : base + 384] = jnp.where(low_half, grads_v[0], grads_v[1]).astype(BF)

        loop(keys_body)
        for t in range(LEN // SIDE):
            rows = slice(t * SIDE, t * SIDE + SIDE)
            dj[rows, base : base + 128] = (dqt[:, rows].T * 0.125).astype(BF)
        sums = jnp.sum(dj[:, base : base + QW].astype(F32), axis=0, keepdims=True)
        vgrad[0:1, cols] = sums[:, 0:128]
        vgrad[1:2, cols] = sums[:, 256:384]

    def joined_grads(dj, rbq):
        for third in range(0, 2 * QW, 256):
            part = mm(tok[...], dj[:, third : third + 256]).astype(BF)
            rbq[:, :, :, :, pl.ds(third, 256)] = part.reshape(-1, 2, 2, 64, 256)

    def back(i, dj):
        def body(t):
            rows = tile_rows(t)
            acc[rows] += mm_nt(dj[rows], gq[i].reshape(1024, 2 * QW))

        loop(body)

    def vectors_body(dev):
        to = rbv.at[dev // 8, lax.rem(dev // 4, 2), lax.rem(dev // 2, 2)]
        lanes = pl.ds(pl.multiple_of(lax.rem(dev, 2) * 128, 128), 128)
        to[0:8, lanes] = vgrad[:, pl.ds(pl.multiple_of(dev // 4 * 128, 128), 128)]
        to[8:16, lanes] = bgrad[:, pl.ds(pl.multiple_of(dev * 128, 128), 128)]

    for i in range(4):
        dj = work.at[i % 2, :, pl.ds(0, 2 * QW)]
        for xx in range(2):
            step = 2 * i + xx
            for copy in pair_in[step]:
                copy.wait()
            attend_back(i, xx, dj)
            if step + 2 < 8:
                load_pair(step + 2)
            rs.run(BACKWARD_PLAN.get(f"a{step}", ()))
        if i < 2:
            rbq = gq.at[i]
            back(i, dj)
        else:
            rs.settle(3 - i)
            rbq = (gu if i == 3 else gd).at[order[0] // 2, :, :, :, :, pl.ds(0, 2 * QW)]
        k = 9 + i
        if i == 3:
            loop(vectors_body, 8 * nz)
            rs.add(12, rbv, 128, (rcv, ryv, rxv, ry2v, rx2v, rzv), False, finish_vectors)
            rs.run([12])
            k = 13
        joined_grads(dj, rbq)
        rs.add(k, rbq, QW, slots(k, QW), True, finisher(9 + i, outq_hbm.at[i], QW))
        rs.run(BACKWARD_PLAN.get(f"j{i}", ()))

    rs.run([13])
    back(2, work.at[0, :, pl.ds(0, 2 * QW)])
    rs.run([14])
    back(3, work.at[1, :, pl.ds(0, 2 * QW)])
    rs.run([15])

    def last(t):
        rows = tile_rows(t)
        mixed[rows] = acc[rows].astype(BF)

    loop(last)
    ig_copy = start_local(mixed, ig_hbm)
    rs.run([16, 17])
    assert len(rs.done) == 14 * 5
    ig_copy.wait()
    for copies in rs.sent.values():
        for copy in copies:
            copy.wait_send()
    for copy in out_copies.values():
        copy.wait()


def layer_call(nz, tok, og, wq, wk, wv, wo, wu, wd, sv, su):
    S, V = jax.ShapeDtypeStruct, pltpu.VMEM
    outs = [
        S((LEN, 1024), BF), S((LEN, 1024), BF), S((4, 64, FW), F32), S((4, 64, FW), F32), S((64, FW), F32),
        S((4, 64, QW), F32), S((16, 128), F32),
        S((8, 4, LEN, 128), BF), S((8, 2, LEN, 128), BF), S((8, LEN, 1024), BF),
    ]

    def gots(n, rows, w, kind):
        r = 32 if rows == 64 else rows
        lead = (n,) if n else ()
        return [
            V((*lead, nz, 2, rows, 2 * w), kind), V((*lead, nz, r, 2 * w), kind), V((*lead, nz, 2, r, w), kind),
            V((*lead, nz, r, w), kind), V((*lead, nz, r, w), kind), V((*lead, nz - 1, rows, w), kind),
        ]

    block = lambda *s: V((*s[:-1], nz, 2, 2, 64, s[-1]), BF)
    scratch = [
        V((nz, 2, 2, 16, 256), BF), block(4, 2 * QW), block(2 * FW), block(4, 2 * FW), block(4, 2 * FW),
        V((16, 1024), F32), V((8, 4096), F32),
        V((LEN, 1024), BF), V((LEN, 1024), BF), V((LEN, 1024), F32), V((LEN, 1024), BF), V((LEN, 128), F32),
        V((LEN, 1024), BF), V((LEN, 1024), BF), V((LEN, 1024), BF), V((LEN, 1024), BF), V((2, LEN, 1024), BF),
        V((2, LEN, 128), BF), V((2, 4, LEN, 128), BF), V((2, 2, LEN, 128), BF),
        V((128, LEN), BF), V((128, LEN), F32), V((8, 1024), F32),
        *gots(2, 64, FW, BF), V((2, nz - 1, 32, 2 * FW), BF), V((2, nz - 1, 2, 32, FW), BF), V((2, 32, FW), BF),
        V((2, 32, FW), BF), V((nz, 2, 2, 16, 256), F32), *gots(0, 16, 128, F32),
        V((2, 64, FW), F32), V((16, 128), F32),
        *[pltpu.SemaphoreType.DMA((14, 11))] * 4, pltpu.SemaphoreType.DMA((96,)),
    ]
    hbm, vmem = pl.BlockSpec(memory_space=pl.ANY), pl.BlockSpec(memory_space=pltpu.VMEM)
    return pl.pallas_call(
        functools.partial(layer_kernel, nz),
        out_shape=outs,
        in_specs=[hbm] * 8 + [vmem, vmem],
        out_specs=[hbm] * len(outs),
        scratch_shapes=scratch,
        compiler_params=pltpu.CompilerParams(
            collective_id=0, has_side_effects=True, vmem_limit_bytes=63 * 1024 * 1024 + 512 * 1024
        ),
        cost_estimate=pl.CostEstimate(flops=90 * 10**9, bytes_accessed=10**8, transcendentals=4 * 10**7),
        name="layer",
    )(tok, og, wq, wk, wv, wo, wu, wd, sv, su)


def finish_kernel(
    lo_in, ig_in, gu_in, gd_in, go_in, gq_in, gv_in, lo, ig, wq, wk, wv, wo, wu, wd, vec, gu, gd, go, gq, gv, sem
):
    pairs = [(gd_in, gd), (gu_in, gu), (gq_in, gq), (go_in, go), (gv_in, gv), (lo_in, lo), (ig_in, ig)]
    copies = [pltpu.make_async_copy(src, dst, sem.at[n]) for n, (src, dst) in enumerate(pairs)]
    for copy in copies:
        copy.start()
    copies[0].wait()
    for i in range(4):
        wd[:, i * FW : i * FW + FW] = gd[i]
    copies[1].wait()
    for i in range(4):
        wu[:, i * FW : i * FW + FW] = gu[i]
    copies[2].wait()
    for i in range(4):
        for m, ref in enumerate((wq, wk, wv)):
            ref[:, i * 128 : i * 128 + 128] = gq[i, :, m * 128 : m * 128 + 128]
    copies[3].wait()
    wo[...] = go[...]
    copies[4].wait()
    quarter = lax.rem(lax.axis_index("dp") * 2 + lax.axis_index("tensor"), 4)
    rows = gv[0:8]
    mine = rows[:, 0:32]
    for q in range(1, 4):
        mine = jnp.where(quarter == q, rows[:, q * 32 : q * 32 + 32], mine)
    vec[0:8] = jnp.concatenate([mine] * 4, axis=1)
    vec[8:16] = gv[8:16]
    copies[5].wait()
    copies[6].wait()


def finish_call(lo, ig, gu, gd, go, gq, gv):
    S, V = jax.ShapeDtypeStruct, pltpu.VMEM
    hbm, vmem = pl.BlockSpec(memory_space=pltpu.MemorySpace.HBM), pl.BlockSpec(memory_space=pltpu.VMEM)
    return pl.pallas_call(
        finish_kernel,
        out_shape=[
            S(lo.shape, BF), S(ig.shape, BF), *[S((64, 512), F32)] * 4, *[S((64, 2048), F32)] * 2,
            S((16, 128), F32),
        ],
        in_specs=[hbm] * 7,
        out_specs=[vmem] * 9,
        scratch_shapes=[*[V(m.shape, F32) for m in (gu, gd, go, gq, gv)], pltpu.SemaphoreType.DMA((7,))],
        compiler_params=pltpu.CompilerParams(vmem_limit_bytes=62 * 1024 * 1024),
        name="finish",
    )(lo, ig, gu, gd, go, gq, gv)


def whole_sequences(tokens, wq, wk, wv, wo, wu, wd, bq, bv, bu, bo, bd, g1, s1, g2, s2, out_grad):
    nz = lax.axis_size("dp") // 4
    sv = jnp.stack([bq, bv, bo, bd, g1, s1, g2, s2])
    lo, ig, gu, gd, go, gq, gv, *_ = layer_call(nz, tokens, out_grad, wq, wk, wv, wo.T, wu, wd.T, sv, bu[None])
    lo, ig, d_wq, d_wk, d_wv, d_wo, d_wu, d_wd, vec = finish_call(lo, ig, gu, gd, go, gq, gv)
    v = [vec[r, :32] for r in range(8)]
    return (lo, ig, d_wq, d_wk, d_wv, d_wo.T, d_wu, d_wd.T, v[0], v[1], vec[8], *v[2:])


def layer_stats(resid):
    center = resid - jnp.mean(resid, axis=-1, keepdims=True)
    inverse = lax.rsqrt(jnp.mean(center * center, axis=-1, keepdims=True) + EPS)
    return (center * inverse, inverse)


def norm_back(grad_in, normed, inverse, gain):
    scaled = grad_in * gain
    first_mean = jnp.mean(scaled, axis=-1, keepdims=True)
    second_mean = jnp.mean(scaled * normed, axis=-1, keepdims=True)
    return inverse * (scaled - first_mean - normed * second_mean)


def gelu_slope(values):
    return (
        0.5 * (1.0 + lax.erf(values * SQRT_HALF))
        + values * jnp.exp(-0.5 * values * values) * INV_ROOT_TAU
    )


def split_heads(matrix):
    return matrix.reshape(matrix.shape[0], matrix.shape[1] // HEAD_DIM, HEAD_DIM)


def widen(part_sum, full_length, offset):
    return lax.dynamic_update_slice_in_dim(
        jnp.zeros((full_length,), jnp.float32), part_sum, offset, 0
    )


def attend_forward(block):
    query_b, key_b, value_b = block
    query_h = split_heads(query_b)
    key_h = split_heads(key_b)
    value_h = split_heads(value_b)
    scores = jnp.einsum("qhd,khd->hqk", query_h, key_h, preferred_element_type=jnp.float32)
    largest = jnp.max(scores, axis=-1, keepdims=True)
    expons = jnp.exp(scores - largest)
    totals = jnp.sum(expons, axis=-1, keepdims=True)
    attn_weights = (expons / totals).astype(jnp.bfloat16)
    context = jnp.einsum("hqk,khd->qhd", attn_weights, value_h, preferred_element_type=jnp.float32)
    return (
        context.reshape(query_b.shape).astype(jnp.bfloat16),
        (largest + jnp.log(totals))[:, :, 0],
    )


def attend_backward(block):
    query_b, key_b, value_b, logsum, grad_ctx = block
    query_h = split_heads(query_b)
    key_h = split_heads(key_b)
    value_h = split_heads(value_b)
    grad_h = split_heads(grad_ctx)
    scores = jnp.einsum("qhd,khd->hqk", query_h, key_h, preferred_element_type=jnp.float32)
    weights_full = jnp.exp(scores - logsum[:, :, None])
    weights_low = weights_full.astype(jnp.bfloat16)
    grad_value = jnp.einsum("hqk,qhd->khd", weights_low, grad_h, preferred_element_type=jnp.float32)
    grad_weights = jnp.einsum("qhd,khd->hqk", grad_h, value_h, preferred_element_type=jnp.float32)
    inner = jnp.sum(weights_full * grad_weights, axis=-1, keepdims=True)
    grad_scores = (weights_full * (grad_weights - inner)).astype(jnp.bfloat16)
    grad_query = jnp.einsum("hqk,khd->qhd", grad_scores, key_h, preferred_element_type=jnp.float32)
    grad_key = jnp.einsum("hqk,qhd->khd", grad_scores, query_h, preferred_element_type=jnp.float32)
    full_shape = query_b.shape
    return (
        grad_query.reshape(full_shape).astype(jnp.bfloat16),
        grad_key.reshape(full_shape).astype(jnp.bfloat16),
        grad_value.reshape(full_shape).astype(jnp.bfloat16),
    )


def on_device(
    tokens,
    weight_query,
    weight_key,
    weight_value,
    weight_output,
    weight_up,
    weight_down,
    bias_query,
    bias_value,
    bias_up,
    bias_output,
    bias_down,
    first_gain,
    first_shift,
    second_gain,
    second_shift,
    out_grad,
):
    w_query, w_key, w_value, w_output, w_up, w_down = (
        lax.all_gather(weight_query, "dp", axis=0, tiled=True),
        lax.all_gather(weight_key, "dp", axis=0, tiled=True),
        lax.all_gather(weight_value, "dp", axis=0, tiled=True),
        lax.all_gather(weight_output, "dp", axis=1, tiled=True),
        lax.all_gather(weight_up, "dp", axis=0, tiled=True),
        lax.all_gather(weight_down, "dp", axis=1, tiled=True),
    )
    vectors = (
        lax.all_gather(bias_query, ("dp", "tensor"), axis=0, tiled=True),
        lax.all_gather(bias_value, ("dp", "tensor"), axis=0, tiled=True),
        lax.all_gather(bias_up, ("dp", "tensor"), axis=0, tiled=True),
        lax.all_gather(bias_output, ("dp", "tensor"), axis=0, tiled=True),
        lax.all_gather(bias_down, ("dp", "tensor"), axis=0, tiled=True),
        lax.all_gather(first_gain, ("dp", "tensor"), axis=0, tiled=True),
        lax.all_gather(first_shift, ("dp", "tensor"), axis=0, tiled=True),
        lax.all_gather(second_gain, ("dp", "tensor"), axis=0, tiled=True),
        lax.all_gather(second_shift, ("dp", "tensor"), axis=0, tiled=True),
    )
    query_all, value_all, up_all, out_bias, down_bias, gain_one, shift_one, gain_two, shift_two = [
        member.astype(jnp.float32) for member in vectors
    ]
    width_here = w_query.shape[1]
    hidden_here = w_up.shape[1]
    full_hidden = up_all.shape[0]
    model_width = tokens.shape[1]
    tensor_pos = lax.axis_index("tensor")
    query_bias = lax.dynamic_slice_in_dim(query_all, tensor_pos * width_here, width_here)
    value_bias = lax.dynamic_slice_in_dim(value_all, tensor_pos * width_here, width_here)
    scale = HEAD_DIM ** (-0.5)
    gathered = lax.all_gather(tokens, "tensor", axis=0, tiled=True)
    joined = jnp.concatenate([w_query, w_key, w_value], axis=1)
    projected = jnp.dot(gathered, joined, preferred_element_type=jnp.float32)
    query_b = ((projected[:, :width_here] + query_bias) * scale).astype(jnp.bfloat16)
    key_b = projected[:, width_here : 2 * width_here].astype(jnp.bfloat16)
    value_b = (projected[:, 2 * width_here :] + value_bias).astype(jnp.bfloat16)
    seq_count = gathered.shape[0] // LEN

    def by_sequence(matrix):
        return matrix.reshape(seq_count, LEN, matrix.shape[-1])

    context, logsum = lax.map(
        attend_forward, (by_sequence(query_b), by_sequence(key_b), by_sequence(value_b))
    )
    context = context.reshape(-1, width_here)
    attn_sum = lax.psum_scatter(
        jnp.dot(context, w_output, preferred_element_type=jnp.float32).astype(jnp.bfloat16),
        "tensor",
        scatter_dimension=0,
        tiled=True,
    ).astype(jnp.float32)
    resid_one = tokens.astype(jnp.float32) + (attn_sum + out_bias)
    normed_one, inverse_one = layer_stats(resid_one)
    hidden = normed_one * gain_one + shift_one
    hidden_low = hidden.astype(jnp.bfloat16)
    ffn_rows = lax.all_gather(hidden_low, "tensor", axis=0, tiled=True)
    up_use, down_use = (w_up, w_down)
    up_bias = lax.dynamic_slice_in_dim(up_all, tensor_pos * hidden_here, hidden_here)
    preact = jnp.dot(ffn_rows, up_use, preferred_element_type=jnp.float32) + up_bias
    active = jax.nn.gelu(preact, approximate=False).astype(jnp.bfloat16)
    down_sum = lax.psum_scatter(
        jnp.dot(active, down_use, preferred_element_type=jnp.float32).astype(jnp.bfloat16),
        "tensor",
        scatter_dimension=0,
        tiled=True,
    ).astype(jnp.float32)
    resid_two = hidden + (down_sum + down_bias)
    normed_two, inverse_two = layer_stats(resid_two)
    layer_out = (normed_two * gain_two + shift_two).astype(jnp.bfloat16)
    grad_top = out_grad.astype(jnp.float32)
    grad_gain_two = jnp.sum(grad_top * normed_two, axis=0)
    grad_shift_two = jnp.sum(grad_top, axis=0)
    d_resid_two = norm_back(grad_top, normed_two, inverse_two, gain_two)
    d_down = d_resid_two.astype(jnp.bfloat16)
    grad_down_bias = jnp.sum(d_down, axis=0, dtype=jnp.float32)
    d_rows = lax.all_gather(d_down, "tensor", axis=0, tiled=True)
    grad_down = jnp.einsum("nf,nd->fd", active, d_rows, preferred_element_type=jnp.float32)
    d_active = jnp.einsum("nd,fd->nf", d_rows, down_use, preferred_element_type=jnp.float32)
    d_pre = (d_active * gelu_slope(preact)).astype(jnp.bfloat16)
    grad_up_part = jnp.sum(d_pre, axis=0, dtype=jnp.float32)
    grad_up = jnp.einsum("nd,nf->df", ffn_rows, d_pre, preferred_element_type=jnp.float32)
    d_from_ffn = lax.psum_scatter(
        jnp.einsum("nf,df->nd", d_pre, up_use, preferred_element_type=jnp.float32).astype(
            jnp.bfloat16
        ),
        "tensor",
        scatter_dimension=0,
        tiled=True,
    ).astype(jnp.float32)
    grad_up_bias = widen(grad_up_part, full_hidden, tensor_pos * hidden_here)
    d_hidden = d_resid_two + d_from_ffn
    grad_gain_one = jnp.sum(d_hidden * normed_one, axis=0)
    grad_shift_one = jnp.sum(d_hidden, axis=0)
    d_resid_one = norm_back(d_hidden, normed_one, inverse_one, gain_one)
    d_attn = d_resid_one.astype(jnp.bfloat16)
    grad_out_bias = jnp.sum(d_attn, axis=0, dtype=jnp.float32)
    d_attn_rows = lax.all_gather(d_attn, "tensor", axis=0, tiled=True)
    grad_output = jnp.einsum("nc,nd->cd", context, d_attn_rows, preferred_element_type=jnp.float32)
    d_context = jnp.einsum(
        "nd,cd->nc", d_attn_rows, w_output, preferred_element_type=jnp.float32
    ).astype(jnp.bfloat16)
    d_query, d_key, d_value = lax.map(
        attend_backward,
        (
            by_sequence(query_b),
            by_sequence(key_b),
            by_sequence(value_b),
            logsum,
            by_sequence(d_context),
        ),
    )
    d_joined = jnp.concatenate(
        [
            (d_query * scale).reshape(-1, width_here),
            d_key.reshape(-1, width_here),
            d_value.reshape(-1, width_here),
        ],
        axis=1,
    )
    grad_joined = jnp.einsum("nd,nc->dc", gathered, d_joined, preferred_element_type=jnp.float32)
    grad_query_w = grad_joined[:, :width_here]
    grad_key_w = grad_joined[:, width_here : 2 * width_here]
    grad_value_w = grad_joined[:, 2 * width_here :]
    bias_sums = jnp.sum(d_joined, axis=0, dtype=jnp.float32)
    grad_query_bias = widen(bias_sums[:width_here], model_width, tensor_pos * width_here)
    grad_value_bias = widen(bias_sums[2 * width_here :], model_width, tensor_pos * width_here)
    d_from_attn = lax.psum_scatter(
        jnp.einsum("nc,dc->nd", d_joined, joined, preferred_element_type=jnp.float32).astype(
            jnp.bfloat16
        ),
        "tensor",
        scatter_dimension=0,
        tiled=True,
    ).astype(jnp.float32)
    input_grad = (d_resid_one + d_from_attn).astype(jnp.bfloat16)
    grad_query_w, grad_key_w, grad_value_w, grad_output, grad_up, grad_down = (
        lax.psum_scatter(
            grad_query_w.astype(jnp.bfloat16), "dp", scatter_dimension=0, tiled=True
        ).astype(jnp.float32),
        lax.psum_scatter(
            grad_key_w.astype(jnp.bfloat16), "dp", scatter_dimension=0, tiled=True
        ).astype(jnp.float32),
        lax.psum_scatter(
            grad_value_w.astype(jnp.bfloat16), "dp", scatter_dimension=0, tiled=True
        ).astype(jnp.float32),
        lax.psum_scatter(
            grad_output.astype(jnp.bfloat16), "dp", scatter_dimension=1, tiled=True
        ).astype(jnp.float32),
        lax.psum_scatter(
            grad_up.astype(jnp.bfloat16), "dp", scatter_dimension=0, tiled=True
        ).astype(jnp.float32),
        lax.psum_scatter(
            grad_down.astype(jnp.bfloat16), "dp", scatter_dimension=1, tiled=True
        ).astype(jnp.float32),
    )
    vector_sums = (
        lax.psum_scatter(grad_query_bias, ("dp", "tensor"), scatter_dimension=0, tiled=True),
        lax.psum_scatter(grad_value_bias, ("dp", "tensor"), scatter_dimension=0, tiled=True),
        lax.psum_scatter(grad_up_bias, ("dp", "tensor"), scatter_dimension=0, tiled=True),
        lax.psum_scatter(grad_out_bias, ("dp", "tensor"), scatter_dimension=0, tiled=True),
        lax.psum_scatter(grad_down_bias, ("dp", "tensor"), scatter_dimension=0, tiled=True),
        lax.psum_scatter(grad_gain_one, ("dp", "tensor"), scatter_dimension=0, tiled=True),
        lax.psum_scatter(grad_shift_one, ("dp", "tensor"), scatter_dimension=0, tiled=True),
        lax.psum_scatter(grad_gain_two, ("dp", "tensor"), scatter_dimension=0, tiled=True),
        lax.psum_scatter(grad_shift_two, ("dp", "tensor"), scatter_dimension=0, tiled=True),
    )
    return (
        layer_out,
        input_grad,
        grad_query_w,
        grad_key_w,
        grad_value_w,
        grad_output,
        grad_up,
        grad_down,
    ) + tuple(vector_sums)


def either(*args):
    sizes = (lax.axis_size("dp"), lax.axis_size("tensor"))
    fits = args[0].shape == (LEN, 1024) and args[5].shape[1] * 2 == 4096 and sizes == (16, 2)
    return whole_sequences(*args) if fits else on_device(*args)


def solution(mesh):
    placed = (
        P(("dp", "tensor"), None),
        P("dp", "tensor"),
        P("dp", "tensor"),
        P("dp", "tensor"),
        P("tensor", "dp"),
        P("dp", "tensor"),
        P("tensor", "dp"),
        P(("dp", "tensor")),
        P(("dp", "tensor")),
        P(("dp", "tensor")),
        P(("dp", "tensor")),
        P(("dp", "tensor")),
        P(("dp", "tensor")),
        P(("dp", "tensor")),
        P(("dp", "tensor")),
        P(("dp", "tensor")),
        P(("dp", "tensor"), None),
    )
    return jax.shard_map(
        either,
        mesh=mesh,
        in_specs=placed,
        out_specs=(
            P(("dp", "tensor"), None),
            P(("dp", "tensor"), None),
            P("dp", "tensor"),
            P("dp", "tensor"),
            P("dp", "tensor"),
            P("tensor", "dp"),
            P("dp", "tensor"),
            P("tensor", "dp"),
            P(("dp", "tensor")),
            P(("dp", "tensor")),
            P(("dp", "tensor")),
            P(("dp", "tensor")),
            P(("dp", "tensor")),
            P(("dp", "tensor")),
            P(("dp", "tensor")),
            P(("dp", "tensor")),
            P(("dp", "tensor")),
        ),
        check_vma=False,
    )
```
